32 devices in a mesh: dp: 4 (over z), expert: 8 (over y, x, core).
Axes of the slice: x: 2, y: 2, z: 4, core: 2. Of those that a mesh axis runs over, the one named last changes fastest.
Arguments:
- tokens: bfloat16 [16384, 1024], P(('dp', 'expert')), may hold values from -6 to 6
- seq_lengths: int32 [32], P(('dp', 'expert')), may hold values from 128 to 512, as said below
- routes: int32 [16384, 1], P(('dp', 'expert')), may hold values from 0 to 7
- w_qkv: bfloat16 [1024, 3072], P(('dp', 'expert')), may hold values from -0.1875 to 0.1875
- w_out: bfloat16 [1024, 1024], P(('dp', 'expert')), may hold values from -0.75 to 0.75
- w_up: bfloat16 [1024, 4096], P(('dp', 'expert')), may hold values from -0.1875 to 0.1875
- w_down: bfloat16 [4096, 1024], P(('dp', 'expert')), may hold values from -0.1875 to 0.1875
- gain_attn: bfloat16 [1024], P(('dp', 'expert')), may hold values from 0.25 to 1.75
- gain_mlp: bfloat16 [1024], P(('dp', 'expert')), may hold values from 0.25 to 1.75
- w_mix: bfloat16 [1024, 2], P(('dp', 'expert')), may hold values from -0.1875 to 0.1875
- expert_up: bfloat16 [8, 1024, 4096], P('expert', 'dp'), may hold values from -0.1875 to 0.1875
- expert_down: bfloat16 [8, 4096, 1024], P('expert', 'dp'), may hold values from -0.1875 to 0.1875
- cotangent: bfloat16 [16384, 1024], P(('dp', 'expert')), may hold values from -6 to 6
Outputs:
- result: float32 [16384, 1024], P(('dp', 'expert'))
- grad_tokens: float32 [16384, 1024], P(('dp', 'expert'))
- grad_w_qkv: float32 [1024, 3072], P(('dp', 'expert'))
- grad_w_out: float32 [1024, 1024], P(('dp', 'expert'))
- grad_w_up: float32 [1024, 4096], P(('dp', 'expert'))
- grad_w_down: float32 [4096, 1024], P(('dp', 'expert'))
- grad_gain_attn: float32 [1024], P(('dp', 'expert'))
- grad_gain_mlp: float32 [1024], P(('dp', 'expert'))
- grad_w_mix: float32 [1024, 2], P(('dp', 'expert'))
- grad_expert_up: float32 [8, 1024, 4096], P('expert', 'dp')
- grad_expert_down: float32 [8, 4096, 1024], P('expert', 'dp')
The draws below stay inside these ranges and needn't reach their ends.
Inputs may be any that keep to these rules, and one draw needn't show every extreme that they name: `seq_lengths`: each slot has from 128 to 512 valid tokens, the first ones of the slot; some slot has exactly 512 and some exactly 128.
All inputs are finite; a program needn't handle non-finite values.
Results may differ from the reference program's by a relative error of at most 0.013.
Values may be sent and summed in bfloat16 or wider, within the bound.
A program may use at most 256 MiB of HBM per device.

```python
import jax
import jax.numpy as jnp
from jax import lax

D = 1024
HEADS = 16
HEAD_DIM = 64
FF = 4096
TOK_DEV = 512
EXPERTS = 8
SEQS = 32
TOKENS = 16384
CAP = 80
N_DP = 4
N_EXPERT = 8


def draw_seq_lengths(key, part):
    value_key = jax.random.fold_in(key, 11)
    shuffle_key = jax.random.fold_in(key, 23)
    values = jax.random.randint(value_key, (SEQS,), TOK_DEV // 4, TOK_DEV + 1)
    shuffled = jax.random.permutation(shuffle_key, SEQS)
    values = values.at[shuffled[0]].set(TOK_DEV)
    values = values.at[shuffled[1]].set(TOK_DEV // 4)
    return values.astype(jnp.int32)


def level_of(own_key, shape, cuts, low, high):
    level, own = 1.0, jax.random.fold_in(own_key, 6)
    for position, blocks in cuts:
        draws = jnp.exp(jax.random.uniform(jax.random.fold_in(own, position), (blocks,), jnp.float32, low / len(cuts), high / len(cuts)))
        level = level * jnp.repeat(draws, shape[position] // blocks).reshape([-1 if axis == position else 1 for axis in range(len(shape))])
    return level


def distinct(key, rows, number_of, top, lift):
    order = jax.random.permutation(jax.random.fold_in(key, 1), number_of)
    boost = order
    for power in range(3):
        boost = boost * boost // number_of
    boost = boost * lift // number_of
    tickets = jax.random.randint(jax.random.fold_in(key, 2), (rows, number_of), 0, 4096) + boost
    fixed_rows = jax.random.permutation(jax.random.fold_in(key, 3), rows)[jnp.arange(number_of) % rows]
    tickets = jnp.where(jnp.arange(rows)[:, None] == fixed_rows[None, :], 1 << 14, tickets)
    score = tickets * number_of + jnp.arange(number_of)
    return lax.top_k(score.astype(jnp.int32), top)[1].astype(jnp.int32)


def normal_values(rng, extent, width, bound, pieces=(), kind=jnp.bfloat16):
    array = width * jax.random.normal(rng, extent, jnp.float32)
    if pieces:
        array = array * level_of(rng, extent, pieces, -0.22, 0.18)
    return jnp.clip(array, -bound, bound).astype(kind)


def setup_inputs(seed: int = 0) -> dict:
    key_list = jax.random.split(jax.random.key(seed), 14)
    return {
        "tokens": normal_values(key_list[0], (TOKENS, D), 1.0, 6.0, ((0, 32),)),
        "seq_lengths": draw_seq_lengths(jax.random.fold_in(key_list[13], 71), 0),
        "routes": distinct(key_list[2], TOKENS, EXPERTS, 1, 1024),
        "w_qkv": normal_values(key_list[3], (D, 3 * D), D ** -0.5, 0.1875, ((0, 32),)),
        "w_out": normal_values(key_list[4], (D, D), (D // 16) ** -0.5, 0.75, ((0, 32),)),
        "w_up": normal_values(key_list[5], (D, FF), D ** -0.5, 0.1875, ((0, 32),)),
        "w_down": normal_values(key_list[6], (FF, D), (FF // 4) ** -0.5, 0.1875, ((0, 32),)),
        "gain_attn": jnp.clip(1.0 + 0.15 * jax.random.normal(key_list[7], (D,), jnp.float32), 0.25, 1.75).astype(jnp.bfloat16),
        "gain_mlp": jnp.clip(1.0 + 0.15 * jax.random.normal(key_list[8], (D,), jnp.float32), 0.25, 1.75).astype(jnp.bfloat16),
        "w_mix": normal_values(key_list[9], (D, 2), D ** -0.5, 0.1875, ((0, 32),)),
        "expert_up": normal_values(key_list[10], (EXPERTS, D, FF), D ** -0.5, 0.1875, ((0, 8), (1, 4))),
        "expert_down": normal_values(key_list[11], (EXPERTS, FF, D), (FF // 4) ** -0.5, 0.1875, ((0, 8), (1, 4))),
        "cotangent": normal_values(key_list[12], (TOKENS, D), 1.0, 6.0, ((0, 32),)),
    }


@jax.custom_vjp
def low(v):
    return lax.optimization_barrier(v.astype(jnp.bfloat16)).astype(jnp.float32)

@jax.custom_vjp
def low_back(v):
    return v

def low_keep(v):
    return (low(v), None)

def low_pass(kept, grad):
    return (grad,)

def back_keep(v):
    return (v, None)

def back_low(kept, grad):
    return (low(grad),)
low.defvjp(low_keep, low_pass)
low_back.defvjp(back_keep, back_low)
epsilon = 1e-05
root_half = 0.7071067811865476
highest = lax.Precision.HIGHEST

def product(left_side, right_side):
    return jnp.dot(left_side, right_side, precision=highest, preferred_element_type=jnp.float32)

def layer_norm(values, gain_row):
    row_mean = lax.optimization_barrier(jnp.mean(values, axis=-1, keepdims=True))
    centred = values - row_mean
    row_var = lax.optimization_barrier(jnp.mean(centred * centred, axis=-1, keepdims=True))
    return centred * lax.rsqrt(row_var + epsilon) * gain_row

def gelu_exact(values):
    return 0.5 * values * (1.0 + lax.erf(values * root_half))

def attend_block(block_qkv, block_lengths):
    seq_count = block_qkv.shape[0]
    length = block_qkv.shape[1]
    queries = block_qkv[..., :D].reshape(seq_count, length, HEADS, HEAD_DIM)
    keys_all = block_qkv[..., D:2 * D].reshape(seq_count, length, HEADS, HEAD_DIM)
    values_all = block_qkv[..., 2 * D:].reshape(seq_count, length, HEADS, HEAD_DIM)
    scores = jnp.einsum('bqhd,bkhd->bhqk', queries, keys_all, precision=highest) * HEAD_DIM ** (-0.5)
    rows_at = jnp.arange(length)[:, None]
    cols_at = jnp.arange(length)[None, :]
    allowed = (cols_at <= rows_at)[None, None] & (cols_at[None, None] < block_lengths[:, None, None, None])
    scores = low_back(jnp.where(allowed, scores, -1000000000.0))
    attn_probs = low(jax.nn.softmax(scores, axis=-1))
    mixed = jnp.einsum('bhqk,bkhd->bqhd', attn_probs, values_all, precision=highest)
    return mixed.reshape(seq_count, length, D)

def attend_pair(pair):
    return attend_block(pair[0], pair[1])

def layer_group(params, group_tokens, group_lengths, group_routes):
    w_qkv, w_out, w_up, w_down, gain_attn, gain_mlp, w_mix, expert_up, expert_down = params
    sources = group_tokens.shape[0]
    flat_rows = group_tokens.reshape(sources * TOK_DEV, D)
    normed = low(layer_norm(flat_rows, gain_attn))
    joined = low(low_back(product(normed, w_qkv))).reshape(sources, TOK_DEV, 3 * D)
    per_block = 8 if sources % 8 == 0 else 1
    attended = lax.map(jax.checkpoint(attend_pair), (joined.reshape(sources // per_block, per_block, TOK_DEV, 3 * D), group_lengths.reshape(sources // per_block, per_block)))
    heads_out = low(low_back(attended.reshape(sources * TOK_DEV, D)))
    after_attn = flat_rows + low_back(product(heads_out, w_out))
    normed_mlp = low(layer_norm(after_attn, gain_mlp))
    hidden = low_back(product(normed_mlp, w_up))
    dense_out = low_back(product(low(gelu_exact(hidden)), w_down))
    mix_weights = jax.nn.softmax(product(normed_mlp, w_mix), axis=-1)
    positions = jnp.arange(TOK_DEV)
    valid_rows = positions[None, :] < group_lengths[:, None]
    route_hits = (group_routes[:, :, None] == jnp.arange(EXPERTS)[None, None, :]) & valid_rows[:, :, None]
    route_ranks = jnp.cumsum(route_hits.astype(jnp.int32), axis=1) - 1
    chosen = lax.optimization_barrier(jnp.sum(jnp.where(route_hits, route_ranks, 0), axis=2))
    kept_rows = valid_rows & (chosen < CAP)
    slot_ids = group_routes * CAP + chosen
    slot_table = ((jnp.arange(EXPERTS * CAP)[None, :, None] == slot_ids[:, None, :]) & kept_rows[:, None, :]).astype(jnp.float32)
    sent_rows = jnp.einsum('sjt,std->sjd', slot_table, normed_mlp.reshape(sources, TOK_DEV, D), precision=highest)
    arrived = low_back(sent_rows.reshape(sources, EXPERTS, CAP, D).transpose(1, 0, 2, 3).reshape(EXPERTS, sources * CAP, D))
    expert_hidden = low_back(jnp.einsum('erd,edf->erf', arrived, expert_up, precision=highest))
    expert_rows = low(low_back(jnp.einsum('erf,efd->erd', low(gelu_exact(expert_hidden)), expert_down, precision=highest)))
    returned = expert_rows.reshape(EXPERTS, sources, CAP, D).transpose(1, 0, 2, 3).reshape(sources, EXPERTS * CAP, D)
    expert_out = jnp.einsum('sjt,sjd->std', slot_table, returned, precision=highest).reshape(sources * TOK_DEV, D)
    mixed = mix_weights[:, 0:1] * dense_out + mix_weights[:, 1:2] * expert_out
    return (after_attn + mixed).reshape(sources, TOK_DEV, D)

def reference(tokens, seq_lengths, routes, w_qkv, w_out, w_up, w_down, gain_attn, gain_mlp, w_mix, expert_up, expert_down, cotangent):
    params = tuple((weight_in.astype(jnp.float32) for weight_in in (w_qkv, w_out, w_up, w_down, gain_attn, gain_mlp, w_mix, expert_up, expert_down)))
    shaped = tokens.astype(jnp.float32).reshape(N_DP, N_EXPERT, TOK_DEV, D)
    pulled = cotangent.astype(jnp.float32).reshape(N_DP, N_EXPERT, TOK_DEV, D)
    lengths_all = seq_lengths.reshape(N_DP, N_EXPERT)
    routes_all = routes.reshape(N_DP, N_EXPERT, TOK_DEV)

    def one_group(totals, inputs):
        group_tokens, group_cot, group_lengths, group_routes = inputs

        def forward(weights, values):
            return layer_group(weights, values, group_lengths, group_routes)
        outputs, backward = jax.vjp(forward, params, group_tokens)
        valid_rows = (jnp.arange(TOK_DEV)[None, :] < group_lengths[:, None]).astype(jnp.float32)
        weight_grads, token_grads = backward(group_cot * valid_rows[:, :, None])
        totals = jax.tree.map(jnp.add, totals, weight_grads)
        return (totals, (outputs, token_grads))
    zeroes = tuple((jnp.zeros_like(weight_in) for weight_in in params))
    totals, (outputs, token_grads) = lax.scan(one_group, zeroes, (shaped, pulled, lengths_all, routes_all))
    return (outputs.reshape(TOKENS, D), token_grads.reshape(TOKENS, D), totals[0], totals[1], totals[2], totals[3], totals[4], totals[5], totals[6], totals[7], totals[8])
```

```python
import functools

import jax
import jax.numpy as jnp
from jax import lax
from jax.experimental import pallas as pl
from jax.experimental.pallas import tpu as pltpu
from jax.sharding import PartitionSpec as P

HEADS = 16

epsilon = 1e-05
root_half = 0.7071067811865476
inv_root_two_pi = 0.3989422804014327
highest = lax.Precision.HIGHEST
both = ("dp", "expert")


def gelu_exact(values):
    return 0.5 * values * (1.0 + lax.erf(values * root_half))


def gelu_slope(values):
    return (
        0.5 * (1.0 + lax.erf(values * root_half))
        + values * jnp.exp(-0.5 * values * values) * inv_root_two_pi
    )


def dot(left, right, dims):
    return lax.dot_general(left, right, (dims, ((), ())), preferred_element_type=jnp.float32)


def matmul(left, right):
    return dot(left, right, ((1,), (0,)))


def matmul_nt(left, right):
    return dot(left, right, ((1,), (1,)))


def matmul_tn(left, right):
    return dot(left, right, ((0,), (0,)))


def norm_forward(values):
    row_mean = jnp.mean(values, axis=-1, keepdims=True)
    centred = values - row_mean
    row_var = jnp.mean(centred * centred, axis=-1, keepdims=True)
    inverse = lax.rsqrt(row_var + epsilon)
    return (centred * inverse, inverse)


def norm_backward(upstream, scaled, inverse, gain_row):
    gain_grad = jnp.sum(upstream * scaled, axis=0)
    inner = upstream * gain_row
    centred_grad = (
        inner
        - jnp.mean(inner, axis=-1, keepdims=True)
        - scaled * jnp.mean(inner * scaled, axis=-1, keepdims=True)
    )
    return (inverse * centred_grad, gain_grad)


def causal_scores(queries, keys_all, length, score_scale):
    row_count = queries.shape[0]
    scores = (
        jnp.einsum("qhd,khd->hqk", queries, keys_all, preferred_element_type=jnp.float32)
        * score_scale
    )
    rows_at = lax.broadcasted_iota(jnp.int32, (row_count, row_count), 0)
    cols_at = lax.broadcasted_iota(jnp.int32, (row_count, row_count), 1)
    allowed = (cols_at <= rows_at) & (cols_at < length)
    return jnp.where(allowed[None], scores, -1000000000.0)


def attention_forward(joined, length):
    tok_rows, width = joined.shape[0], joined.shape[1] // 3
    head_width = width // HEADS
    score_scale = head_width ** (-0.5)
    queries, keys_all, values_all = (
        joined[:, i * width : (i + 1) * width].reshape(tok_rows, HEADS, head_width) for i in range(3)
    )
    scores = causal_scores(queries, keys_all, length, score_scale)
    top_score = jnp.max(scores, axis=-1, keepdims=True)
    raised = jnp.exp(scores - top_score)
    row_total = jnp.sum(raised, axis=-1, keepdims=True)
    log_total = top_score + jnp.log(row_total)
    attn_probs = (raised / row_total).astype(jnp.bfloat16)
    heads_out = (
        jnp.einsum("hqk,khd->qhd", attn_probs, values_all, preferred_element_type=jnp.float32)
        .reshape(tok_rows, width)
        .astype(jnp.bfloat16)
    )
    return heads_out, log_total


def attention_backward(joined, heads_grad, log_total, length):
    tok_rows, width = joined.shape[0], joined.shape[1] // 3
    head_width = width // HEADS
    score_scale = head_width ** (-0.5)
    queries, keys_all, values_all = (
        joined[:, i * width : (i + 1) * width].reshape(tok_rows, HEADS, head_width) for i in range(3)
    )
    heads_grad = heads_grad.reshape(tok_rows, HEADS, head_width)
    probs_exact = jnp.exp(causal_scores(queries, keys_all, length, score_scale) - log_total)
    probs_low = probs_exact.astype(jnp.bfloat16)
    grad_values = jnp.einsum(
        "hqk,qhd->khd", probs_low, heads_grad, preferred_element_type=jnp.float32
    )
    prob_grad = jnp.einsum(
        "qhd,khd->hqk", heads_grad, values_all, preferred_element_type=jnp.float32
    )
    row_delta = jnp.sum(prob_grad * probs_exact, axis=-1, keepdims=True)
    score_grad = (probs_exact * (prob_grad - row_delta)).astype(jnp.bfloat16)
    grad_queries = (
        jnp.einsum("hqk,khd->qhd", score_grad, keys_all, preferred_element_type=jnp.float32)
        * score_scale
    )
    grad_keys = (
        jnp.einsum("hqk,qhd->khd", score_grad, queries, preferred_element_type=jnp.float32)
        * score_scale
    )
    return jnp.concatenate(
        [g.reshape(tok_rows, width) for g in (grad_queries, grad_keys, grad_values)], axis=1
    ).astype(jnp.bfloat16)


MESH = pl.DeviceIdType.MESH


def plane():
    here = lax.axis_index("expert")
    core, x, y = here % 2, (here // 2) % 2, here // 4
    return here // 2, core, x, y, here + 1 - 2 * core, here + 2 - 4 * x, here + 4 - 8 * y


def greet(depth, others, count):
    level = lax.axis_index("dp")
    barrier = pltpu.get_barrier_semaphore()
    for other in others:
        pl.semaphore_signal(barrier, inc=1, device_id=(level, other), device_id_type=MESH)
    if count:
        for step in range(1, depth):
            pl.semaphore_signal(
                barrier,
                inc=1,
                device_id=((level + step) % depth, lax.axis_index("expert")),
                device_id_type=MESH,
            )
    pl.semaphore_wait(barrier, len(others) + (depth - 1 if count else 0))


def remote(source, target, sems, slot, level, where):
    return pltpu.make_async_remote_copy(
        src_ref=source,
        dst_ref=target,
        send_sem=sems[0].at[slot],
        recv_sem=sems[1].at[slot],
        device_id=(level, where),
        device_id_type=MESH,
    )


def gather_kernel(depth, count, swap, *refs):
    shards, refs = refs[:count], refs[count:]
    if swap:
        wide, refs = refs[0], refs[1:]
    fulls, refs = refs[:count], refs[count:]
    if swap:
        parts, refs = refs[0], refs[1:]
    keep = refs[0]
    z_sems, x_sems, y_sems, d_sems, c_sems, w_sems = (refs[1 + 2 * i : 3 + 2 * i] for i in range(6))
    level, here = lax.axis_index("dp"), lax.axis_index("expert")
    chip, core, x, y, twin, x_next, y_next = plane()
    x_chip, y_chip, far_chip = chip + 1 - 2 * x, chip + 2 - 4 * y, 3 - chip
    greet(depth, (twin, x_next, y_next), True)
    started = []

    def send(*a):
        copy = remote(*a)
        copy.start()
        started.append(copy)

    def to_twin(i, step, chip_at, source=None):
        spot = fulls[i].at[(level + depth - step) % depth, chip_at, core]
        send(spot if source is None else source, spot, c_sems, (i, step, chip_at), level, twin)

    locals_ = []
    for step in range(1, depth):
        for i in range(count):
            send(shards[i], fulls[i].at[level, chip, core], z_sems, (i, step), (level + step) % depth, here)
    if swap:
        width = wide.shape[1] // depth

        def columns(at):
            return wide.at[:, pl.ds(pl.multiple_of(at * width, width), width)]

        for step in range(1, depth):
            target = (level + step) % depth
            send(columns(target), parts.at[level], w_sems, (step,), target, here)
        copy = pltpu.make_async_copy(columns(level), parts.at[level], keep.at[count])
        copy.start()
        locals_.append(copy)
    for i in range(count):
        copy = pltpu.make_async_copy(shards[i], fulls[i].at[level, chip, core], keep.at[i])
        copy.start()
        locals_.append(copy)
    for step in range(depth):
        source = (level + depth - step) % depth
        for i in range(count):
            spot = fulls[i].at[source, chip, core]
            if step:
                remote(shards[i], spot, z_sems, (i, step), level, here).wait_recv()
            origin = spot if step else shards[i]
            send(origin, spot, x_sems, (i, step), level, x_next)
            send(origin, spot, y_sems, (i, step), level, y_next)
            to_twin(i, step, chip, origin)
    for step in range(depth):
        source = (level + depth - step) % depth
        for i in range(count):
            x_spot, y_spot = fulls[i].at[source, x_chip, core], fulls[i].at[source, y_chip, core]
            remote(shards[i], x_spot, x_sems, (i, step), level, here).wait_recv()
            if step % 2 == 0:
                send(x_spot, x_spot, d_sems, (i, step), level, y_next)
            to_twin(i, step, x_chip)
            remote(shards[i], y_spot, y_sems, (i, step), level, here).wait_recv()
            if step % 2 == 1:
                send(y_spot, y_spot, d_sems, (i, step), level, x_next)
            to_twin(i, step, y_chip)
    for step in range(depth):
        source = (level + depth - step) % depth
        for i in range(count):
            spot = fulls[i].at[source, far_chip, core]
            remote(shards[i], spot, d_sems, (i, step), level, here).wait_recv()
            to_twin(i, step, far_chip)
    for step in range(depth):
        source = (level + depth - step) % depth
        for i in range(count):
            for chip_at in range(4):
                spot = fulls[i].at[source, chip_at, 1 - core]
                remote(shards[i], spot, c_sems, (i, step, chip_at), level, here).wait_recv()
    if swap:
        for step in range(1, depth):
            spot = parts.at[(level + depth - step) % depth]
            remote(columns(level), spot, w_sems, (step,), level, here).wait_recv()
    for copy in locals_:
        copy.wait()
    for copy in started:
        copy.wait_send()


def gather_plane(shards, ident, wide=None):
    depth, count = lax.axis_size("dp"), len(shards)
    if lax.axis_size("expert") != 8:
        fulls = [lax.all_gather(s, both, axis=0, tiled=True) for s in shards]
        if wide is not None:
            fulls.append(lax.all_to_all(wide, "dp", split_axis=1, concat_axis=0, tiled=True))
        return fulls
    swap = wide is not None
    extra = [wide] if swap else []
    extra_out = [jax.ShapeDtypeStruct((depth, wide.shape[0], wide.shape[1] // depth), wide.dtype)] if swap else []
    kinds = []
    for shape in ((count, depth),) * 4 + ((count, depth, 4),):
        kinds += [pltpu.SemaphoreType.DMA(shape)] * 2
    kinds += [pltpu.SemaphoreType.DMA((depth,))] * 2
    fulls = pl.pallas_call(
        functools.partial(gather_kernel, depth, count, swap),
        out_shape=[jax.ShapeDtypeStruct((depth, 4, 2) + s.shape, s.dtype) for s in shards] + extra_out,
        in_specs=[pl.BlockSpec(memory_space=pl.ANY)] * (count + swap),
        out_specs=[pl.BlockSpec(memory_space=pl.ANY)] * (count + swap),
        scratch_shapes=[pltpu.SemaphoreType.DMA((count + 1,))] + kinds,
        compiler_params=pltpu.CompilerParams(collective_id=ident, has_side_effects=True),
        name=f"gather_plane_{ident}",
    )(*shards, *extra)
    full = [f.reshape((-1,) + s.shape[1:]) for f, s in zip(fulls, shards)]
    return full + [p.reshape((-1, p.shape[2])) for p in fulls[count:]]


def scatter_kernel(depth, count, with_z, swap, *refs):
    grads, refs = refs[:count], refs[count:]
    if swap:
        tall, refs = refs[0], refs[1:]
    outs, refs = refs[:count], refs[count:]
    if swap:
        parts, keep, w_sems, refs = refs[0], refs[-1], refs[-3:-1], refs[1:-3]
    n = 0
    own, twins, first, second = (refs[n + i * count : n + (i + 1) * count] for i in range(4))
    n += 4 * count
    levels = refs[n : n + count] if with_z else ()
    n += count if with_z else 0
    load, c_sems, f_sems, s_sems = refs[n], refs[n + 1 : n + 3], refs[n + 3 : n + 5], refs[n + 5 : n + 7]
    z_sems = refs[n + 7 : n + 9]
    level, here = lax.axis_index("dp"), lax.axis_index("expert")
    chip, core, x, y, twin, x_next, y_next = plane()
    greet(depth, (twin, x_next, y_next), with_z or swap)
    started, loads = [], {}

    def send(*a):
        copy = remote(*a)
        copy.start()
        started.append(copy)

    if swap:
        width = tall.shape[2]

        def columns(at):
            return parts.at[:, pl.ds(pl.multiple_of(at * width, width), width)]

        for step in range(1, depth):
            target = (level + step) % depth
            send(tall.at[target], columns(level), w_sems, (step,), target, here)
        stay = pltpu.make_async_copy(tall.at[level], columns(level), keep.at[0])
        stay.start()
    order = [(step, (step + level + 1) % depth) for step in range(depth)]
    for step, at in order:
        for i in range(count):
            send(grads[i].at[at, :, 1 - core], twins[i].at[step], c_sems, (i, step), level, twin)
            loads[i, step] = pltpu.make_async_copy(grads[i].at[at, :, core], own[i].at[step], load.at[i, step])
            loads[i, step].start()

    def add(target, other):
        target[...] = (target[...].astype(jnp.float32) + other[...].astype(jnp.float32)).astype(jnp.bfloat16)

    def chips(step):
        if step % 2 == 0:
            return (1 - x, 3 - x), (x, 2 + x), x_next, y_next, 1 - y, y
        return (2 - 2 * y, 3 - 2 * y), (2 * y, 2 * y + 1), y_next, x_next, 1 - x, x

    for step, at in order:
        away, near, first_next, second_next, other, mine = chips(step)
        for i in range(count):
            loads[i, step].wait()
            remote(own[i].at[step], twins[i].at[step], c_sems, (i, step), level, here).wait_recv()
            for side in range(2):
                add(own[i].at[step, away[side]], twins[i].at[step, away[side]])
                send(own[i].at[step, away[side]], first[i].at[step, side], f_sems, (i, step, side), level, first_next)
            for side in range(2):
                add(own[i].at[step, near[side]], twins[i].at[step, near[side]])
    for step, at in order:
        away, near, first_next, second_next, other, mine = chips(step)
        for i in range(count):
            for side in range(2):
                remote(own[i].at[step, 0], first[i].at[step, side], f_sems, (i, step, side), level, here).wait_recv()
                add(own[i].at[step, near[side]], first[i].at[step, side])
            across = chip + 2 - 4 * y if step % 2 == 0 else chip + 1 - 2 * x
            send(own[i].at[step, across], second[i].at[step], s_sems, (i, step), level, second_next)
    for step, at in order:
        for i in range(count):
            remote(own[i].at[step, 0], second[i].at[step], s_sems, (i, step), level, here).wait_recv()
            add(second[i].at[step], own[i].at[step, chip])
            if with_z:
                if step < depth - 1:
                    send(second[i].at[step], levels[i].at[step], z_sems, (i, step), at, here)
            else:
                outs[i][at] = second[i][step]
    if with_z:
        for i in range(count):
            total = second[i][depth - 1].astype(jnp.float32)
            for step in range(depth - 1):
                remote(second[i].at[step], levels[i].at[step], z_sems, (i, step), level, here).wait_recv()
                total = total + levels[i][step].astype(jnp.float32)
            outs[i][...] = total
    if swap:
        for step in range(1, depth):
            spot = columns((level + depth - step) % depth)
            remote(tall.at[level], spot, w_sems, (step,), level, here).wait_recv()
        stay.wait()
    for copy in started:
        copy.wait_send()


def scatter_plane(grads, ident, with_z, tall=None):
    depth, count = lax.axis_size("dp"), len(grads)
    if lax.axis_size("expert") != 8:
        sums = [lax.psum_scatter(g, both, scatter_dimension=0, tiled=True).astype(jnp.float32) for g in grads]
        if tall is not None:
            sums.append(lax.all_to_all(tall, "dp", split_axis=0, concat_axis=1, tiled=True))
        return sums
    swap = tall is not None
    extra = [tall.reshape((depth, -1, tall.shape[1]))] if swap else []
    extra_out = [jax.ShapeDtypeStruct((tall.shape[0] // depth, tall.shape[1] * depth), tall.dtype)] if swap else []
    grads = [g.reshape((depth, 4, 2, g.shape[0] // (8 * depth)) + g.shape[1:]) for g in grads]
    blocks = [g.shape[3:] for g in grads]
    low = jnp.bfloat16
    scratch = [pltpu.VMEM((depth, 4) + b, low) for b in blocks] * 2
    scratch += [pltpu.VMEM((depth, 2) + b, low) for b in blocks]
    scratch += [pltpu.VMEM((depth,) + b, low) for b in blocks]
    if with_z:
        scratch += [pltpu.VMEM((depth - 1,) + b, low) for b in blocks]
    sems = [pltpu.SemaphoreType.DMA((count, depth))] * 3 + [pltpu.SemaphoreType.DMA((count, depth, 2))] * 2
    sems += [pltpu.SemaphoreType.DMA((count, depth))] * 2
    if with_z:
        sems += [pltpu.SemaphoreType.DMA((count, depth))] * 2
    if swap:
        sems += [pltpu.SemaphoreType.DMA((depth,))] * 2 + [pltpu.SemaphoreType.DMA((1,))]
    sums = pl.pallas_call(
        functools.partial(scatter_kernel, depth, count, with_z, swap),
        out_shape=[
            jax.ShapeDtypeStruct(b, jnp.float32) if with_z else jax.ShapeDtypeStruct((depth,) + b, low) for b in blocks
        ]
        + extra_out,
        in_specs=[pl.BlockSpec(memory_space=pl.ANY)] * (count + swap),
        out_specs=[pl.BlockSpec(memory_space=pltpu.VMEM)] * count + [pl.BlockSpec(memory_space=pl.ANY)] * swap,
        scratch_shapes=scratch + sems,
        compiler_params=pltpu.CompilerParams(
            collective_id=ident, has_side_effects=True, vmem_limit_bytes=48 * 2**20
        ),
        name=f"scatter_plane_{ident}",
    )(*grads, *extra)
    if with_z:
        return list(sums)
    low_sums = [lax.psum_scatter(s, "dp", scatter_dimension=0).astype(jnp.float32) for s in sums[:count]]
    return low_sums + list(sums[count:])


def body(
    tokens,
    seq_lengths,
    routes,
    w_qkv,
    w_out,
    w_up,
    w_down,
    gain_attn,
    gain_mlp,
    w_mix,
    expert_up,
    expert_down,
    cotangent,
):
    tok_rows, model_width = tokens.shape
    axis_dp, axis_experts = lax.axis_size("dp"), lax.axis_size("expert")
    expert_total = axis_experts * expert_up.shape[0]
    capacity = max(2, 5 * tok_rows // (4 * expert_total))
    slots = expert_total * capacity
    ff_expert = expert_up.shape[2]

    small = jnp.concatenate([gain_attn[:, None], gain_mlp[:, None], w_mix], axis=1)
    small = jnp.pad(small, ((0, 0), (0, 128 - small.shape[1])))
    length = seq_lengths[0]
    valid_rows = jnp.arange(tok_rows, dtype=jnp.int32) < length

    route_ids = routes[:, 0]
    expert_ids = jnp.arange(expert_total, dtype=jnp.int32)
    route_hits = (route_ids[:, None] == expert_ids[None, :]) & valid_rows[:, None]
    route_ranks = jnp.cumsum(route_hits.astype(jnp.int32), axis=0) - 1
    chosen = jnp.sum(jnp.where(route_hits, route_ranks, 0), axis=1)
    kept_rows = valid_rows & (chosen < capacity)
    slot_ids = route_ids * capacity + chosen
    slot_table = (
        (jnp.arange(slots, dtype=jnp.int32)[:, None] == slot_ids[None, :]) & kept_rows[None, :]
    ).astype(jnp.bfloat16)

    def dispatch(rows):
        picked = matmul(slot_table, rows).astype(jnp.bfloat16)
        picked = picked.reshape(expert_total, capacity, model_width)
        arrived = lax.all_to_all(picked, "expert", split_axis=0, concat_axis=0, tiled=True)
        return arrived.reshape(slots, model_width)

    def spread(rows):
        return lax.all_gather(rows, "dp", axis=0, tiled=True)

    def give_back(rows):
        summed = lax.psum_scatter(rows, "dp", scatter_dimension=0, tiled=True)
        summed = summed.reshape(expert_total, capacity, model_width)
        back = lax.all_to_all(summed, "expert", split_axis=0, concat_axis=0, tiled=True)
        return matmul_tn(slot_table, back.reshape(slots, model_width))

    down_part = expert_down[0]

    upstream_low = jnp.where(valid_rows[:, None], cotangent, jnp.zeros_like(cotangent))
    upstream = upstream_low.astype(jnp.float32)
    pulled_here = dispatch(upstream_low)
    pulled_here, w_qkv, w_out, small = lax.optimization_barrier((pulled_here, w_qkv, w_out, small))
    pulled_rows = spread(pulled_here)
    qkv_full, out_full, small_full = gather_plane([w_qkv, w_out, small], 0)
    gain_one = small_full[:, 0].astype(jnp.float32)
    gain_two = small_full[:, 1].astype(jnp.float32)
    mix_full = small_full[:, 2:4]
    mix_lean = (mix_full[:, 0] - mix_full[:, 1].astype(jnp.float32)).astype(jnp.float32)

    inputs = tokens.astype(jnp.float32)
    scaled_one, inverse_one = norm_forward(inputs)
    normed_one = (scaled_one * gain_one).astype(jnp.bfloat16)
    joined = matmul(normed_one, qkv_full).astype(jnp.bfloat16)
    heads_out, log_total = attention_forward(joined, length)
    after_attn = inputs + matmul(heads_out, out_full)
    scaled_two, inverse_two = norm_forward(after_attn)
    normed_two = (scaled_two * gain_two).astype(jnp.bfloat16)

    rows_here = dispatch(normed_two)
    rows_here, w_up, w_down = lax.optimization_barrier((rows_here, w_up, w_down))
    rows_in = spread(rows_here)
    up_full, down_full, up_part = gather_plane([w_up, w_down], 1, expert_up[0])
    act_pull = matmul_nt(pulled_rows, down_part)

    mix_weights = jax.nn.softmax(matmul(normed_two, mix_full), axis=-1)
    hidden = matmul(normed_two, up_full)
    activated = gelu_exact(hidden).astype(jnp.bfloat16)
    dense_out = matmul(activated, down_full)
    dense_pull = matmul_nt(upstream_low, down_full)
    pull_dense = jnp.sum(activated.astype(jnp.float32) * dense_pull, axis=1, keepdims=True)
    mix_both = mix_weights[:, 0:1] * mix_weights[:, 1:2]
    lean_dense = mix_both * pull_dense
    dense_grad_out = (upstream * mix_weights[:, 0:1]).astype(jnp.bfloat16)
    hidden_grad = (mix_weights[:, 0:1] * dense_pull * gelu_slope(hidden)).astype(jnp.bfloat16)
    grad_down = matmul_tn(activated, dense_grad_out).astype(jnp.bfloat16)
    grad_up = matmul_tn(normed_two, hidden_grad).astype(jnp.bfloat16)
    normed_grad = matmul_nt(hidden_grad, up_full) + lean_dense * mix_lean[None, :]

    row_mix = jax.nn.softmax(matmul(rows_in, mix_full), axis=-1)
    pre_act = matmul(rows_in, up_part)
    act_rows = gelu_exact(pre_act).astype(jnp.bfloat16)
    pull_rows = jnp.sum(act_rows.astype(jnp.float32) * act_pull, axis=1, keepdims=True)
    lean_rows = row_mix[:, 0:1] * row_mix[:, 1:2] * pull_rows
    pre_grad = (row_mix[:, 1:2] * act_pull * gelu_slope(pre_act)).astype(jnp.bfloat16)
    input_grad = (matmul_nt(pre_grad, up_part) - lean_rows * mix_lean[None, :]).astype(jnp.bfloat16)
    in_grad_back = give_back(input_grad)
    made = matmul(act_rows, down_part).astype(jnp.bfloat16)
    expert_out = give_back(made)
    result = after_attn + mix_weights[:, 0:1] * dense_out + mix_weights[:, 1:2] * expert_out
    grad_rows = (pulled_rows.astype(jnp.float32) * row_mix[:, 1:2]).astype(jnp.bfloat16)
    grad_expert_down = matmul_tn(act_rows, grad_rows)[None]
    grad_expert_up = matmul_tn(rows_in, pre_grad).astype(jnp.bfloat16)
    grad_up, grad_down, grad_expert_up = scatter_plane([grad_up, grad_down], 2, False, grad_expert_up)
    grad_expert_up = grad_expert_up.astype(jnp.float32)[None]

    normed_grad = normed_grad + in_grad_back
    lean_grad = jnp.sum(normed_two.astype(jnp.float32) * lean_dense, axis=0) - jnp.sum(
        rows_in.astype(jnp.float32) * lean_rows, axis=0
    )
    mlp_in_grad, grad_gain_two = norm_backward(normed_grad, scaled_two, inverse_two, gain_two)
    resid_grad = upstream + mlp_in_grad
    attn_grad = resid_grad.astype(jnp.bfloat16)
    grad_out = matmul_tn(heads_out, attn_grad)
    heads_grad = matmul_nt(attn_grad, out_full).astype(jnp.bfloat16)
    joined_grad = attention_backward(joined, heads_grad, log_total, length)
    grad_qkv = matmul_tn(normed_one, joined_grad)
    normed_one_grad = matmul_nt(joined_grad, qkv_full)
    attn_in_grad, grad_gain_one = norm_backward(normed_one_grad, scaled_one, inverse_one, gain_one)
    grad_inputs = resid_grad + attn_in_grad

    small_grads = jnp.stack([grad_gain_one, grad_gain_two, lean_grad, -lean_grad], axis=1)
    small_grads = jnp.pad(small_grads, ((0, 0), (0, 128 - small_grads.shape[1])))
    small_grads = small_grads.astype(jnp.bfloat16)
    grad_qkv, grad_out, small_grads = scatter_plane(
        [grad_qkv.astype(jnp.bfloat16), grad_out.astype(jnp.bfloat16), small_grads], 3, True
    )
    return (
        result,
        grad_inputs,
        grad_qkv,
        grad_out,
        grad_up,
        grad_down,
        small_grads[:, 0],
        small_grads[:, 1],
        small_grads[:, 2:4],
        grad_expert_up,
        grad_expert_down,
    )


def solution(mesh):
    rows, vector = P(both, None), P(both)
    experts = P("expert", "dp", None)
    return jax.shard_map(
        body,
        mesh=mesh,
        in_specs=(rows, vector, rows, rows, rows, rows, rows, vector, vector, rows, experts, experts, rows),
        out_specs=(rows, rows, rows, rows, rows, rows, vector, vector, rows, experts, experts),
        check_vma=False,
    )
```

```python
import functools

import jax
import jax.numpy as jnp
from jax import lax
from jax.experimental import pallas as pl
from jax.experimental.pallas import tpu as pltpu
from jax.sharding import PartitionSpec as P

HEADS = 16

epsilon = 1e-05
root_half = 0.7071067811865476
inv_root_two_pi = 0.3989422804014327
highest = lax.Precision.HIGHEST
both = ("dp", "expert")


def gelu_pair(values):
    half = 0.5 * (1.0 + lax.erf(values * root_half))
    return values * half, half + values * jnp.exp(-0.5 * values * values) * inv_root_two_pi


def dot(left, right, dims):
    return lax.dot_general(left, right, (dims, ((), ())), preferred_element_type=jnp.float32)


def matmul(left, right):
    return dot(left, right, ((1,), (0,)))


def matmul_nt(left, right):
    return dot(left, right, ((1,), (1,)))


def matmul_tn(left, right):
    return dot(left, right, ((0,), (0,)))


def norm_forward(values):
    row_mean = jnp.mean(values, axis=-1, keepdims=True)
    centred = values - row_mean
    row_var = jnp.mean(centred * centred, axis=-1, keepdims=True)
    inverse = lax.rsqrt(row_var + epsilon)
    return (centred * inverse, inverse)


def norm_backward(upstream, scaled, inverse, gain_row):
    gain_grad = jnp.sum(upstream * scaled, axis=0)
    inner = upstream * gain_row
    centred_grad = (
        inner
        - jnp.mean(inner, axis=-1, keepdims=True)
        - scaled * jnp.mean(inner * scaled, axis=-1, keepdims=True)
    )
    return (inverse * centred_grad, gain_grad)


def head_scores(queries, keys_all, length, row_start, scale):
    scores = matmul_nt(queries, keys_all) * scale
    rows_at = row_start + lax.broadcasted_iota(jnp.int32, scores.shape, 0)
    cols_at = lax.broadcasted_iota(jnp.int32, scores.shape, 1)
    return jnp.where((cols_at <= rows_at) & (cols_at < length), scores, -1000000000.0)


def attention_forward_kernel(head_width, bands, length_ref, q_ref, k_ref, v_ref, out_ref, log_ref):
    length = length_ref[0]
    scale = head_width ** (-0.5)
    tok_rows, lanes = q_ref.shape
    height = tok_rows // bands
    lane = lax.broadcasted_iota(jnp.int32, (1, lanes), 1) // head_width
    for band in range(bands):
        top, end = band * height, (band + 1) * height
        keys_all, values_all = k_ref[0:end, :], v_ref[0:end, :]
        queries = q_ref[top:end, :]
        mixed = jnp.zeros((height, lanes), jnp.float32)
        logs = []
        for head in range(lanes // head_width):
            mine = lane == head
            scores = head_scores(jnp.where(mine, queries, 0), keys_all, length, top, scale)
            top_score = jnp.max(scores, axis=-1, keepdims=True)
            raised = jnp.exp(scores - top_score)
            row_total = jnp.sum(raised, axis=-1, keepdims=True)
            probs = (raised / row_total).astype(jnp.bfloat16)
            mixed = mixed + matmul(probs, jnp.where(mine, values_all, 0))
            logs.append(top_score + jnp.log(row_total))
        out_ref[top:end, :] = mixed.astype(jnp.bfloat16)
        spread = jnp.broadcast_to(logs[0], (height, lanes))
        for head in range(1, len(logs)):
            spread = jnp.where(lane == head, logs[head], spread)
        log_ref[top:end, :] = spread


def attention_forward(joined, length):
    tok_rows, width = joined.shape[0], joined.shape[1] // 3
    head_width = width // HEADS
    lanes = max(128, head_width)
    tiles = width // lanes
    bands = 4

    def part(which):
        return pl.BlockSpec((tok_rows, lanes), lambda i: (0, which * tiles + i))

    return pl.pallas_call(
        functools.partial(attention_forward_kernel, head_width, bands),
        grid=(tiles,),
        out_shape=[
            jax.ShapeDtypeStruct((tok_rows, width), jnp.bfloat16),
            jax.ShapeDtypeStruct((tok_rows, width), jnp.float32),
        ],
        in_specs=[pl.BlockSpec(memory_space=pltpu.SMEM), part(0), part(1), part(2)],
        out_specs=[part(0), part(0)],
        compiler_params=pltpu.CompilerParams(vmem_limit_bytes=32 * 2**20),
        cost_estimate=pl.CostEstimate(flops=4 * tok_rows * tok_rows * width, bytes_accessed=10 * tok_rows * width, transcendentals=0),
        name="attention_forward",
    )(length, joined, joined, joined)


def attention_backward_kernel(head_width, bands, length_ref, q_ref, k_ref, v_ref, g_ref, log_ref, dq_ref, dk_ref, dv_ref, dk_sum, dv_sum):
    length = length_ref[0]
    scale = head_width ** (-0.5)
    tok_rows, lanes = q_ref.shape
    height = tok_rows // bands
    lane = lax.broadcasted_iota(jnp.int32, (1, lanes), 1) // head_width
    dk_sum[...] = jnp.zeros_like(dk_sum)
    dv_sum[...] = jnp.zeros_like(dv_sum)
    for band in range(bands):
        top, end = band * height, (band + 1) * height
        keys_all, values_all = k_ref[0:end, :], v_ref[0:end, :]
        queries, grads, logs = q_ref[top:end, :], g_ref[top:end, :], log_ref[top:end, :]
        dq = jnp.zeros((height, lanes), jnp.float32)
        for head in range(lanes // head_width):
            mine = lane == head
            own_q, own_g = jnp.where(mine, queries, 0), jnp.where(mine, grads, 0)
            log_total = logs[:, head * head_width : head * head_width + 1]
            probs = jnp.exp(head_scores(own_q, keys_all, length, top, scale) - log_total)
            dv_sum[0:end, :] += matmul_tn(probs.astype(jnp.bfloat16), own_g)
            prob_grad = matmul_nt(own_g, values_all)
            row_delta = jnp.sum(prob_grad * probs, axis=-1, keepdims=True)
            score_grad = (probs * (prob_grad - row_delta)).astype(jnp.bfloat16)
            dq = dq + matmul(score_grad, jnp.where(mine, keys_all, 0))
            dk_sum[0:end, :] += matmul_tn(score_grad, own_q)
        dq_ref[top:end, :] = (dq * scale).astype(jnp.bfloat16)
    dk_ref[...] = (dk_sum[...] * scale).astype(jnp.bfloat16)
    dv_ref[...] = dv_sum[...].astype(jnp.bfloat16)


def attention_backward(joined, heads_grad, log_total, length):
    tok_rows, width = joined.shape[0], joined.shape[1] // 3
    head_width = width // HEADS
    lanes = max(128, head_width)
    tiles = width // lanes
    bands = 4

    def part(which):
        return pl.BlockSpec((tok_rows, lanes), lambda i: (0, which * tiles + i))

    return pl.pallas_call(
        functools.partial(attention_backward_kernel, head_width, bands),
        grid=(tiles,),
        out_shape=[jax.ShapeDtypeStruct((tok_rows, width), jnp.bfloat16)] * 3,
        in_specs=[pl.BlockSpec(memory_space=pltpu.SMEM), part(0), part(1), part(2), part(0), part(0)],
        out_specs=[part(0)] * 3,
        scratch_shapes=[pltpu.VMEM((tok_rows, lanes), jnp.float32)] * 2,
        compiler_params=pltpu.CompilerParams(vmem_limit_bytes=32 * 2**20),
        cost_estimate=pl.CostEstimate(flops=10 * tok_rows * tok_rows * width, bytes_accessed=20 * tok_rows * width, transcendentals=0),
        name="attention_backward",
    )(length, joined, joined, joined, heads_grad, log_total)


def expert_kernel(rows_ref, pulled_ref, up_ref, down_ref, small_ref, lean_ref, act_ref, pre_ref, grad_ref, in_ref, sum_ref):
    rows_in, pulled = rows_ref[...], pulled_ref[...]
    logits = matmul(rows_in, small_ref[...])
    first, second = logits[:, 2:3], logits[:, 3:4]
    top = jnp.maximum(first, second)
    first, second = jnp.exp(first - top), jnp.exp(second - top)
    mix_dense, mix_expert = first / (first + second), second / (first + second)
    pre_act = matmul(rows_in, up_ref[...])
    act_pull = matmul_nt(pulled, down_ref[...])
    gelu, slope = gelu_pair(pre_act)
    act = gelu.astype(jnp.bfloat16)
    act_ref[...] = act
    lean = mix_dense * mix_expert * jnp.sum(act.astype(jnp.float32) * act_pull, axis=1, keepdims=True)
    pre_grad = (mix_expert * act_pull * slope).astype(jnp.bfloat16)
    pre_ref[...] = pre_grad
    in_ref[...] = (matmul_nt(pre_grad, up_ref[...]) - lean * lean_ref[...]).astype(jnp.bfloat16)
    grad_ref[...] = (pulled.astype(jnp.float32) * mix_expert).astype(jnp.bfloat16)
    part = jnp.sum(rows_in.astype(jnp.float32) * lean, axis=0, keepdims=True)
    sum_ref[...] = jnp.where(pl.program_id(0) == 0, part, sum_ref[...] + part)


def expert_branch(rows_in, pulled_rows, up_part, down_part, small_full, mix_lean):
    count, width = rows_in.shape
    hidden = up_part.shape[1]
    height = 256

    def tall(columns):
        return pl.BlockSpec((height, columns), lambda i: (i, 0))

    def whole(array):
        return pl.BlockSpec(array.shape, lambda i: (0, 0))

    low = jnp.bfloat16
    return pl.pallas_call(
        expert_kernel,
        grid=(count // height,),
        out_shape=[
            jax.ShapeDtypeStruct((count, hidden), low),
            jax.ShapeDtypeStruct((count, hidden), low),
            jax.ShapeDtypeStruct((count, width), low),
            jax.ShapeDtypeStruct((count, width), low),
            jax.ShapeDtypeStruct((1, width), jnp.float32),
        ],
        in_specs=[tall(width), tall(width), whole(up_part), whole(down_part), whole(small_full), whole(mix_lean)],
        out_specs=[tall(hidden), tall(hidden), tall(width), tall(width), whole(mix_lean)],
        compiler_params=pltpu.CompilerParams(vmem_limit_bytes=48 * 2**20),
        cost_estimate=pl.CostEstimate(
            flops=6 * count * width * hidden, bytes_accessed=12 * count * width, transcendentals=0
        ),
        name="expert_branch",
    )(rows_in, pulled_rows, up_part, down_part, small_full, mix_lean)


def dense_kernel(normed_ref, up_ref, down_ref, grad_ref, mix_ref, gdown_ref, gup_ref, ngrad_ref, out_ref, pull_ref):
    normed, upstream, mix = normed_ref[...], grad_ref[...], mix_ref[...]
    hidden = matmul(normed, up_ref[...])
    dense_pull = matmul_nt(upstream, down_ref[...])
    gelu, slope = gelu_pair(hidden)
    act = gelu.astype(jnp.bfloat16)
    pull = jnp.sum(act.astype(jnp.float32) * dense_pull, axis=1, keepdims=True)
    hidden_grad = (mix * dense_pull * slope).astype(jnp.bfloat16)
    grad_out = (upstream.astype(jnp.float32) * mix).astype(jnp.bfloat16)
    gdown_ref[...] = matmul_tn(act, grad_out).astype(jnp.bfloat16)
    gup_ref[...] = matmul_tn(normed, hidden_grad).astype(jnp.bfloat16)
    ngrad = matmul_nt(hidden_grad, up_ref[...])
    dense_out = matmul(act, down_ref[...])

    @pl.when(pl.program_id(0) == 0)
    def _():
        ngrad_ref[...] = ngrad
        out_ref[...] = dense_out
        pull_ref[...] = pull

    @pl.when(pl.program_id(0) > 0)
    def _():
        ngrad_ref[...] += ngrad
        out_ref[...] += dense_out
        pull_ref[...] += pull


def dense_branch(normed_two, up_full, down_full, upstream_low, mix):
    rows, width = normed_two.shape
    ff = up_full.shape[1]
    block = 512

    def whole(columns):
        return pl.BlockSpec((rows, columns), lambda i: (0, 0))

    across, down = pl.BlockSpec((width, block), lambda i: (0, i)), pl.BlockSpec((block, width), lambda i: (i, 0))
    return pl.pallas_call(
        dense_kernel,
        grid=(ff // block,),
        out_shape=[
            jax.ShapeDtypeStruct((ff, width), jnp.bfloat16),
            jax.ShapeDtypeStruct((width, ff), jnp.bfloat16),
            jax.ShapeDtypeStruct((rows, width), jnp.float32),
            jax.ShapeDtypeStruct((rows, width), jnp.float32),
            jax.ShapeDtypeStruct((rows, 1), jnp.float32),
        ],
        in_specs=[whole(width), across, down, whole(width), whole(1)],
        out_specs=[down, across, whole(width), whole(width), whole(1)],
        compiler_params=pltpu.CompilerParams(vmem_limit_bytes=48 * 2**20),
        cost_estimate=pl.CostEstimate(flops=12 * rows * width * ff, bytes_accessed=8 * width * ff, transcendentals=0),
        name="dense_branch",
    )(normed_two, up_full, down_full, upstream_low, mix)


MESH = pl.DeviceIdType.MESH


def plane():
    here = lax.axis_index("expert")
    core, x, y = here % 2, (here // 2) % 2, here // 4
    return here // 2, core, x, y, here + 1 - 2 * core, here + 2 - 4 * x, here + 4 - 8 * y


def greet(depth, others, count):
    level = lax.axis_index("dp")
    barrier = pltpu.get_barrier_semaphore()
    for other in others:
        pl.semaphore_signal(barrier, inc=1, device_id=(level, other), device_id_type=MESH)
    if count:
        for step in range(1, depth):
            pl.semaphore_signal(
                barrier,
                inc=1,
                device_id=((level + step) % depth, lax.axis_index("expert")),
                device_id_type=MESH,
            )
    pl.semaphore_wait(barrier, len(others) + (depth - 1 if count else 0))


def remote(source, target, sems, slot, level, where):
    return pltpu.make_async_remote_copy(
        src_ref=source,
        dst_ref=target,
        send_sem=sems[0].at[slot],
        recv_sem=sems[1].at[slot],
        device_id=(level, where),
        device_id_type=MESH,
    )


def gather_kernel(depth, count, more, *refs):
    shards, refs = refs[:count], refs[count:]
    if more:
        wide, picked, refs = refs[0], refs[1], refs[2:]
    fulls, refs = refs[:count], refs[count:]
    if more:
        parts, arrived, refs = refs[0], refs[1], refs[2:]
    keep, sems = refs[0], refs[1:]
    z_sems, x_sems, y_sems, d_sems, c_sems, w_sems, p_sems = (sems[2 * i : 2 * i + 2] for i in range(7))
    level, here = lax.axis_index("dp"), lax.axis_index("expert")
    chip, core, x, y, twin, x_next, y_next = plane()
    x_chip, y_chip, far_chip = chip + 1 - 2 * x, chip + 2 - 4 * y, 3 - chip
    mates = [(here + step) % 8 for step in range(1, 8)] if more else (twin, x_next, y_next)
    greet(depth, mates, True)
    started, locals_ = [], []

    def send(*a):
        copy = remote(*a)
        copy.start()
        started.append(copy)

    def stay(source, target, slot):
        copy = pltpu.make_async_copy(source, target, keep.at[slot])
        copy.start()
        locals_.append(copy)

    def to_twin(i, step, chip_at, source=None):
        spot = fulls[i].at[(level + depth - step) % depth, chip_at, core]
        send(spot if source is None else source, spot, c_sems, (i, step, chip_at), level, twin)

    for step in range(1, depth):
        for i in range(count):
            send(shards[i], fulls[i].at[level, chip, core], z_sems, (i, step), (level + step) % depth, here)
    for i in range(count):
        stay(shards[i], fulls[i].at[level, chip, core], i)
    for step in range(depth):
        source = (level + depth - step) % depth
        for i in range(count):
            spot = fulls[i].at[source, chip, core]
            if step:
                remote(shards[i], spot, z_sems, (i, step), level, here).wait_recv()
            origin = spot if step else shards[i]
            send(origin, spot, x_sems, (i, step), level, x_next)
            send(origin, spot, y_sems, (i, step), level, y_next)
            to_twin(i, step, chip, origin)
        if more and step == 0:
            width = wide.shape[1] // depth

            def columns(at):
                return wide.at[:, pl.ds(pl.multiple_of(at * width, width), width)]

            for way in range(1, depth):
                target = (level + way) % depth
                send(columns(target), parts.at[level], w_sems, (way,), target, here)
            stay(columns(level), parts.at[level], count)
            for way in range(1, 8):
                mate = (here + way) % 8
                send(picked.at[mate], arrived.at[here], p_sems, (way,), level, mate)
            stay(picked.at[here], arrived.at[here], count + 1)
    for step in range(depth):
        source = (level + depth - step) % depth
        for i in range(count):
            x_spot, y_spot = fulls[i].at[source, x_chip, core], fulls[i].at[source, y_chip, core]
            remote(shards[i], x_spot, x_sems, (i, step), level, here).wait_recv()
            if step % 2 == 0:
                send(x_spot, x_spot, d_sems, (i, step), level, y_next)
            to_twin(i, step, x_chip)
            remote(shards[i], y_spot, y_sems, (i, step), level, here).wait_recv()
            if step % 2 == 1:
                send(y_spot, y_spot, d_sems, (i, step), level, x_next)
            to_twin(i, step, y_chip)
    for step in range(depth):
        source = (level + depth - step) % depth
        for i in range(count):
            spot = fulls[i].at[source, far_chip, core]
            remote(shards[i], spot, d_sems, (i, step), level, here).wait_recv()
            to_twin(i, step, far_chip)
    for step in range(depth):
        source = (level + depth - step) % depth
        for i in range(count):
            for chip_at in range(4):
                spot = fulls[i].at[source, chip_at, 1 - core]
                remote(shards[i], spot, c_sems, (i, step, chip_at), level, here).wait_recv()
    if more:
        for way in range(1, depth):
            spot = parts.at[(level + depth - way) % depth]
            remote(columns(level), spot, w_sems, (way,), level, here).wait_recv()
        for way in range(1, 8):
            spot = arrived.at[(here + 8 - way) % 8]
            remote(picked.at[here], spot, p_sems, (way,), level, here).wait_recv()
    for copy in locals_:
        copy.wait()
    for copy in started:
        copy.wait_send()


def gather_plane(shards, ident, wide=None, picked=None):
    depth, count, more = lax.axis_size("dp"), len(shards), wide is not None
    if lax.axis_size("expert") != 8:
        fulls = [lax.all_gather(s, both, axis=0, tiled=True) for s in shards]
        if more:
            fulls.append(lax.all_to_all(wide, "dp", split_axis=1, concat_axis=0, tiled=True))
            fulls.append(lax.all_to_all(picked, "expert", split_axis=0, concat_axis=0, tiled=True))
        return fulls
    extra, extra_out = [], []
    if more:
        extra = [wide, picked]
        extra_out = [
            jax.ShapeDtypeStruct((depth, wide.shape[0], wide.shape[1] // depth), wide.dtype),
            jax.ShapeDtypeStruct(picked.shape, picked.dtype),
        ]
    kinds = []
    for shape in ((count, depth),) * 4 + ((count, depth, 4), (depth,), (8,)):
        kinds += [pltpu.SemaphoreType.DMA(shape)] * 2
    fulls = pl.pallas_call(
        functools.partial(gather_kernel, depth, count, more),
        out_shape=[jax.ShapeDtypeStruct((depth, 4, 2) + s.shape, s.dtype) for s in shards] + extra_out,
        in_specs=[pl.BlockSpec(memory_space=pl.ANY)] * (count + len(extra)),
        out_specs=[pl.BlockSpec(memory_space=pl.ANY)] * (count + len(extra)),
        scratch_shapes=[pltpu.SemaphoreType.DMA((count + 2,))] + kinds,
        compiler_params=pltpu.CompilerParams(collective_id=ident, has_side_effects=True),
        cost_estimate=pl.CostEstimate(flops=1, bytes_accessed=1, transcendentals=0),
        name=f"gather_plane_{ident}",
    )(*shards, *extra)
    full = [f.reshape((-1,) + s.shape[1:]) for f, s in zip(fulls, shards)]
    if more:
        full += [fulls[count].reshape((-1, extra_out[0].shape[2])), fulls[count + 1]]
    return full


def scatter_kernel(depth, count, with_z, work, *refs):
    grads, refs = refs[:count], refs[count:]
    if with_z:
        tall, refs = refs[0], refs[1:]
    if work:
        operands, refs = refs[:5], refs[5:]
    outs, refs = refs[:count], refs[count:]
    if work:
        results, buffers, refs = refs[:3], refs[-8:], refs[3:-8]
    if with_z:
        parts, keep, w_sems, refs = refs[0], refs[-1], refs[-3:-1], refs[1:-3]
    own, twins, first, second = (refs[i * count : (i + 1) * count] for i in range(4))
    n = 4 * count
    levels = refs[n : n + count] if with_z else ()
    n += len(levels)
    load, c_sems, f_sems, s_sems = refs[n], refs[n + 1 : n + 3], refs[n + 3 : n + 5], refs[n + 5 : n + 7]
    z_sems = refs[n + 7 : n + 9]
    level, here = lax.axis_index("dp"), lax.axis_index("expert")
    chip, core, x, y, twin, x_next, y_next = plane()
    greet(depth, (twin, x_next, y_next), with_z)
    started, loads = [], {}

    def send(*a):
        copy = remote(*a)
        copy.start()
        started.append(copy)

    if with_z:
        width = tall.shape[2]

        def columns(at):
            return parts.at[:, pl.ds(pl.multiple_of(at * width, width), width)]

        for way in range(1, depth):
            target = (level + way) % depth
            send(tall.at[target], columns(level), w_sems, (way,), target, here)
        kept = pltpu.make_async_copy(tall.at[level], columns(level), keep.at[0])
        kept.start()
    order = [(step, (step + level + 1) % depth) for step in range(depth)]
    for step, at in order:
        for i in range(count):
            send(grads[i].at[at, :, 1 - core], twins[i].at[step], c_sems, (i, step), level, twin)
            loads[i, step] = pltpu.make_async_copy(grads[i].at[at, :, core], own[i].at[step], load.at[i, step])
            loads[i, step].start()
    jobs = expert_work(operands, results, buffers) if work else iter(())

    def add(target, other):
        target[...] = (target[...].astype(jnp.float32) + other[...].astype(jnp.float32)).astype(jnp.bfloat16)

    def chips(step):
        if step % 2 == 0:
            return (1 - x, 3 - x), (x, 2 + x), x_next, y_next
        return (2 - 2 * y, 3 - 2 * y), (2 * y, 2 * y + 1), y_next, x_next

    for step, at in order:
        away, near, first_next, second_next = chips(step)
        for i in range(count):
            loads[i, step].wait()
            remote(own[i].at[step], twins[i].at[step], c_sems, (i, step), level, here).wait_recv()
            for side in range(2):
                add(own[i].at[step, away[side]], twins[i].at[step, away[side]])
                send(own[i].at[step, away[side]], first[i].at[step, side], f_sems, (i, step, side), level, first_next)
        for i in range(count):
            for side in range(2):
                add(own[i].at[step, near[side]], twins[i].at[step, near[side]])
    next(jobs, None)
    next(jobs, None)
    for step, at in order:
        away, near, first_next, second_next = chips(step)
        for i in range(count):
            for side in range(2):
                remote(own[i].at[step, 0], first[i].at[step, side], f_sems, (i, step, side), level, here).wait_recv()
                add(own[i].at[step, near[side]], first[i].at[step, side])
            across = chip + 2 - 4 * y if step % 2 == 0 else chip + 1 - 2 * x
            send(own[i].at[step, across], second[i].at[step], s_sems, (i, step), level, second_next)
        if step == 1:
            next(jobs, None)
    for _ in jobs:
        pass
    for step, at in order:
        for i in range(count):
            remote(own[i].at[step, 0], second[i].at[step], s_sems, (i, step), level, here).wait_recv()
            add(second[i].at[step], own[i].at[step, chip])
            if with_z:
                if step < depth - 1:
                    send(second[i].at[step], levels[i].at[step], z_sems, (i, step), at, here)
            else:
                outs[i][at] = second[i][step]
    if with_z:
        for i in range(count):
            total = second[i][depth - 1].astype(jnp.float32)
            for step in range(depth - 1):
                remote(second[i].at[step], levels[i].at[step], z_sems, (i, step), level, here).wait_recv()
                total = total + levels[i][step].astype(jnp.float32)
            outs[i][...] = total
        for way in range(1, depth):
            spot = columns((level + depth - way) % depth)
            remote(tall.at[level], spot, w_sems, (way,), level, here).wait_recv()
        kept.wait()
    for copy in started:
        copy.wait_send()


def expert_work(operands, results, buffers):
    act, grads, rows_in, pre_grad, down = operands
    act_at, grads_at, rows_at, pre_at, down_at, tall, low, sems = buffers
    pairs = ((act, act_at), (grads, grads_at), (down, down_at), (rows_in, rows_at), (pre_grad, pre_at))
    copies = [pltpu.make_async_copy(a, b, sems.at[i]) for i, (a, b) in enumerate(pairs)]
    for copy in copies:
        copy.start()
    width = act.shape[1]
    tile = tall.shape[1]
    height = low.shape[1]
    flights = []

    def put(slot, stage, target, sem):
        copy = pltpu.make_async_copy(stage.at[slot], target, sems.at[sem + slot])
        copy.start()
        flights.append(copy)

    def settle(keep):
        while len(flights) > keep:
            flights.pop(0).wait()

    copies[0].wait()
    copies[1].wait()
    for i in range(width // tile):
        settle(1)
        tall[i % 2] = matmul_tn(act_at[:, i * tile : (i + 1) * tile], grads_at[...])
        put(i % 2, tall, results[0].at[i * tile : (i + 1) * tile], 5)
    yield
    copies[2].wait()
    settle(0)
    for i in range(act.shape[0] // height):
        settle(1)
        low[i % 2] = matmul(act_at[i * height : (i + 1) * height, :], down_at[...]).astype(jnp.bfloat16)
        put(i % 2, low, results[2].at[i * height : (i + 1) * height], 7)
    yield
    settle(0)
    copies[3].wait()
    copies[4].wait()
    for i in range(width // tile):
        settle(1)
        low[i % 2, 0:tile] = matmul_tn(rows_at[:, i * tile : (i + 1) * tile], pre_at[...]).astype(jnp.bfloat16)
        copy = pltpu.make_async_copy(low.at[i % 2, 0:tile], results[1].at[i * tile : (i + 1) * tile], sems.at[7 + i % 2])
        copy.start()
        flights.append(copy)
    yield
    settle(0)


def scatter_plane(grads, ident, work=None, tall=None):
    depth, count, with_z = lax.axis_size("dp"), len(grads), tall is not None
    low = jnp.bfloat16
    if lax.axis_size("expert") != 8:
        sums = [lax.psum_scatter(g, both, scatter_dimension=0, tiled=True).astype(jnp.float32) for g in grads]
        if work is not None:
            act, grad_rows, rows_in, pre_grad, down = work
            sums.append(matmul_tn(act, grad_rows))
            sums.append(matmul_tn(rows_in, pre_grad).astype(low))
            sums.append(matmul(act, down).astype(low))
        if with_z:
            sums.append(lax.all_to_all(tall, "dp", split_axis=0, concat_axis=1, tiled=True))
        return sums
    grads = [g.reshape((depth, 4, 2, g.shape[0] // (8 * depth)) + g.shape[1:]) for g in grads]
    blocks = [g.shape[3:] for g in grads]
    scratch = [pltpu.VMEM((depth, 4) + b, low) for b in blocks] * 2
    scratch += [pltpu.VMEM((depth, 2) + b, low) for b in blocks]
    scratch += [pltpu.VMEM((depth,) + b, low) for b in blocks]
    if with_z:
        scratch += [pltpu.VMEM((depth - 1,) + b, low) for b in blocks]
    sems = [pltpu.SemaphoreType.DMA((count, depth))] * 3 + [pltpu.SemaphoreType.DMA((count, depth, 2))] * 2
    sems += [pltpu.SemaphoreType.DMA((count, depth))] * 2
    operands, made = (), []
    if with_z:
        sems += [pltpu.SemaphoreType.DMA((count, depth))] * 2
        sems += [pltpu.SemaphoreType.DMA((depth,))] * 2 + [pltpu.SemaphoreType.DMA((1,))]
        operands = (tall.reshape((depth, -1, tall.shape[1])),)
        made = [jax.ShapeDtypeStruct((tall.shape[0] // depth, tall.shape[1] * depth), tall.dtype)]
    if work is not None:
        operands = tuple(work)
        act, down = work[0], work[4]
        made = [
            jax.ShapeDtypeStruct((act.shape[1], act.shape[1]), jnp.float32),
            jax.ShapeDtypeStruct((act.shape[1], work[3].shape[1]), low),
            jax.ShapeDtypeStruct((act.shape[0], down.shape[1]), low),
        ]
        sems += [pltpu.VMEM(o.shape, o.dtype) for o in operands]
        sems += [
            pltpu.VMEM((2, 256, down.shape[1]), jnp.float32),
            pltpu.VMEM((2, act.shape[0] // 4, down.shape[1]), low),
            pltpu.SemaphoreType.DMA((9,)),
        ]
    return list(
        pl.pallas_call(
            functools.partial(scatter_kernel, depth, count, with_z, work is not None),
            out_shape=[
                jax.ShapeDtypeStruct(b, jnp.float32) if with_z else jax.ShapeDtypeStruct((depth,) + b, low) for b in blocks
            ]
            + made,
            in_specs=[pl.BlockSpec(memory_space=pl.ANY)] * (count + len(operands)),
            out_specs=[pl.BlockSpec(memory_space=pltpu.VMEM)] * count + [pl.BlockSpec(memory_space=pl.ANY)] * len(made),
            scratch_shapes=scratch + sems,
            compiler_params=pltpu.CompilerParams(
                collective_id=ident, has_side_effects=True, vmem_limit_bytes=(32 if with_z else 58) * 2**20
            ),
            cost_estimate=pl.CostEstimate(flops=1, bytes_accessed=200 * 2**20, transcendentals=0),
            name=f"scatter_plane_{ident}",
        )(*grads, *operands)
    )


def finish_scatter(sums):
    if lax.axis_size("expert") != 8:
        return sums
    return [lax.psum_scatter(s, "dp", scatter_dimension=0).astype(jnp.float32) for s in sums]


def body(
    tokens,
    seq_lengths,
    routes,
    w_qkv,
    w_out,
    w_up,
    w_down,
    gain_attn,
    gain_mlp,
    w_mix,
    expert_up,
    expert_down,
    cotangent,
):
    tok_rows, model_width = tokens.shape
    axis_dp, axis_experts = lax.axis_size("dp"), lax.axis_size("expert")
    expert_total = axis_experts * expert_up.shape[0]
    capacity = max(2, 5 * tok_rows // (4 * expert_total))
    slots = expert_total * capacity
    ff_expert = expert_up.shape[2]

    small = jnp.concatenate([gain_attn[:, None], gain_mlp[:, None], w_mix], axis=1)
    small = jnp.pad(small, ((0, 0), (0, 128 - small.shape[1])))
    length = seq_lengths[0]
    valid_rows = jnp.arange(tok_rows, dtype=jnp.int32) < length

    route_ids = routes[:, 0]
    expert_ids = jnp.arange(expert_total, dtype=jnp.int32)
    route_hits = (route_ids[:, None] == expert_ids[None, :]) & valid_rows[:, None]
    route_ranks = jnp.cumsum(route_hits.astype(jnp.int32), axis=0) - 1
    chosen = jnp.sum(jnp.where(route_hits, route_ranks, 0), axis=1)
    kept_rows = valid_rows & (chosen < capacity)
    slot_ids = route_ids * capacity + chosen
    slot_table = (
        (jnp.arange(slots, dtype=jnp.int32)[:, None] == slot_ids[None, :]) & kept_rows[None, :]
    ).astype(jnp.bfloat16)

    def pick(rows):
        return matmul(slot_table, rows).astype(jnp.bfloat16).reshape(expert_total, capacity, model_width)

    def dispatch(rows):
        arrived = lax.all_to_all(pick(rows), "expert", split_axis=0, concat_axis=0, tiled=True)
        return arrived.reshape(slots, model_width)

    def spread(rows):
        return lax.all_gather(rows, "dp", axis=0, tiled=True)

    def unspread(rows):
        return lax.psum_scatter(rows, "dp", scatter_dimension=0, tiled=True)

    def give_back(summed):
        summed = summed.reshape(expert_total, capacity, model_width)
        back = lax.all_to_all(summed, "expert", split_axis=0, concat_axis=0, tiled=True)
        return matmul_tn(slot_table, back.reshape(slots, model_width))

    down_part = expert_down[0]

    upstream_low = jnp.where(valid_rows[:, None], cotangent, jnp.zeros_like(cotangent))
    upstream = upstream_low.astype(jnp.float32)
    qkv_full, out_full, small_full, up_part, pulled_here = gather_plane(
        [w_qkv, w_out, small], 0, expert_up[0], pick(upstream_low)
    )
    pulled_rows = spread(pulled_here.reshape(slots, model_width))
    gain_one = small_full[:, 0].astype(jnp.float32)
    gain_two = small_full[:, 1].astype(jnp.float32)
    mix_full = small_full[:, 2:4]
    mix_lean = (mix_full[:, 0] - mix_full[:, 1].astype(jnp.float32)).astype(jnp.float32)

    inputs = tokens.astype(jnp.float32)
    scaled_one, inverse_one = norm_forward(inputs)
    normed_one = (scaled_one * gain_one).astype(jnp.bfloat16)
    joined = matmul(normed_one, qkv_full).astype(jnp.bfloat16)
    heads_out, log_total = attention_forward(joined, seq_lengths)
    after_attn = inputs + matmul(heads_out, out_full)
    scaled_two, inverse_two = norm_forward(after_attn)
    normed_two = (scaled_two * gain_two).astype(jnp.bfloat16)

    rows_here = dispatch(normed_two)
    rows_here, w_up, w_down = lax.optimization_barrier((rows_here, w_up, w_down))
    rows_in = spread(rows_here)
    up_full, down_full = gather_plane([w_up, w_down], 1)

    pulled_rows, up_full, down_full = lax.optimization_barrier((pulled_rows, up_full, down_full))
    mix_weights = jax.nn.softmax(matmul(normed_two, mix_full), axis=-1)
    grad_down, grad_up, normed_grad, dense_out, pull_dense = dense_branch(
        normed_two, up_full, down_full, upstream_low, mix_weights[:, 0:1]
    )
    lean_dense = mix_weights[:, 0:1] * mix_weights[:, 1:2] * pull_dense
    normed_grad = normed_grad + lean_dense * mix_lean[None, :]

    rows_in, grad_up, grad_down, normed_grad = lax.optimization_barrier((rows_in, grad_up, grad_down, normed_grad))
    act_rows, pre_grad, grad_rows, input_grad, lean_rows = expert_branch(
        rows_in, pulled_rows, up_part, down_part, small_full, mix_lean[None, :]
    )
    in_grad_here = unspread(input_grad)
    up_sums, down_sums, grad_expert_down, grad_expert_up, made = scatter_plane(
        [grad_up, grad_down], 2, (act_rows, grad_rows, rows_in, pre_grad, down_part)
    )
    grad_expert_down = grad_expert_down[None]
    in_grad_here, up_sums, down_sums = lax.optimization_barrier((in_grad_here, up_sums, down_sums))
    grad_up, grad_down = finish_scatter([up_sums, down_sums])
    in_grad_here, made = lax.optimization_barrier((in_grad_here, made))
    expert_out = give_back(unspread(made))
    result = after_attn + mix_weights[:, 0:1] * dense_out + mix_weights[:, 1:2] * expert_out
    in_grad_back = give_back(in_grad_here)

    normed_grad = normed_grad + in_grad_back
    lean_grad = jnp.sum(normed_two.astype(jnp.float32) * lean_dense, axis=0) - lean_rows[0]
    mlp_in_grad, grad_gain_two = norm_backward(normed_grad, scaled_two, inverse_two, gain_two)
    resid_grad = upstream + mlp_in_grad
    attn_grad = resid_grad.astype(jnp.bfloat16)
    grad_out = matmul_tn(heads_out, attn_grad)
    heads_grad = matmul_nt(attn_grad, out_full).astype(jnp.bfloat16)
    joined_grad = jnp.concatenate(
        attention_backward(joined, heads_grad, log_total, seq_lengths), axis=1
    )
    grad_qkv = matmul_tn(normed_one, joined_grad)
    normed_one_grad = matmul_nt(joined_grad, qkv_full)
    attn_in_grad, grad_gain_one = norm_backward(normed_one_grad, scaled_one, inverse_one, gain_one)
    grad_inputs = resid_grad + attn_in_grad

    small_grads = jnp.stack([grad_gain_one, grad_gain_two, lean_grad, -lean_grad], axis=1)
    small_grads = jnp.pad(small_grads, ((0, 0), (0, 128 - small_grads.shape[1])))
    small_grads = small_grads.astype(jnp.bfloat16)
    grad_qkv, grad_out, small_grads, grad_expert_up = scatter_plane(
        [grad_qkv.astype(jnp.bfloat16), grad_out.astype(jnp.bfloat16), small_grads], 3, tall=grad_expert_up
    )
    grad_expert_up = grad_expert_up.astype(jnp.float32)[None]
    return (
        result,
        grad_inputs,
        grad_qkv,
        grad_out,
        grad_up,
        grad_down,
        small_grads[:, 0],
        small_grads[:, 1],
        small_grads[:, 2:4],
        grad_expert_up,
        grad_expert_down,
    )


def solution(mesh):
    rows, vector = P(both, None), P(both)
    experts = P("expert", "dp", None)
    return jax.shard_map(
        body,
        mesh=mesh,
        in_specs=(rows, vector, rows, rows, rows, rows, rows, vector, vector, rows, experts, experts, rows),
        out_specs=(rows, rows, rows, rows, rows, rows, vector, vector, rows, experts, experts),
        check_vma=False,
    )
```

```python
import functools

import jax
import jax.numpy as jnp
from jax import lax
from jax.experimental import pallas as pl
from jax.experimental.pallas import tpu as pltpu
from jax.sharding import PartitionSpec as P

HEADS = 16

epsilon = 1e-05
root_half = 0.7071067811865476
inv_root_two_pi = 0.3989422804014327
highest = lax.Precision.HIGHEST
both = ("dp", "expert")


def gelu_pair(values):
    half = 0.5 * (1.0 + lax.erf(values * root_half))
    return values * half, half + values * jnp.exp(-0.5 * values * values) * inv_root_two_pi


def dot(left, right, dims):
    return lax.dot_general(left, right, (dims, ((), ())), preferred_element_type=jnp.float32)


def matmul(left, right):
    return dot(left, right, ((1,), (0,)))


def matmul_nt(left, right):
    return dot(left, right, ((1,), (1,)))


def matmul_tn(left, right):
    return dot(left, right, ((0,), (0,)))


def norm_forward(values):
    row_mean = jnp.mean(values, axis=-1, keepdims=True)
    centred = values - row_mean
    row_var = jnp.mean(centred * centred, axis=-1, keepdims=True)
    inverse = lax.rsqrt(row_var + epsilon)
    return (centred * inverse, inverse)


def norm_backward(upstream, scaled, inverse, gain_row):
    gain_grad = jnp.sum(upstream * scaled, axis=0)
    inner = upstream * gain_row
    centred_grad = (
        inner
        - jnp.mean(inner, axis=-1, keepdims=True)
        - scaled * jnp.mean(inner * scaled, axis=-1, keepdims=True)
    )
    return (inverse * centred_grad, gain_grad)


def head_scores(queries, keys_all, length, row_start, scale):
    scores = matmul_nt(queries, keys_all) * scale
    rows_at = row_start + lax.broadcasted_iota(jnp.int32, scores.shape, 0)
    cols_at = lax.broadcasted_iota(jnp.int32, scores.shape, 1)
    return jnp.where((cols_at <= rows_at) & (cols_at < length), scores, -1000000000.0)


def attention_forward_kernel(head_width, bands, length_ref, q_ref, k_ref, v_ref, out_ref, log_ref):
    length = length_ref[0]
    scale = head_width ** (-0.5)
    tok_rows, lanes = q_ref.shape
    height = tok_rows // bands
    lane = lax.broadcasted_iota(jnp.int32, (1, lanes), 1) // head_width
    for band in range(bands):
        top, end = band * height, (band + 1) * height
        keys_all, values_all = k_ref[0:end, :], v_ref[0:end, :]
        queries = q_ref[top:end, :]
        mixed = jnp.zeros((height, lanes), jnp.float32)
        logs = []
        for head in range(lanes // head_width):
            mine = lane == head
            scores = head_scores(jnp.where(mine, queries, 0), keys_all, length, top, scale)
            top_score = jnp.max(scores, axis=-1, keepdims=True)
            raised = jnp.exp(scores - top_score)
            row_total = jnp.sum(raised, axis=-1, keepdims=True)
            probs = (raised / row_total).astype(jnp.bfloat16)
            mixed = mixed + matmul(probs, jnp.where(mine, values_all, 0))
            logs.append(top_score + jnp.log(row_total))
        out_ref[top:end, :] = mixed.astype(jnp.bfloat16)
        spread = jnp.broadcast_to(logs[0], (height, lanes))
        for head in range(1, len(logs)):
            spread = jnp.where(lane == head, logs[head], spread)
        log_ref[top:end, :] = spread


def attention_forward(joined, length):
    tok_rows, width = joined.shape[0], joined.shape[1] // 3
    head_width = width // HEADS
    lanes = max(128, head_width)
    tiles = width // lanes
    bands = 2

    def part(which):
        return pl.BlockSpec((tok_rows, lanes), lambda i: (0, which * tiles + i))

    return pl.pallas_call(
        functools.partial(attention_forward_kernel, head_width, bands),
        grid=(tiles,),
        out_shape=[
            jax.ShapeDtypeStruct((tok_rows, width), jnp.bfloat16),
            jax.ShapeDtypeStruct((tok_rows, width), jnp.float32),
        ],
        in_specs=[pl.BlockSpec(memory_space=pltpu.SMEM), part(0), part(1), part(2)],
        out_specs=[part(0), part(0)],
        compiler_params=pltpu.CompilerParams(vmem_limit_bytes=32 * 2**20),
        cost_estimate=pl.CostEstimate(flops=4 * tok_rows * tok_rows * width, bytes_accessed=10 * tok_rows * width, transcendentals=0),
        name="attention_forward",
    )(length, joined, joined, joined)


def attention_backward_kernel(head_width, bands, length_ref, q_ref, k_ref, v_ref, g_ref, o_ref, log_ref, dq_ref, dk_ref, dv_ref, dk_sum, dv_sum):
    length = length_ref[0]
    scale = head_width ** (-0.5)
    tok_rows, lanes = q_ref.shape
    height = tok_rows // bands
    lane = lax.broadcasted_iota(jnp.int32, (1, lanes), 1) // head_width
    for band in range(bands):
        top, end = band * height, (band + 1) * height
        keys_all, values_all = k_ref[0:end, :], v_ref[0:end, :]
        queries, grads = q_ref[top:end, :], g_ref[top:end, :]
        turned = lax.transpose(log_ref[top:end, :], (1, 0))
        products = lax.transpose(grads.astype(jnp.float32) * o_ref[top:end, :].astype(jnp.float32), (1, 0))
        dq = jnp.zeros((height, lanes), jnp.float32)
        dk = jnp.zeros((end, lanes), jnp.float32)
        dv = jnp.zeros((end, lanes), jnp.float32)
        keys_at = lax.broadcasted_iota(jnp.int32, (end, height), 0)
        rows_at = top + lax.broadcasted_iota(jnp.int32, (end, height), 1)
        allowed = (keys_at <= rows_at) & (keys_at < length)
        for head in range(lanes // head_width):
            mine = lane == head
            own_q, own_g = jnp.where(mine, queries, 0), jnp.where(mine, grads, 0)
            log_total = turned[head * head_width : head * head_width + 1, :]
            delta = jnp.sum(products[head * head_width : (head + 1) * head_width, :], axis=0, keepdims=True)
            scores = jnp.where(allowed, matmul_nt(keys_all, own_q) * scale, -1000000000.0)
            probs = jnp.exp(scores - log_total)
            prob_grad = matmul_nt(values_all, own_g)
            score_grad = (probs * (prob_grad - delta)).astype(jnp.bfloat16)
            dv = dv + matmul(probs.astype(jnp.bfloat16), own_g)
            dk = dk + matmul(score_grad, own_q)
            dq = dq + matmul_tn(score_grad, jnp.where(mine, keys_all, 0))
        dq_ref[top:end, :] = (dq * scale).astype(jnp.bfloat16)
        if band == 0:
            dk_sum[...] = jnp.zeros_like(dk_sum)
            dv_sum[...] = jnp.zeros_like(dv_sum)
        dk_sum[0:end, :] += dk
        dv_sum[0:end, :] += dv
    dk_ref[...] = (dk_sum[...] * scale).astype(jnp.bfloat16)
    dv_ref[...] = dv_sum[...].astype(jnp.bfloat16)


def attention_backward(joined, heads_grad, heads_out, log_total, length):
    tok_rows, width = joined.shape[0], joined.shape[1] // 3
    head_width = width // HEADS
    lanes = max(128, head_width)
    tiles = width // lanes
    bands = 2

    def part(which):
        return pl.BlockSpec((tok_rows, lanes), lambda i: (0, which * tiles + i))

    return pl.pallas_call(
        functools.partial(attention_backward_kernel, head_width, bands),
        grid=(tiles,),
        out_shape=[jax.ShapeDtypeStruct((tok_rows, width), jnp.bfloat16)] * 3,
        in_specs=[pl.BlockSpec(memory_space=pltpu.SMEM), part(0), part(1), part(2), part(0), part(0), part(0)],
        out_specs=[part(0)] * 3,
        scratch_shapes=[pltpu.VMEM((tok_rows, lanes), jnp.float32)] * 2,
        compiler_params=pltpu.CompilerParams(vmem_limit_bytes=32 * 2**20),
        cost_estimate=pl.CostEstimate(flops=10 * tok_rows * tok_rows * width, bytes_accessed=20 * tok_rows * width, transcendentals=0),
        name="attention_backward",
    )(length, joined, joined, joined, heads_grad, heads_out, log_total)


def expert_kernel(rows_ref, pulled_ref, up_ref, down_ref, small_ref, lean_ref, act_ref, pre_ref, grad_ref, in_ref, sum_ref):
    rows_in, pulled = rows_ref[...], pulled_ref[...]
    logits = matmul(rows_in, small_ref[...])
    first, second = logits[:, 2:3], logits[:, 3:4]
    top = jnp.maximum(first, second)
    first, second = jnp.exp(first - top), jnp.exp(second - top)
    mix_dense, mix_expert = first / (first + second), second / (first + second)
    pre_act = matmul(rows_in, up_ref[...])
    act_pull = matmul_nt(pulled, down_ref[...])
    gelu, slope = gelu_pair(pre_act)
    act = gelu.astype(jnp.bfloat16)
    act_ref[...] = act
    lean = mix_dense * mix_expert * jnp.sum(act.astype(jnp.float32) * act_pull, axis=1, keepdims=True)
    pre_grad = (mix_expert * act_pull * slope).astype(jnp.bfloat16)
    pre_ref[...] = pre_grad
    in_ref[...] = (matmul_nt(pre_grad, up_ref[...]) - lean * lean_ref[...]).astype(jnp.bfloat16)
    grad_ref[...] = (pulled.astype(jnp.float32) * mix_expert).astype(jnp.bfloat16)
    part = jnp.sum(rows_in.astype(jnp.float32) * lean, axis=0, keepdims=True)
    sum_ref[...] = jnp.where(pl.program_id(0) == 0, part, sum_ref[...] + part)


def expert_branch(rows_in, pulled_rows, up_part, down_part, small_full, mix_lean):
    count, width = rows_in.shape
    hidden = up_part.shape[1]
    height = 256

    def tall(columns):
        return pl.BlockSpec((height, columns), lambda i: (i, 0))

    def whole(array):
        return pl.BlockSpec(array.shape, lambda i: (0, 0))

    low = jnp.bfloat16
    return pl.pallas_call(
        expert_kernel,
        grid=(count // height,),
        out_shape=[
            jax.ShapeDtypeStruct((count, hidden), low),
            jax.ShapeDtypeStruct((count, hidden), low),
            jax.ShapeDtypeStruct((count, width), low),
            jax.ShapeDtypeStruct((count, width), low),
            jax.ShapeDtypeStruct((1, width), jnp.float32),
        ],
        in_specs=[tall(width), tall(width), whole(up_part), whole(down_part), whole(small_full), whole(mix_lean)],
        out_specs=[tall(hidden), tall(hidden), tall(width), tall(width), whole(mix_lean)],
        compiler_params=pltpu.CompilerParams(vmem_limit_bytes=48 * 2**20),
        cost_estimate=pl.CostEstimate(
            flops=6 * count * width * hidden, bytes_accessed=12 * count * width, transcendentals=0
        ),
        name="expert_branch",
    )(rows_in, pulled_rows, up_part, down_part, small_full, mix_lean)


def dense_kernel(normed_ref, up_ref, down_ref, grad_ref, mix_ref, gdown_ref, gup_ref, ngrad_ref, out_ref, pull_ref):
    normed, upstream, mix = normed_ref[...], grad_ref[...], mix_ref[...]
    hidden = matmul(normed, up_ref[...])
    dense_pull = matmul_nt(upstream, down_ref[...])
    gelu, slope = gelu_pair(hidden)
    act = gelu.astype(jnp.bfloat16)
    pull = jnp.sum(act.astype(jnp.float32) * dense_pull, axis=1, keepdims=True)
    hidden_grad = (mix * dense_pull * slope).astype(jnp.bfloat16)
    grad_out = (upstream.astype(jnp.float32) * mix).astype(jnp.bfloat16)
    gdown_ref[...] = matmul_tn(act, grad_out).astype(jnp.bfloat16)
    gup_ref[...] = matmul_tn(normed, hidden_grad).astype(jnp.bfloat16)
    ngrad = matmul_nt(hidden_grad, up_ref[...])
    dense_out = matmul(act, down_ref[...])

    @pl.when(pl.program_id(0) == 0)
    def _():
        ngrad_ref[...] = ngrad
        out_ref[...] = dense_out
        pull_ref[...] = pull

    @pl.when(pl.program_id(0) > 0)
    def _():
        ngrad_ref[...] += ngrad
        out_ref[...] += dense_out
        pull_ref[...] += pull


def dense_branch(normed_two, up_full, down_full, upstream_low, mix):
    rows, width = normed_two.shape
    ff = up_full.shape[1]
    block = 512

    def whole(columns):
        return pl.BlockSpec((rows, columns), lambda i: (0, 0))

    across, down = pl.BlockSpec((width, block), lambda i: (0, i)), pl.BlockSpec((block, width), lambda i: (i, 0))
    return pl.pallas_call(
        dense_kernel,
        grid=(ff // block,),
        out_shape=[
            jax.ShapeDtypeStruct((ff, width), jnp.bfloat16),
            jax.ShapeDtypeStruct((width, ff), jnp.bfloat16),
            jax.ShapeDtypeStruct((rows, width), jnp.float32),
            jax.ShapeDtypeStruct((rows, width), jnp.float32),
            jax.ShapeDtypeStruct((rows, 1), jnp.float32),
        ],
        in_specs=[whole(width), across, down, whole(width), whole(1)],
        out_specs=[down, across, whole(width), whole(width), whole(1)],
        compiler_params=pltpu.CompilerParams(vmem_limit_bytes=48 * 2**20),
        cost_estimate=pl.CostEstimate(flops=12 * rows * width * ff, bytes_accessed=8 * width * ff, transcendentals=0),
        name="dense_branch",
    )(normed_two, up_full, down_full, upstream_low, mix)


MESH = pl.DeviceIdType.MESH


def plane():
    here = lax.axis_index("expert")
    core, x, y = here % 2, (here // 2) % 2, here // 4
    return here // 2, core, x, y, here + 1 - 2 * core, here + 2 - 4 * x, here + 4 - 8 * y


def greet(depth, others, count):
    level = lax.axis_index("dp")
    barrier = pltpu.get_barrier_semaphore()
    for other in others:
        pl.semaphore_signal(barrier, inc=1, device_id=(level, other), device_id_type=MESH)
    if count:
        for step in range(1, depth):
            pl.semaphore_signal(
                barrier,
                inc=1,
                device_id=((level + step) % depth, lax.axis_index("expert")),
                device_id_type=MESH,
            )
    pl.semaphore_wait(barrier, len(others) + (depth - 1 if count else 0))


def remote(source, target, sems, slot, level, where):
    return pltpu.make_async_remote_copy(
        src_ref=source,
        dst_ref=target,
        send_sem=sems[0].at[slot],
        recv_sem=sems[1].at[slot],
        device_id=(level, where),
        device_id_type=MESH,
    )


def gather_kernel(depth, count, more, *refs):
    shards, refs = refs[:count], refs[count:]
    if more:
        wide, picked, refs = refs[0], refs[1], refs[2:]
    fulls, refs = refs[:count], refs[count:]
    if more:
        parts, arrived, refs = refs[0], refs[1], refs[2:]
    keep, sems = refs[0], refs[1:]
    up_sems, x_sems, y_sems, d_sems, c_sems, w_sems, p_sems, low_sems = (sems[2 * i : 2 * i + 2] for i in range(8))
    z_sems = (up_sems, low_sems)
    level, here = lax.axis_index("dp"), lax.axis_index("expert")
    chip, core, x, y, twin, x_next, y_next = plane()
    x_chip, y_chip, far_chip = chip + 1 - 2 * x, chip + 2 - 4 * y, 3 - chip
    mates = [(here + step) % 8 for step in range(1, 8)] if more else (twin, x_next, y_next)
    greet(depth, mates, True)
    started, locals_ = [], []

    def send(*a):
        copy = remote(*a)
        copy.start()
        started.append(copy)

    def stay(source, target, slot):
        copy = pltpu.make_async_copy(source, target, keep.at[slot])
        copy.start()
        locals_.append(copy)

    def to_twin(i, step, chip_at, source=None):
        spot = fulls[i].at[(level + depth - step) % depth, chip_at, core]
        send(spot if source is None else source, spot, c_sems, (i, step, chip_at), level, twin)

    def along(i, hop, way, source):
        block = fulls[i].at[source, chip, core]
        target = (level + (1 if way == 0 else depth - 1)) % depth
        return remote(shards[i] if hop == 0 else block, block, z_sems[way], (i, hop), target, here)

    def ahead(way):
        return level < depth - 1 if way == 0 else level > 0

    def comes(hop, way):
        return level >= hop if way == 0 else level < depth - hop

    def back(hop, way):
        return (level + depth - hop) % depth if way == 0 else (level + hop) % depth

    def across(i, step, origin, begin):
        block = fulls[i].at[(level + depth - step) % depth, chip, core]
        copies = (
            remote(origin, block, x_sems, (i, step), level, x_next),
            remote(origin, block, y_sems, (i, step), level, y_next),
            remote(origin, block, c_sems, (i, step, chip), level, twin),
        )
        for copy in copies:
            if begin:
                copy.start()
            else:
                copy.wait_send()

    if more:
        for step in range(1, depth):
            for i in range(count):
                target = (level + step) % depth
                send(shards[i], fulls[i].at[level, chip, core], up_sems, (i, step), target, here)
    else:
        for way in range(2):

            @pl.when(ahead(way))
            def _(way=way):
                for i in range(count):
                    along(i, 0, way, level).start()

    for i in range(count):
        stay(shards[i], fulls[i].at[level, chip, core], i)
        across(i, 0, shards[i], True)
    if more:
        width = wide.shape[1] // depth

        def columns(at):
            return wide.at[:, pl.ds(pl.multiple_of(at * width, width), width)]

        for way in range(1, 8):
            mate = (here + way) % 8
            send(picked.at[mate], arrived.at[here], p_sems, (way,), level, mate)
        stay(picked.at[here], arrived.at[here], count + 1)
        for way in range(1, depth):
            target = (level + way) % depth
            send(columns(target), parts.at[level], w_sems, (way,), target, here)
        stay(columns(level), parts.at[level], count)
    for hop in range(1, depth):
        if more:
            for i in range(count):
                block = fulls[i].at[back(hop, 0), chip, core]
                remote(block, block, up_sems, (i, hop), level, here).wait_recv()
                across(i, hop, block, True)
            continue
        for way in range(2):

            @pl.when(comes(hop, way))
            def _(hop=hop, way=way):
                source = back(hop, way)
                for i in range(count):
                    block = fulls[i].at[source, chip, core]
                    remote(block, block, z_sems[way], (i, hop - 1), level, here).wait_recv()

                    @pl.when(ahead(way))
                    def _():
                        along(i, hop, way, source).start()

                    across(i, hop if way == 0 else depth - hop, block, True)

    for step in range(depth):
        source = (level + depth - step) % depth
        for i in range(count):
            x_spot, y_spot = fulls[i].at[source, x_chip, core], fulls[i].at[source, y_chip, core]
            remote(shards[i], x_spot, x_sems, (i, step), level, here).wait_recv()
            if step % 2 == 0:
                send(x_spot, x_spot, d_sems, (i, step), level, y_next)
            to_twin(i, step, x_chip)
            remote(shards[i], y_spot, y_sems, (i, step), level, here).wait_recv()
            if step % 2 == 1:
                send(y_spot, y_spot, d_sems, (i, step), level, x_next)
            to_twin(i, step, y_chip)
    for step in range(depth):
        source = (level + depth - step) % depth
        for i in range(count):
            spot = fulls[i].at[source, far_chip, core]
            remote(shards[i], spot, d_sems, (i, step), level, here).wait_recv()
            to_twin(i, step, far_chip)
    for step in range(depth):
        source = (level + depth - step) % depth
        for i in range(count):
            for chip_at in range(4):
                spot = fulls[i].at[source, chip_at, 1 - core]
                remote(shards[i], spot, c_sems, (i, step, chip_at), level, here).wait_recv()
    if more:
        for way in range(1, depth):
            spot = parts.at[(level + depth - way) % depth]
            remote(columns(level), spot, w_sems, (way,), level, here).wait_recv()
        for way in range(1, 8):
            spot = arrived.at[(here + 8 - way) % 8]
            remote(picked.at[here], spot, p_sems, (way,), level, here).wait_recv()
    for i in range(count):
        for step in range(depth):
            across(i, step, shards[i], False)
        for hop in () if more else range(depth):
            for way in range(2):

                @pl.when(comes(hop, way) & ahead(way))
                def _(i=i, hop=hop, way=way):
                    along(i, hop, way, back(hop, way)).wait_send()

    for copy in locals_:
        copy.wait()
    for copy in started:
        copy.wait_send()


def gather_plane(shards, ident, wide=None, picked=None):
    depth, count, more = lax.axis_size("dp"), len(shards), wide is not None
    if lax.axis_size("expert") != 8:
        fulls = [lax.all_gather(s, both, axis=0, tiled=True) for s in shards]
        if more:
            fulls.append(lax.all_to_all(wide, "dp", split_axis=1, concat_axis=0, tiled=True))
            fulls.append(lax.all_to_all(picked, "expert", split_axis=0, concat_axis=0, tiled=True))
        return fulls
    extra, extra_out = [], []
    if more:
        extra = [wide, picked]
        extra_out = [
            jax.ShapeDtypeStruct((depth, wide.shape[0], wide.shape[1] // depth), wide.dtype),
            jax.ShapeDtypeStruct(picked.shape, picked.dtype),
        ]
    kinds = []
    for shape in ((count, depth),) * 4 + ((count, depth, 4), (depth,), (8,), (count, depth)):
        kinds += [pltpu.SemaphoreType.DMA(shape)] * 2
    fulls = pl.pallas_call(
        functools.partial(gather_kernel, depth, count, more),
        out_shape=[jax.ShapeDtypeStruct((depth, 4, 2) + s.shape, s.dtype) for s in shards] + extra_out,
        in_specs=[pl.BlockSpec(memory_space=pl.ANY)] * (count + len(extra)),
        out_specs=[pl.BlockSpec(memory_space=pl.ANY)] * (count + len(extra)),
        scratch_shapes=[pltpu.SemaphoreType.DMA((count + 2,))] + kinds,
        compiler_params=pltpu.CompilerParams(collective_id=ident, has_side_effects=True),
        cost_estimate=pl.CostEstimate(flops=1, bytes_accessed=1, transcendentals=0),
        name=f"gather_plane_{ident}",
    )(*shards, *extra)
    full = [f.reshape((-1,) + s.shape[1:]) for f, s in zip(fulls, shards)]
    if more:
        full += [fulls[count].reshape((-1, extra_out[0].shape[2])), fulls[count + 1]]
    return full


def scatter_kernel(depth, count, with_z, work, *refs):
    grads, refs = refs[:count], refs[count:]
    if with_z:
        tall, summed, refs = refs[0], refs[1], refs[2:]
    if work:
        operands, refs = refs[:5], refs[5:]
    if with_z:
        outs, refs = refs[:count], refs[count:]
    else:
        packed, refs = refs[0], refs[1:]
        width = packed.shape[2]
        made_rows = operands[0].shape[0] // depth
        tops = [0]
        for grad in grads:
            tops.append(tops[-1] + grad.shape[3] * grad.shape[4] // width)
    if work:
        results, buffers, refs = (*refs[:2], packed), refs[-8:], refs[2:-8]
        staged, staged_sems, refs = refs[-2], refs[-1], refs[:-2]
    if with_z:
        parts, returned, keep, p_sems, w_sems = refs[0], refs[1], refs[-1], refs[-3:-1], refs[-5:-3]
        refs = refs[2:-5]
    own, twins, first, second = (refs[i * count : (i + 1) * count] for i in range(4))
    n = 4 * count
    levels = refs[n : n + count] if with_z else ()
    n += len(levels)
    load, c_sems, f_sems, s_sems = refs[n], refs[n + 1 : n + 3], refs[n + 3 : n + 5], refs[n + 5 : n + 7]
    z_sems = refs[n + 7 : n + 9]
    level, here = lax.axis_index("dp"), lax.axis_index("expert")
    chip, core, x, y, twin, x_next, y_next = plane()
    greet(depth, [(here + way) % 8 for way in range(1, 8)] if with_z else (twin, x_next, y_next), with_z)
    started, loads, flown = [], {}, []

    def send(*a):
        copy = remote(*a)
        copy.start()
        started.append(copy)

    if with_z:
        width = tall.shape[2]

        def columns(at):
            return parts.at[:, pl.ds(pl.multiple_of(at * width, width), width)]

        for way in range(1, depth):
            target = (level + way) % depth
            send(tall.at[target], columns(level), w_sems, (way,), target, here)
        kept = [
            pltpu.make_async_copy(tall.at[level], columns(level), keep.at[0]),
            pltpu.make_async_copy(summed.at[here], returned.at[here], keep.at[1]),
        ]
        for copy in kept:
            copy.start()
    order = [(step, (step + level + 1) % depth) for step in range(depth)]
    for step, at in order:
        for i in range(count):
            send(grads[i].at[at, :, 1 - core], twins[i].at[step], c_sems, (i, step), level, twin)
            loads[i, step] = pltpu.make_async_copy(grads[i].at[at, :, core], own[i].at[step], load.at[i, step])
            loads[i, step].start()
    if with_z:
        for way in range(1, 8):
            mate = (here + way) % 8
            send(summed.at[mate], returned.at[here], p_sems, (way,), level, mate)
    jobs = expert_work(operands, results, buffers) if work else iter(())

    def add(target, other):
        target[...] = (target[...].astype(jnp.float32) + other[...].astype(jnp.float32)).astype(jnp.bfloat16)

    def chips(step):
        if step % 2 == 0:
            return (1 - x, 3 - x), (x, 2 + x), x_next, y_next
        return (2 - 2 * y, 3 - 2 * y), (2 * y, 2 * y + 1), y_next, x_next

    for step, at in order:
        away, near, first_next, second_next = chips(step)
        for i in range(count):
            loads[i, step].wait()
            remote(own[i].at[step], twins[i].at[step], c_sems, (i, step), level, here).wait_recv()
            for side in range(2):
                add(own[i].at[step, away[side]], twins[i].at[step, away[side]])
                send(own[i].at[step, away[side]], first[i].at[step, side], f_sems, (i, step, side), level, first_next)
        for i in range(count):
            for side in range(2):
                add(own[i].at[step, near[side]], twins[i].at[step, near[side]])
    next(jobs, None)
    next(jobs, None)
    for step, at in order:
        away, near, first_next, second_next = chips(step)
        for i in range(count):
            for side in range(2):
                remote(own[i].at[step, 0], first[i].at[step, side], f_sems, (i, step, side), level, here).wait_recv()
                add(own[i].at[step, near[side]], first[i].at[step, side])
            across = chip + 2 - 4 * y if step % 2 == 0 else chip + 1 - 2 * x
            send(own[i].at[step, across], second[i].at[step], s_sems, (i, step), level, second_next)
        if step == 1:
            next(jobs, None)
    for _ in jobs:
        pass
    for step, at in order:
        for i in range(count):
            remote(own[i].at[step, 0], second[i].at[step], s_sems, (i, step), level, here).wait_recv()
            add(second[i].at[step], own[i].at[step, chip])
            if with_z:
                if step < depth - 1:
                    send(second[i].at[step], levels[i].at[step], z_sems, (i, step), at, here)
            else:
                sums = second[i][step]
                for piece in range(sums.shape[1] // width):
                    place = pl.ds(tops[i] + piece * sums.shape[0], sums.shape[0])
                    staged[step, place] = sums[:, piece * width : (piece + 1) * width]
        if not with_z:
            copy = pltpu.make_async_copy(staged.at[step], packed.at[at, made_rows:], staged_sems.at[step])
            copy.start()
            flown.append(copy)
    for copy in flown:
        copy.wait()
    if with_z:
        for i in range(count):
            total = second[i][depth - 1].astype(jnp.float32)
            for step in range(depth - 1):
                remote(second[i].at[step], levels[i].at[step], z_sems, (i, step), level, here).wait_recv()
                total = total + levels[i][step].astype(jnp.float32)
            outs[i][...] = total
        for way in range(1, depth):
            spot = columns((level + depth - way) % depth)
            remote(tall.at[level], spot, w_sems, (way,), level, here).wait_recv()
        for way in range(1, 8):
            spot = returned.at[(here + 8 - way) % 8]
            remote(spot, spot, p_sems, (way,), level, here).wait_recv()
        for copy in kept:
            copy.wait()
    for copy in started:
        copy.wait_send()


def expert_work(operands, results, buffers):
    act, grads, rows_in, pre_grad, down = operands
    act_at, grads_at, rows_at, pre_at, down_at, tall, low, sems = buffers
    pairs = ((act, act_at), (grads, grads_at), (down, down_at), (rows_in, rows_at), (pre_grad, pre_at))
    copies = [pltpu.make_async_copy(a, b, sems.at[i]) for i, (a, b) in enumerate(pairs)]
    for copy in copies:
        copy.start()
    width = act.shape[1]
    tile = tall.shape[1]
    height = low.shape[1]
    flights = []

    def put(slot, stage, target, sem):
        copy = pltpu.make_async_copy(stage.at[slot], target, sems.at[sem + slot])
        copy.start()
        flights.append(copy)

    def settle(keep):
        while len(flights) > keep:
            flights.pop(0).wait()

    copies[0].wait()
    copies[1].wait()
    for i in range(width // tile):
        settle(1)
        tall[i % 2] = matmul_tn(act_at[:, i * tile : (i + 1) * tile], grads_at[...])
        put(i % 2, tall, results[0].at[i * tile : (i + 1) * tile], 5)
    yield
    copies[2].wait()
    settle(0)
    for i in range(results[2].shape[0]):
        settle(1)
        low[i % 2] = matmul(act_at[i * height : (i + 1) * height, :], down_at[...]).astype(jnp.bfloat16)
        put(i % 2, low, results[2].at[i, 0:height], 7)
    yield
    settle(0)
    copies[3].wait()
    copies[4].wait()
    for i in range(width // tile):
        settle(1)
        low[i % 2, 0:tile] = matmul_tn(rows_at[:, i * tile : (i + 1) * tile], pre_at[...]).astype(jnp.bfloat16)
        copy = pltpu.make_async_copy(low.at[i % 2, 0:tile], results[1].at[i * tile : (i + 1) * tile], sems.at[7 + i % 2])
        copy.start()
        flights.append(copy)
    yield
    settle(0)


def scatter_plane(grads, ident, work=None, tall=None, summed=None):
    depth, count, with_z = lax.axis_size("dp"), len(grads), tall is not None
    low = jnp.bfloat16
    if lax.axis_size("expert") != 8:
        sums = [lax.psum_scatter(g, both, scatter_dimension=0, tiled=True).astype(jnp.float32) for g in grads]
        if work is not None:
            act, grad_rows, rows_in, pre_grad, down = work
            sums.append(matmul(act, down).astype(low))
            sums.append(matmul_tn(act, grad_rows))
            sums.append(matmul_tn(rows_in, pre_grad).astype(low))
        if with_z:
            sums.append(lax.all_to_all(tall, "dp", split_axis=0, concat_axis=1, tiled=True))
            sums.append(lax.all_to_all(summed, "expert", split_axis=0, concat_axis=0, tiled=True))
        return sums
    grads = [g.reshape((depth, 4, 2, g.shape[0] // (8 * depth)) + g.shape[1:]) for g in grads]
    blocks = [g.shape[3:] for g in grads]
    width = min(b[1] for b in blocks)
    sums = [jax.ShapeDtypeStruct(b, jnp.float32) for b in blocks]
    if not with_z:
        sums = [jax.ShapeDtypeStruct((depth, sum(b[0] * b[1] for b in blocks) // width, width), low)]
    scratch = [pltpu.VMEM((depth, 4) + b, low) for b in blocks] * 2
    scratch += [pltpu.VMEM((depth, 2) + b, low) for b in blocks]
    scratch += [pltpu.VMEM((depth,) + b, low) for b in blocks]
    if with_z:
        scratch += [pltpu.VMEM((depth - 1,) + b, low) for b in blocks]
    sems = [pltpu.SemaphoreType.DMA((count, depth))] * 3 + [pltpu.SemaphoreType.DMA((count, depth, 2))] * 2
    sems += [pltpu.SemaphoreType.DMA((count, depth))] * 2
    operands, made = (), []
    if with_z:
        sems += [pltpu.SemaphoreType.DMA((count, depth))] * 2
        sems += [pltpu.SemaphoreType.DMA((depth,))] * 2
        sems += [pltpu.SemaphoreType.DMA((8,))] * 2 + [pltpu.SemaphoreType.DMA((2,))]
        operands = (tall.reshape((depth, -1, tall.shape[1])), summed)
        made = [
            jax.ShapeDtypeStruct((tall.shape[0] // depth, tall.shape[1] * depth), tall.dtype),
            jax.ShapeDtypeStruct(summed.shape, summed.dtype),
        ]
    if work is not None:
        operands = tuple(work)
        act, down = work[0], work[4]
        made = [
            jax.ShapeDtypeStruct((act.shape[1], act.shape[1]), jnp.float32),
            jax.ShapeDtypeStruct((act.shape[1], work[3].shape[1]), low),
        ]
        sems += [pltpu.VMEM((depth,) + sums[0].shape[1:], low), pltpu.SemaphoreType.DMA((depth,))]
        sums = [jax.ShapeDtypeStruct((depth, act.shape[0] // depth + sums[0].shape[1], width), low)]
        sems += [pltpu.VMEM(o.shape, o.dtype) for o in operands]
        sems += [
            pltpu.VMEM((2, 256, down.shape[1]), jnp.float32),
            pltpu.VMEM((2, act.shape[0] // depth, down.shape[1]), low),
            pltpu.SemaphoreType.DMA((9,)),
        ]
    return list(
        pl.pallas_call(
            functools.partial(scatter_kernel, depth, count, with_z, work is not None),
            out_shape=sums + made,
            in_specs=[pl.BlockSpec(memory_space=pl.ANY)] * (count + len(operands)),
            out_specs=[pl.BlockSpec(memory_space=pltpu.VMEM if with_z else pl.ANY)] * len(sums) + [pl.BlockSpec(memory_space=pl.ANY)] * len(made),
            scratch_shapes=scratch + sems,
            compiler_params=pltpu.CompilerParams(
                collective_id=ident, has_side_effects=True, vmem_limit_bytes=(32 if with_z else 58) * 2**20
            ),
            cost_estimate=pl.CostEstimate(flops=1, bytes_accessed=200 * 2**20, transcendentals=0),
            name=f"scatter_plane_{ident}",
        )(*grads, *operands)
    )


def finish_scatter(packed, shapes):
    packed = lax.psum_scatter(packed, "dp", scatter_dimension=0)
    width = packed.shape[1]
    top = packed.shape[0] - sum(rows * columns for rows, columns in shapes) // width
    outs = [packed[:top]]
    for rows, columns in shapes:
        pieces = columns // width
        blocks = [packed[top + i * rows : top + (i + 1) * rows].astype(jnp.float32) for i in range(pieces)]
        outs.append(jnp.concatenate(blocks, axis=1))
        top += pieces * rows
    return outs


def body(
    tokens,
    seq_lengths,
    routes,
    w_qkv,
    w_out,
    w_up,
    w_down,
    gain_attn,
    gain_mlp,
    w_mix,
    expert_up,
    expert_down,
    cotangent,
):
    tok_rows, model_width = tokens.shape
    axis_dp, axis_experts = lax.axis_size("dp"), lax.axis_size("expert")
    expert_total = axis_experts * expert_up.shape[0]
    capacity = max(2, 5 * tok_rows // (4 * expert_total))
    slots = expert_total * capacity
    ff_expert = expert_up.shape[2]

    small = jnp.concatenate([gain_attn[:, None], gain_mlp[:, None], w_mix], axis=1)
    small = jnp.pad(small, ((0, 0), (0, 128 - small.shape[1])))
    length = seq_lengths[0]
    valid_rows = jnp.arange(tok_rows, dtype=jnp.int32) < length

    route_ids = routes[:, 0]
    expert_ids = jnp.arange(expert_total, dtype=jnp.int32)
    route_hits = (route_ids[:, None] == expert_ids[None, :]) & valid_rows[:, None]
    route_ranks = jnp.cumsum(route_hits.astype(jnp.int32), axis=0) - 1
    chosen = jnp.sum(jnp.where(route_hits, route_ranks, 0), axis=1)
    kept_rows = valid_rows & (chosen < capacity)
    slot_ids = route_ids * capacity + chosen
    slot_table = (
        (jnp.arange(slots, dtype=jnp.int32)[:, None] == slot_ids[None, :]) & kept_rows[None, :]
    ).astype(jnp.bfloat16)

    def pick(rows):
        return matmul(slot_table, rows).astype(jnp.bfloat16).reshape(expert_total, capacity, model_width)

    def dispatch(rows):
        arrived = lax.all_to_all(pick(rows), "expert", split_axis=0, concat_axis=0, tiled=True)
        return arrived.reshape(slots, model_width)

    def spread(rows):
        return lax.all_gather(rows, "dp", axis=0, tiled=True)

    def unspread(rows):
        return lax.psum_scatter(rows, "dp", scatter_dimension=0, tiled=True)

    def give_back(summed):
        summed = summed.reshape(expert_total, capacity, model_width)
        back = lax.all_to_all(summed, "expert", split_axis=0, concat_axis=0, tiled=True)
        return matmul_tn(slot_table, back.reshape(slots, model_width))

    down_part = expert_down[0]

    upstream_low = jnp.where(valid_rows[:, None], cotangent, jnp.zeros_like(cotangent))
    upstream = upstream_low.astype(jnp.float32)
    qkv_full, out_full, small_full, up_part, pulled_here = gather_plane(
        [w_qkv, w_out, small], 0, expert_up[0], pick(upstream_low)
    )
    pulled_rows = spread(pulled_here.reshape(slots, model_width))
    gain_one = small_full[:, 0].astype(jnp.float32)
    gain_two = small_full[:, 1].astype(jnp.float32)
    mix_full = small_full[:, 2:4]
    mix_lean = (mix_full[:, 0] - mix_full[:, 1].astype(jnp.float32)).astype(jnp.float32)

    inputs = tokens.astype(jnp.float32)
    scaled_one, inverse_one = norm_forward(inputs)
    normed_one = (scaled_one * gain_one).astype(jnp.bfloat16)
    joined = matmul(normed_one, qkv_full).astype(jnp.bfloat16)
    heads_out, log_total = attention_forward(joined, seq_lengths)
    after_attn = inputs + matmul(heads_out, out_full)
    scaled_two, inverse_two = norm_forward(after_attn)
    normed_two = (scaled_two * gain_two).astype(jnp.bfloat16)

    rows_here = dispatch(normed_two)
    rows_here, w_up, w_down = lax.optimization_barrier((rows_here, w_up, w_down))
    rows_in = spread(rows_here)
    up_full, down_full = gather_plane([w_up, w_down], 1)

    pulled_rows, up_full, down_full = lax.optimization_barrier((pulled_rows, up_full, down_full))
    mix_weights = jax.nn.softmax(matmul(normed_two, mix_full), axis=-1)
    grad_down, grad_up, normed_grad, dense_out, pull_dense = dense_branch(
        normed_two, up_full, down_full, upstream_low, mix_weights[:, 0:1]
    )
    lean_dense = mix_weights[:, 0:1] * mix_weights[:, 1:2] * pull_dense
    normed_grad = normed_grad + lean_dense * mix_lean[None, :]

    rows_in, grad_up, grad_down, normed_grad = lax.optimization_barrier((rows_in, grad_up, grad_down, normed_grad))
    act_rows, pre_grad, grad_rows, input_grad, lean_rows = expert_branch(
        rows_in, pulled_rows, up_part, down_part, small_full, mix_lean[None, :]
    )
    in_grad_here = unspread(input_grad)
    *sums, grad_expert_down, grad_expert_up = scatter_plane(
        [grad_up, grad_down], 2, (act_rows, grad_rows, rows_in, pre_grad, down_part)
    )
    grad_expert_down = grad_expert_down[None]
    in_grad_here, *sums = lax.optimization_barrier((in_grad_here, *sums))
    if len(sums) == 1:
        outs_here, grad_up, grad_down = finish_scatter(sums[0], (w_up.shape, w_down.shape))
    else:
        grad_up, grad_down, outs_here = sums[0], sums[1], unspread(sums[2])
    in_grad_back = give_back(in_grad_here)

    normed_grad = normed_grad + in_grad_back
    lean_grad = jnp.sum(normed_two.astype(jnp.float32) * lean_dense, axis=0) - lean_rows[0]
    mlp_in_grad, grad_gain_two = norm_backward(normed_grad, scaled_two, inverse_two, gain_two)
    resid_grad = upstream + mlp_in_grad
    attn_grad = resid_grad.astype(jnp.bfloat16)
    grad_out = matmul_tn(heads_out, attn_grad)
    heads_grad = matmul_nt(attn_grad, out_full).astype(jnp.bfloat16)
    joined_grad = jnp.concatenate(
        attention_backward(joined, heads_grad, heads_out, log_total, seq_lengths), axis=1
    )
    grad_qkv = matmul_tn(normed_one, joined_grad)
    normed_one_grad = matmul_nt(joined_grad, qkv_full)
    attn_in_grad, grad_gain_one = norm_backward(normed_one_grad, scaled_one, inverse_one, gain_one)
    grad_inputs = resid_grad + attn_in_grad

    small_grads = jnp.stack([grad_gain_one, grad_gain_two, lean_grad, -lean_grad], axis=1)
    small_grads = jnp.pad(small_grads, ((0, 0), (0, 128 - small_grads.shape[1])))
    small_grads = small_grads.astype(jnp.bfloat16)
    grad_qkv, grad_out, small_grads, grad_expert_up, returned = scatter_plane(
        [grad_qkv.astype(jnp.bfloat16), grad_out.astype(jnp.bfloat16), small_grads],
        3,
        tall=grad_expert_up,
        summed=outs_here.reshape(expert_total, capacity, model_width),
    )
    expert_out = matmul_tn(slot_table, returned.reshape(slots, model_width))
    result = after_attn + mix_weights[:, 0:1] * dense_out + mix_weights[:, 1:2] * expert_out
    grad_expert_up = grad_expert_up.astype(jnp.float32)[None]
    return (
        result,
        grad_inputs,
        grad_qkv,
        grad_out,
        grad_up,
        grad_down,
        small_grads[:, 0],
        small_grads[:, 1],
        small_grads[:, 2:4],
        grad_expert_up,
        grad_expert_down,
    )


def solution(mesh):
    rows, vector = P(both, None), P(both)
    experts = P("expert", "dp", None)
    return jax.shard_map(
        body,
        mesh=mesh,
        in_specs=(rows, vector, rows, rows, rows, rows, rows, vector, vector, rows, experts, experts, rows),
        out_specs=(rows, rows, rows, rows, rows, rows, vector, vector, rows, experts, experts),
        check_vma=False,
    )
```

```python
import functools

import jax
import jax.numpy as jnp
from jax import lax
from jax.experimental import pallas as pl
from jax.experimental.pallas import tpu as pltpu
from jax.sharding import PartitionSpec as P

HEADS = 16

epsilon = 1e-05
root_half = 0.7071067811865476
inv_root_two_pi = 0.3989422804014327
highest = lax.Precision.HIGHEST
both = ("dp", "expert")


def gelu_pair(values):
    half = 0.5 * (1.0 + lax.erf(values * root_half))
    return values * half, half + values * jnp.exp(-0.5 * values * values) * inv_root_two_pi


def dot(left, right, dims):
    return lax.dot_general(left, right, (dims, ((), ())), preferred_element_type=jnp.float32)


def matmul(left, right):
    return dot(left, right, ((1,), (0,)))


def matmul_nt(left, right):
    return dot(left, right, ((1,), (1,)))


def matmul_tn(left, right):
    return dot(left, right, ((0,), (0,)))


def norm_forward(values):
    row_mean = jnp.mean(values, axis=-1, keepdims=True)
    centred = values - row_mean
    row_var = jnp.mean(centred * centred, axis=-1, keepdims=True)
    inverse = lax.rsqrt(row_var + epsilon)
    return (centred * inverse, inverse)


def norm_backward(upstream, scaled, inverse, gain_row):
    gain_grad = jnp.sum(upstream * scaled, axis=0)
    inner = upstream * gain_row
    centred_grad = (
        inner
        - jnp.mean(inner, axis=-1, keepdims=True)
        - scaled * jnp.mean(inner * scaled, axis=-1, keepdims=True)
    )
    return (inverse * centred_grad, gain_grad)


def head_scores(queries, keys_all, length, row_start, scale):
    scores = matmul_nt(queries, keys_all) * scale
    rows_at = row_start + lax.broadcasted_iota(jnp.int32, scores.shape, 0)
    cols_at = lax.broadcasted_iota(jnp.int32, scores.shape, 1)
    return jnp.where((cols_at <= rows_at) & (cols_at < length), scores, -1000000000.0)


def attention_forward_kernel(head_width, bands, length_ref, q_ref, k_ref, v_ref, out_ref, log_ref):
    length = length_ref[0]
    scale = head_width ** (-0.5)
    tok_rows, lanes = q_ref.shape
    height = tok_rows // bands
    lane = lax.broadcasted_iota(jnp.int32, (1, lanes), 1) // head_width
    for band in range(bands):
        top, end = band * height, (band + 1) * height
        keys_all, values_all = k_ref[0:end, :], v_ref[0:end, :]
        queries = q_ref[top:end, :]
        mixed = jnp.zeros((height, lanes), jnp.float32)
        logs = []
        for head in range(lanes // head_width):
            mine = lane == head
            scores = head_scores(jnp.where(mine, queries, 0), keys_all, length, top, scale)
            top_score = jnp.max(scores, axis=-1, keepdims=True)
            raised = jnp.exp(scores - top_score)
            row_total = jnp.sum(raised, axis=-1, keepdims=True)
            probs = (raised / row_total).astype(jnp.bfloat16)
            mixed = mixed + matmul(probs, jnp.where(mine, values_all, 0))
            logs.append(top_score + jnp.log(row_total))
        out_ref[top:end, :] = mixed.astype(jnp.bfloat16)
        spread = jnp.broadcast_to(logs[0], (height, lanes))
        for head in range(1, len(logs)):
            spread = jnp.where(lane == head, logs[head], spread)
        log_ref[top:end, :] = spread


def attention_forward(joined, length):
    tok_rows, width = joined.shape[0], joined.shape[1] // 3
    head_width = width // HEADS
    lanes = max(128, head_width)
    tiles = width // lanes
    bands = 2

    def part(which):
        return pl.BlockSpec((tok_rows, lanes), lambda i: (0, which * tiles + i))

    return pl.pallas_call(
        functools.partial(attention_forward_kernel, head_width, bands),
        grid=(tiles,),
        out_shape=[
            jax.ShapeDtypeStruct((tok_rows, width), jnp.bfloat16),
            jax.ShapeDtypeStruct((tok_rows, width), jnp.float32),
        ],
        in_specs=[pl.BlockSpec(memory_space=pltpu.SMEM), part(0), part(1), part(2)],
        out_specs=[part(0), part(0)],
        compiler_params=pltpu.CompilerParams(vmem_limit_bytes=32 * 2**20),
        cost_estimate=pl.CostEstimate(flops=4 * tok_rows * tok_rows * width, bytes_accessed=10 * tok_rows * width, transcendentals=0),
        name="attention_forward",
    )(length, joined, joined, joined)


def attention_backward_kernel(head_width, bands, length_ref, q_ref, k_ref, v_ref, g_ref, o_ref, log_ref, dq_ref, dk_ref, dv_ref, dk_sum, dv_sum):
    length = length_ref[0]
    scale = head_width ** (-0.5)
    tok_rows, lanes = q_ref.shape
    height = tok_rows // bands
    lane = lax.broadcasted_iota(jnp.int32, (1, lanes), 1) // head_width
    for band in range(bands):
        top, end = band * height, (band + 1) * height
        keys_all, values_all = k_ref[0:end, :], v_ref[0:end, :]
        queries, grads = q_ref[top:end, :], g_ref[top:end, :]
        turned = lax.transpose(log_ref[top:end, :], (1, 0))
        products = lax.transpose(grads.astype(jnp.float32) * o_ref[top:end, :].astype(jnp.float32), (1, 0))
        dq = jnp.zeros((height, lanes), jnp.float32)
        dk = jnp.zeros((end, lanes), jnp.float32)
        dv = jnp.zeros((end, lanes), jnp.float32)
        keys_at = lax.broadcasted_iota(jnp.int32, (end, height), 0)
        rows_at = top + lax.broadcasted_iota(jnp.int32, (end, height), 1)
        allowed = (keys_at <= rows_at) & (keys_at < length)
        for head in range(lanes // head_width):
            mine = lane == head
            own_q, own_g = jnp.where(mine, queries, 0), jnp.where(mine, grads, 0)
            log_total = turned[head * head_width : head * head_width + 1, :]
            delta = jnp.sum(products[head * head_width : (head + 1) * head_width, :], axis=0, keepdims=True)
            scores = jnp.where(allowed, matmul_nt(keys_all, own_q) * scale, -1000000000.0)
            probs = jnp.exp(scores - log_total)
            prob_grad = matmul_nt(values_all, own_g)
            score_grad = (probs * (prob_grad - delta)).astype(jnp.bfloat16)
            dv = dv + matmul(probs.astype(jnp.bfloat16), own_g)
            dk = dk + matmul(score_grad, own_q)
            dq = dq + matmul_tn(score_grad, jnp.where(mine, keys_all, 0))
        dq_ref[top:end, :] = (dq * scale).astype(jnp.bfloat16)
        if band == 0:
            dk_sum[...] = jnp.zeros_like(dk_sum)
            dv_sum[...] = jnp.zeros_like(dv_sum)
        dk_sum[0:end, :] += dk
        dv_sum[0:end, :] += dv
    dk_ref[...] = (dk_sum[...] * scale).astype(jnp.bfloat16)
    dv_ref[...] = dv_sum[...].astype(jnp.bfloat16)


def attention_backward(joined, heads_grad, heads_out, log_total, length):
    tok_rows, width = joined.shape[0], joined.shape[1] // 3
    head_width = width // HEADS
    lanes = max(128, head_width)
    tiles = width // lanes
    bands = 2

    def part(which):
        return pl.BlockSpec((tok_rows, lanes), lambda i: (0, which * tiles + i))

    return pl.pallas_call(
        functools.partial(attention_backward_kernel, head_width, bands),
        grid=(tiles,),
        out_shape=[jax.ShapeDtypeStruct((tok_rows, width), jnp.bfloat16)] * 3,
        in_specs=[pl.BlockSpec(memory_space=pltpu.SMEM), part(0), part(1), part(2), part(0), part(0), part(0)],
        out_specs=[part(0)] * 3,
        scratch_shapes=[pltpu.VMEM((tok_rows, lanes), jnp.float32)] * 2,
        compiler_params=pltpu.CompilerParams(vmem_limit_bytes=32 * 2**20),
        cost_estimate=pl.CostEstimate(flops=10 * tok_rows * tok_rows * width, bytes_accessed=20 * tok_rows * width, transcendentals=0),
        name="attention_backward",
    )(length, joined, joined, joined, heads_grad, heads_out, log_total)


def expert_kernel(rows_ref, pull_ref, up_ref, small_ref, lean_ref, act_ref, pre_ref, mix_ref, in_ref, sum_ref):
    low = jnp.bfloat16
    chains = [slice(top, top + 256) for top in range(0, rows_ref.shape[0], 256)]
    pre_acts = [matmul(rows_ref[rows, :], up_ref[...]) for rows in chains]
    all_logits = [matmul(rows_ref[rows, :], small_ref[...]) for rows in chains]
    parts = []
    for rows, pre_act, logits in zip(chains, pre_acts, all_logits):
        first, second = logits[:, 2:3], logits[:, 3:4]
        top = jnp.maximum(first, second)
        first, second = jnp.exp(first - top), jnp.exp(second - top)
        mix_dense, mix_expert = first / (first + second), second / (first + second)
        act_pull = pull_ref[rows, :]
        gelu, slope = gelu_pair(pre_act)
        act = gelu.astype(low)
        act_ref[rows, :] = act
        lean = mix_dense * mix_expert * jnp.sum(act.astype(jnp.float32) * act_pull, axis=1, keepdims=True)
        pre_grad = (mix_expert * act_pull * slope).astype(low)
        pre_ref[rows, :] = pre_grad
        in_ref[rows, :] = (matmul_nt(pre_grad, up_ref[...]) - lean * lean_ref[...]).astype(low)
        mix_ref[rows, :] = mix_expert
        parts.append(jnp.sum(rows_ref[rows, :].astype(jnp.float32) * lean, axis=0, keepdims=True))
    part = sum(parts[1:], parts[0])
    sum_ref[...] = jnp.where(pl.program_id(0) == 0, part, sum_ref[...] + part)


def expert_branch(rows_in, act_pull, up_part, small_full, mix_lean):
    count, width = rows_in.shape
    hidden = up_part.shape[1]
    height = 512

    def tall(columns):
        return pl.BlockSpec((height, columns), lambda i: (i, 0))

    def whole(array):
        return pl.BlockSpec(array.shape, lambda i: (0, 0))

    low = jnp.bfloat16
    return pl.pallas_call(
        expert_kernel,
        grid=(count // height,),
        out_shape=[
            jax.ShapeDtypeStruct((count, hidden), low),
            jax.ShapeDtypeStruct((count, hidden), low),
            jax.ShapeDtypeStruct((count, 1), jnp.float32),
            jax.ShapeDtypeStruct((count, width), low),
            jax.ShapeDtypeStruct((1, width), jnp.float32),
        ],
        in_specs=[tall(width), tall(hidden), whole(up_part), whole(small_full), whole(mix_lean)],
        out_specs=[tall(hidden), tall(hidden), tall(1), tall(width), whole(mix_lean)],
        compiler_params=pltpu.CompilerParams(vmem_limit_bytes=58 * 2**20),
        cost_estimate=pl.CostEstimate(
            flops=4 * count * width * hidden, bytes_accessed=16 * count * width, transcendentals=0
        ),
        name="expert_branch",
    )(rows_in, act_pull, up_part, small_full, mix_lean)


def dense_kernel(normed_ref, up_ref, down_ref, grad_ref, mix_ref, gdown_ref, gup_ref, ngrad_ref, out_ref, pull_ref):
    normed, upstream, mix = normed_ref[...], grad_ref[...], mix_ref[...]
    hidden = matmul(normed, up_ref[...])
    dense_pull = matmul_nt(upstream, down_ref[...])
    gelu, slope = gelu_pair(hidden)
    act = gelu.astype(jnp.bfloat16)
    pull = jnp.sum(act.astype(jnp.float32) * dense_pull, axis=1, keepdims=True)
    hidden_grad = (mix * dense_pull * slope).astype(jnp.bfloat16)
    grad_out = (upstream.astype(jnp.float32) * mix).astype(jnp.bfloat16)
    gdown_ref[...] = matmul_tn(act, grad_out).astype(jnp.bfloat16)
    gup_ref[...] = matmul_tn(normed, hidden_grad).astype(jnp.bfloat16)
    ngrad = matmul_nt(hidden_grad, up_ref[...])
    dense_out = matmul(act, down_ref[...])

    @pl.when(pl.program_id(0) == 0)
    def _():
        ngrad_ref[...] = ngrad
        out_ref[...] = dense_out
        pull_ref[...] = pull

    @pl.when(pl.program_id(0) > 0)
    def _():
        ngrad_ref[...] += ngrad
        out_ref[...] += dense_out
        pull_ref[...] += pull


def dense_branch(normed_two, up_full, down_full, upstream_low, mix):
    rows, width = normed_two.shape
    ff = up_full.shape[1]
    block = 512

    def whole(columns):
        return pl.BlockSpec((rows, columns), lambda i: (0, 0))

    across, down = pl.BlockSpec((width, block), lambda i: (0, i)), pl.BlockSpec((block, width), lambda i: (i, 0))
    return pl.pallas_call(
        dense_kernel,
        grid=(ff // block,),
        out_shape=[
            jax.ShapeDtypeStruct((ff, width), jnp.bfloat16),
            jax.ShapeDtypeStruct((width, ff), jnp.bfloat16),
            jax.ShapeDtypeStruct((rows, width), jnp.float32),
            jax.ShapeDtypeStruct((rows, width), jnp.float32),
            jax.ShapeDtypeStruct((rows, 1), jnp.float32),
        ],
        in_specs=[whole(width), across, down, whole(width), whole(1)],
        out_specs=[down, across, whole(width), whole(width), whole(1)],
        compiler_params=pltpu.CompilerParams(vmem_limit_bytes=48 * 2**20),
        cost_estimate=pl.CostEstimate(flops=12 * rows * width * ff, bytes_accessed=8 * width * ff, transcendentals=0),
        name="dense_branch",
    )(normed_two, up_full, down_full, upstream_low, mix)


MESH = pl.DeviceIdType.MESH


def plane():
    here = lax.axis_index("expert")
    core, x, y = here % 2, (here // 2) % 2, here // 4
    return here // 2, core, x, y, here + 1 - 2 * core, here + 2 - 4 * x, here + 4 - 8 * y


def greet(depth, others, count):
    level = lax.axis_index("dp")
    barrier = pltpu.get_barrier_semaphore()
    for other in others:
        pl.semaphore_signal(barrier, inc=1, device_id=(level, other), device_id_type=MESH)
    if count:
        for step in range(1, depth):
            pl.semaphore_signal(
                barrier,
                inc=1,
                device_id=((level + step) % depth, lax.axis_index("expert")),
                device_id_type=MESH,
            )
    pl.semaphore_wait(barrier, len(others) + (depth - 1 if count else 0))


def remote(source, target, sems, slot, level, where):
    return pltpu.make_async_remote_copy(
        src_ref=source,
        dst_ref=target,
        send_sem=sems[0].at[slot],
        recv_sem=sems[1].at[slot],
        device_id=(level, where),
        device_id_type=MESH,
    )


def slot_shape(tok_rows):
    experts = lax.axis_size("expert")
    return (experts, max(2, 5 * tok_rows // (4 * experts)))


def slots_of(routes, length, tok_rows):
    experts, capacity = slot_shape(tok_rows)
    rows_at = lax.broadcasted_iota(jnp.int32, (tok_rows, 1), 0)
    hits = (routes == lax.broadcasted_iota(jnp.int32, (tok_rows, experts), 1)) & (rows_at < length)
    hits = hits.astype(jnp.float32)
    ahead = lax.broadcasted_iota(jnp.int32, (tok_rows, tok_rows), 1) < lax.broadcasted_iota(jnp.int32, (tok_rows, tok_rows), 0)
    ranks = matmul(ahead.astype(jnp.bfloat16), hits.astype(jnp.bfloat16))
    rank = jnp.sum(hits * ranks, axis=1, keepdims=True)
    kept = (rows_at < length) & (rank < capacity)
    slot = routes * capacity + rank.astype(jnp.int32)
    slots_at = lax.broadcasted_iota(jnp.int32, (tok_rows, experts * capacity), 1)
    return ((slots_at == slot) & kept).astype(jnp.bfloat16)


def pick_rows(rows, routes, length, picked):
    experts, capacity, _ = picked.shape
    table = slots_of(routes[...], length[0], rows.shape[0])
    chosen = matmul_tn(table, rows[...]).astype(jnp.bfloat16)
    for expert in range(experts):
        picked[expert] = chosen[expert * capacity : (expert + 1) * capacity]


def gather_kernel(depth, count, more, *refs):
    shards, refs = refs[:count], refs[count:]
    if more:
        wide, rows, routes, length, refs = refs[0], refs[1], refs[2], refs[3], refs[4:]
    fulls, refs = refs[:count], refs[count:]
    if more:
        parts, arrived, picked, refs = refs[0], refs[1], refs[-1], refs[2:-1]
    keep, sems = refs[0], refs[1:]
    up_sems, x_sems, y_sems, d_sems, c_sems, w_sems, p_sems, low_sems = (sems[2 * i : 2 * i + 2] for i in range(8))
    z_sems = (up_sems, low_sems)
    level, here = lax.axis_index("dp"), lax.axis_index("expert")
    chip, core, x, y, twin, x_next, y_next = plane()
    x_chip, y_chip, far_chip = chip + 1 - 2 * x, chip + 2 - 4 * y, 3 - chip
    mates = [(here + step) % 8 for step in range(1, 8)] if more else (twin, x_next, y_next)
    greet(depth, mates, True)
    started, locals_ = [], []

    def send(*a):
        copy = remote(*a)
        copy.start()
        started.append(copy)

    def stay(source, target, slot):
        copy = pltpu.make_async_copy(source, target, keep.at[slot])
        copy.start()
        locals_.append(copy)

    def to_twin(i, step, chip_at, source=None):
        spot = fulls[i].at[(level + depth - step) % depth, chip_at, core]
        send(spot if source is None else source, spot, c_sems, (i, step, chip_at), level, twin)

    def along(i, hop, way, source):
        block = fulls[i].at[source, chip, core]
        target = (level + (1 if way == 0 else depth - 1)) % depth
        return remote(shards[i] if hop == 0 else block, block, z_sems[way], (i, hop), target, here)

    def ahead(way):
        return level < depth - 1 if way == 0 else level > 0

    def comes(hop, way):
        return level >= hop if way == 0 else level < depth - hop

    def back(hop, way):
        return (level + depth - hop) % depth if way == 0 else (level + hop) % depth

    def across(i, step, origin, begin):
        block = fulls[i].at[(level + depth - step) % depth, chip, core]
        copies = (
            remote(origin, block, x_sems, (i, step), level, x_next),
            remote(origin, block, y_sems, (i, step), level, y_next),
            remote(origin, block, c_sems, (i, step, chip), level, twin),
        )
        for copy in copies:
            if begin:
                copy.start()
            else:
                copy.wait_send()

    if more:
        for step in range(1, depth):
            for i in range(count):
                target = (level + step) % depth
                send(shards[i], fulls[i].at[level, chip, core], up_sems, (i, step), target, here)
    else:
        for way in range(2):

            @pl.when(ahead(way))
            def _(way=way):
                for i in range(count):
                    along(i, 0, way, level).start()

    for i in range(count):
        stay(shards[i], fulls[i].at[level, chip, core], i)
        across(i, 0, shards[i], True)
    if more:
        width = wide.shape[1] // depth

        def columns(at):
            return wide.at[:, pl.ds(pl.multiple_of(at * width, width), width)]

        for way in range(1, depth):
            target = (level + way) % depth
            send(columns(target), parts.at[level], w_sems, (way,), target, here)
        stay(columns(level), parts.at[level], count)
        pick_rows(rows, routes, length, picked)
        for way in range(1, 8):
            mate = (here + way) % 8
            send(picked.at[mate], arrived.at[here], p_sems, (way,), level, mate)
        stay(picked.at[here], arrived.at[here], count + 1)
    for hop in range(1, depth):
        if more:
            for i in range(count):
                block = fulls[i].at[back(hop, 0), chip, core]
                remote(block, block, up_sems, (i, hop), level, here).wait_recv()
                across(i, hop, block, True)
            continue
        for way in range(2):

            @pl.when(comes(hop, way))
            def _(hop=hop, way=way):
                source = back(hop, way)
                for i in range(count):
                    block = fulls[i].at[source, chip, core]
                    remote(block, block, z_sems[way], (i, hop - 1), level, here).wait_recv()

                    @pl.when(ahead(way))
                    def _():
                        along(i, hop, way, source).start()

                    across(i, hop if way == 0 else depth - hop, block, True)

    for step in range(depth):
        source = (level + depth - step) % depth
        for i in range(count):
            x_spot, y_spot = fulls[i].at[source, x_chip, core], fulls[i].at[source, y_chip, core]
            remote(shards[i], x_spot, x_sems, (i, step), level, here).wait_recv()
            if step % 2 == 0:
                send(x_spot, x_spot, d_sems, (i, step), level, y_next)
            to_twin(i, step, x_chip)
            remote(shards[i], y_spot, y_sems, (i, step), level, here).wait_recv()
            if step % 2 == 1:
                send(y_spot, y_spot, d_sems, (i, step), level, x_next)
            to_twin(i, step, y_chip)
    for step in range(depth):
        source = (level + depth - step) % depth
        for i in range(count):
            spot = fulls[i].at[source, far_chip, core]
            remote(shards[i], spot, d_sems, (i, step), level, here).wait_recv()
            to_twin(i, step, far_chip)
    for step in range(depth):
        source = (level + depth - step) % depth
        for i in range(count):
            for chip_at in range(4):
                spot = fulls[i].at[source, chip_at, 1 - core]
                remote(shards[i], spot, c_sems, (i, step, chip_at), level, here).wait_recv()
    if more:
        for way in range(1, depth):
            spot = parts.at[(level + depth - way) % depth]
            remote(columns(level), spot, w_sems, (way,), level, here).wait_recv()
        for way in range(1, 8):
            spot = arrived.at[(here + 8 - way) % 8]
            remote(picked.at[here], spot, p_sems, (way,), level, here).wait_recv()
    for i in range(count):
        for step in range(depth):
            across(i, step, shards[i], False)
        for hop in () if more else range(depth):
            for way in range(2):

                @pl.when(comes(hop, way) & ahead(way))
                def _(i=i, hop=hop, way=way):
                    along(i, hop, way, back(hop, way)).wait_send()

    for copy in locals_:
        copy.wait()
    for copy in started:
        copy.wait_send()


def gather_plane(shards, ident, wide=None, rows=None, routes=None, length=None):
    depth, count, more = lax.axis_size("dp"), len(shards), wide is not None
    if lax.axis_size("expert") != 8:
        fulls = [lax.all_gather(s, both, axis=0, tiled=True) for s in shards]
        if more:
            fulls.append(lax.all_to_all(wide, "dp", split_axis=1, concat_axis=0, tiled=True))
            picked = matmul_tn(slots_of(routes, length, rows.shape[0]), rows).astype(rows.dtype).reshape(slot_shape(rows.shape[0]) + rows.shape[1:])
            fulls.append(lax.all_to_all(picked, "expert", split_axis=0, concat_axis=0, tiled=True))
        return fulls
    extra, extra_out = [], []
    if more:
        picked = jax.ShapeDtypeStruct(slot_shape(rows.shape[0]) + rows.shape[1:], rows.dtype)
        extra = [wide, rows, routes, length]
        extra_out = [
            jax.ShapeDtypeStruct((depth, wide.shape[0], wide.shape[1] // depth), wide.dtype),
            jax.ShapeDtypeStruct(picked.shape, picked.dtype),
        ]
    kinds = []
    for shape in ((count, depth),) * 4 + ((count, depth, 4), (depth,), (8,), (count, depth)):
        kinds += [pltpu.SemaphoreType.DMA(shape)] * 2
    fulls = pl.pallas_call(
        functools.partial(gather_kernel, depth, count, more),
        out_shape=[jax.ShapeDtypeStruct((depth, 4, 2) + s.shape, s.dtype) for s in shards] + extra_out,
        in_specs=[pl.BlockSpec(memory_space=pl.ANY)] * (count + more)
        + [pl.BlockSpec(memory_space=pltpu.VMEM)] * 2 * more
        + [pl.BlockSpec(memory_space=pltpu.SMEM)] * more,
        out_specs=[pl.BlockSpec(memory_space=pl.ANY)] * (count + len(extra_out)),
        scratch_shapes=[pltpu.SemaphoreType.DMA((count + 2,))]
        + kinds
        + ([pltpu.VMEM(picked.shape, picked.dtype)] if more else []),
        compiler_params=pltpu.CompilerParams(collective_id=ident, has_side_effects=True),
        cost_estimate=pl.CostEstimate(flops=1, bytes_accessed=1, transcendentals=0),
        name=f"gather_plane_{ident}",
    )(*shards, *extra)
    full = [f.reshape((-1,) + s.shape[1:]) for f, s in zip(fulls, shards)]
    if more:
        full += [fulls[count].reshape((-1, extra_out[0].shape[2])), fulls[count + 1]]
    return full


def scatter_kernel(depth, count, with_z, work, *refs):
    grads, refs = refs[:count], refs[count:]
    if with_z:
        tall, summed, refs = refs[0], refs[1], refs[2:]
    if work:
        operands, refs = refs[:6], refs[6:]
    if with_z:
        outs, refs = refs[:count], refs[count:]
    else:
        packed, refs = refs[0], refs[1:]
        width = packed.shape[2]
        made_rows = operands[0].shape[0] // depth
        tops = [0]
        for grad in grads:
            tops.append(tops[-1] + grad.shape[3] * grad.shape[4] // width)
    if work:
        results, buffers, refs = (*refs[:2], packed), refs[-9:], refs[2:-9]
        staged, staged_sems, refs = refs[-2], refs[-1], refs[:-2]
    if with_z:
        parts, returned, keep, p_sems, w_sems = refs[0], refs[1], refs[-1], refs[-3:-1], refs[-5:-3]
        refs = refs[2:-5]
    own, twins, first, second = (refs[i * count : (i + 1) * count] for i in range(4))
    n = 4 * count
    levels = refs[n : n + count] if with_z else ()
    n += len(levels)
    load, c_sems, f_sems, s_sems = refs[n], refs[n + 1 : n + 3], refs[n + 3 : n + 5], refs[n + 5 : n + 7]
    z_sems = refs[n + 7 : n + 9]
    level, here = lax.axis_index("dp"), lax.axis_index("expert")
    chip, core, x, y, twin, x_next, y_next = plane()
    greet(depth, [(here + way) % 8 for way in range(1, 8)] if with_z else (twin, x_next, y_next), with_z)
    started, loads, flown = [], {}, []

    def send(*a):
        copy = remote(*a)
        copy.start()
        started.append(copy)

    if with_z:
        width = tall.shape[2]

        def columns(at):
            return parts.at[:, pl.ds(pl.multiple_of(at * width, width), width)]

        capacity = returned.shape[1]

        def slots(mate):
            return summed.at[pl.ds(pl.multiple_of(mate * capacity, 16), capacity)]

        for way in range(1, depth):
            target = (level + way) % depth
            send(tall.at[target], columns(level), w_sems, (way,), target, here)
        kept = [
            pltpu.make_async_copy(tall.at[level], columns(level), keep.at[0]),
            pltpu.make_async_copy(slots(here), returned.at[here], keep.at[1]),
        ]
        for copy in kept:
            copy.start()
    order = [(step, (step + level + 1) % depth) for step in range(depth)]
    for step, at in order:
        for i in range(count):
            send(grads[i].at[at, :, 1 - core], twins[i].at[step], c_sems, (i, step), level, twin)
            loads[i, step] = pltpu.make_async_copy(grads[i].at[at, :, core], own[i].at[step], load.at[i, step])
            loads[i, step].start()
    if with_z:
        for way in range(1, 8):
            mate = (here + way) % 8
            send(slots(mate), returned.at[here], p_sems, (way,), level, mate)
    jobs = expert_work(operands, results, buffers) if work else iter(())

    def add(target, other):
        target[...] = (target[...].astype(jnp.float32) + other[...].astype(jnp.float32)).astype(jnp.bfloat16)

    def chips(step):
        if step % 2 == 0:
            return (1 - x, 3 - x), (x, 2 + x), x_next, y_next
        return (2 - 2 * y, 3 - 2 * y), (2 * y, 2 * y + 1), y_next, x_next

    for step, at in order:
        away, near, first_next, second_next = chips(step)
        for i in range(count):
            loads[i, step].wait()
            remote(own[i].at[step], twins[i].at[step], c_sems, (i, step), level, here).wait_recv()
            for side in range(2):
                add(own[i].at[step, away[side]], twins[i].at[step, away[side]])
                send(own[i].at[step, away[side]], first[i].at[step, side], f_sems, (i, step, side), level, first_next)
        for i in range(count):
            for side in range(2):
                add(own[i].at[step, near[side]], twins[i].at[step, near[side]])
    next(jobs, None)
    next(jobs, None)
    for step, at in order:
        away, near, first_next, second_next = chips(step)
        for i in range(count):
            for side in range(2):
                remote(own[i].at[step, 0], first[i].at[step, side], f_sems, (i, step, side), level, here).wait_recv()
                add(own[i].at[step, near[side]], first[i].at[step, side])
            across = chip + 2 - 4 * y if step % 2 == 0 else chip + 1 - 2 * x
            send(own[i].at[step, across], second[i].at[step], s_sems, (i, step), level, second_next)
        if step == 1:
            next(jobs, None)
    for _ in jobs:
        pass
    for step, at in order:
        for i in range(count):
            remote(own[i].at[step, 0], second[i].at[step], s_sems, (i, step), level, here).wait_recv()
            add(second[i].at[step], own[i].at[step, chip])
            if with_z:
                if step < depth - 1:
                    send(second[i].at[step], levels[i].at[step], z_sems, (i, step), at, here)
            else:
                sums = second[i][step]
                for piece in range(sums.shape[1] // width):
                    place = pl.ds(tops[i] + piece * sums.shape[0], sums.shape[0])
                    staged[step, place] = sums[:, piece * width : (piece + 1) * width]
        if not with_z:
            copy = pltpu.make_async_copy(staged.at[step], packed.at[at, made_rows:], staged_sems.at[step])
            copy.start()
            flown.append(copy)
    for copy in flown:
        copy.wait()
    if with_z:
        for i in range(count):
            total = second[i][depth - 1].astype(jnp.float32)
            for step in range(depth - 1):
                remote(second[i].at[step], levels[i].at[step], z_sems, (i, step), level, here).wait_recv()
                total = total + levels[i][step].astype(jnp.float32)
            outs[i][...] = total
        for way in range(1, depth):
            source = (level + depth - way) % depth
            remote(tall.at[level], columns(source), w_sems, (way,), level, here).wait_recv()
        for way in range(1, 8):
            spot = returned.at[(here + 8 - way) % 8]
            remote(spot, spot, p_sems, (way,), level, here).wait_recv()
        for copy in kept:
            copy.wait()
    for copy in started:
        copy.wait_send()


def expert_work(operands, results, buffers):
    act, pulled, rows_in, pre_grad, down, mix = operands
    act_at, grads_at, rows_at, pre_at, down_at, mix_at, tall, low, sems = buffers
    pairs = ((act, act_at), (pulled, grads_at), (down, down_at), (rows_in, rows_at), (pre_grad, pre_at), (mix, mix_at))
    copies = [pltpu.make_async_copy(a, b, sems.at[i]) for i, (a, b) in enumerate(pairs)]
    for copy in copies:
        copy.start()
    width = act.shape[1]
    tile = tall.shape[1]
    height = low.shape[1]
    flights = []

    def put(slot, stage, target, sem):
        copy = pltpu.make_async_copy(stage.at[slot], target, sems.at[sem + slot])
        copy.start()
        flights.append(copy)

    def settle(keep):
        while len(flights) > keep:
            flights.pop(0).wait()

    for i in (0, 1, 5):
        copies[i].wait()
    grads_at[...] = (grads_at[...].astype(jnp.float32) * mix_at[...]).astype(jnp.bfloat16)
    for i in range(width // tile):
        settle(1)
        tall[i % 2] = matmul_tn(act_at[:, i * tile : (i + 1) * tile], grads_at[...])
        put(i % 2, tall, results[0].at[i * tile : (i + 1) * tile], 6)
    yield
    copies[2].wait()
    settle(0)
    for i in range(results[2].shape[0]):
        settle(1)
        low[i % 2] = matmul(act_at[i * height : (i + 1) * height, :], down_at[...]).astype(jnp.bfloat16)
        put(i % 2, low, results[2].at[i, 0:height], 8)
    yield
    settle(0)
    copies[3].wait()
    copies[4].wait()
    for i in range(width // tile):
        settle(1)
        low[i % 2, 0:tile] = matmul_tn(rows_at[:, i * tile : (i + 1) * tile], pre_at[...]).astype(jnp.bfloat16)
        copy = pltpu.make_async_copy(low.at[i % 2, 0:tile], results[1].at[i * tile : (i + 1) * tile], sems.at[8 + i % 2])
        copy.start()
        flights.append(copy)
    yield
    settle(0)


def scatter_plane(grads, ident, work=None, tall=None, summed=None, tok_rows=None):
    depth, count, with_z = lax.axis_size("dp"), len(grads), tall is not None
    low = jnp.bfloat16
    if lax.axis_size("expert") != 8:
        sums = [lax.psum_scatter(g, both, scatter_dimension=0, tiled=True).astype(jnp.float32) for g in grads]
        if work is not None:
            act, pulled, rows_in, pre_grad, down, mix = work
            grad_rows = (pulled.astype(jnp.float32) * mix).astype(low)
            sums.append(matmul(act, down).astype(low))
            sums.append(matmul_tn(act, grad_rows))
            sums.append(matmul_tn(rows_in, pre_grad).astype(low))
        if with_z:
            sums.append(lax.all_to_all(tall, "dp", split_axis=0, concat_axis=1, tiled=True))
            summed = summed.reshape(slot_shape(tok_rows) + summed.shape[1:])
            sums.append(lax.all_to_all(summed, "expert", split_axis=0, concat_axis=0, tiled=True))
        return sums
    grads = [g.reshape((depth, 4, 2, g.shape[0] // (8 * depth)) + g.shape[1:]) for g in grads]
    blocks = [g.shape[3:] for g in grads]
    width = min(b[1] for b in blocks)
    sums = [jax.ShapeDtypeStruct(b, jnp.float32) for b in blocks]
    if not with_z:
        sums = [jax.ShapeDtypeStruct((depth, sum(b[0] * b[1] for b in blocks) // width, width), low)]
    scratch = [pltpu.VMEM((depth, 4) + b, low) for b in blocks] * 2
    scratch += [pltpu.VMEM((depth, 2) + b, low) for b in blocks]
    scratch += [pltpu.VMEM((depth,) + b, low) for b in blocks]
    if with_z:
        scratch += [pltpu.VMEM((depth - 1,) + b, low) for b in blocks]
    sems = [pltpu.SemaphoreType.DMA((count, depth))] * 3 + [pltpu.SemaphoreType.DMA((count, depth, 2))] * 2
    sems += [pltpu.SemaphoreType.DMA((count, depth))] * 2
    operands, made = (), []
    if with_z:
        sems += [pltpu.SemaphoreType.DMA((count, depth))] * 2
        sems += [pltpu.SemaphoreType.DMA((depth,))] * 2
        sems += [pltpu.SemaphoreType.DMA((8,))] * 2 + [pltpu.SemaphoreType.DMA((2,))]
        operands = (tall.reshape((depth, -1, tall.shape[1])), summed)
        made = [
            jax.ShapeDtypeStruct((tall.shape[0] // depth, tall.shape[1] * depth), tall.dtype),
            jax.ShapeDtypeStruct(slot_shape(tok_rows) + summed.shape[1:], summed.dtype),
        ]
    if work is not None:
        operands = tuple(work)
        act, down = work[0], work[4]
        made = [
            jax.ShapeDtypeStruct((act.shape[1], act.shape[1]), jnp.float32),
            jax.ShapeDtypeStruct((act.shape[1], work[3].shape[1]), low),
        ]
        sems += [pltpu.VMEM((depth,) + sums[0].shape[1:], low), pltpu.SemaphoreType.DMA((depth,))]
        sums = [jax.ShapeDtypeStruct((depth, act.shape[0] // depth + sums[0].shape[1], width), low)]
        sems += [pltpu.VMEM(o.shape, o.dtype) for o in operands]
        sems += [
            pltpu.VMEM((2, 256, down.shape[1]), jnp.float32),
            pltpu.VMEM((2, act.shape[0] // depth, down.shape[1]), low),
            pltpu.SemaphoreType.DMA((10,)),
        ]
    return list(
        pl.pallas_call(
            functools.partial(scatter_kernel, depth, count, with_z, work is not None),
            out_shape=sums + made,
            in_specs=[pl.BlockSpec(memory_space=pl.ANY)] * (count + len(operands)),
            out_specs=[pl.BlockSpec(memory_space=pltpu.VMEM if with_z else pl.ANY)] * len(sums)
            + [pl.BlockSpec(memory_space=pl.ANY)] * len(made),
            scratch_shapes=scratch + sems,
            compiler_params=pltpu.CompilerParams(
                collective_id=ident, has_side_effects=True, vmem_limit_bytes=58 * 2**20
            ),
            cost_estimate=pl.CostEstimate(flops=1, bytes_accessed=200 * 2**20, transcendentals=0),
            name=f"scatter_plane_{ident}",
        )(*grads, *operands)
    )


def finish_scatter(packed, top, shapes):
    packed = lax.psum_scatter(packed, "dp", scatter_dimension=0)
    width = packed.shape[1]
    outs = [packed]
    for rows, columns in shapes:
        pieces = columns // width
        blocks = [packed[top + i * rows : top + (i + 1) * rows].astype(jnp.float32) for i in range(pieces)]
        outs.append(jnp.concatenate(blocks, axis=1))
        top += pieces * rows
    return outs


def body(
    tokens,
    seq_lengths,
    routes,
    w_qkv,
    w_out,
    w_up,
    w_down,
    gain_attn,
    gain_mlp,
    w_mix,
    expert_up,
    expert_down,
    cotangent,
):
    tok_rows, model_width = tokens.shape
    axis_dp, axis_experts = lax.axis_size("dp"), lax.axis_size("expert")
    expert_total = axis_experts * expert_up.shape[0]
    capacity = max(2, 5 * tok_rows // (4 * expert_total))
    slots = expert_total * capacity
    ff_expert = expert_up.shape[2]

    small = jnp.concatenate([gain_attn[:, None], gain_mlp[:, None], w_mix], axis=1)
    small = jnp.pad(small, ((0, 0), (0, 128 - small.shape[1])))
    length = seq_lengths[0]
    valid_rows = jnp.arange(tok_rows, dtype=jnp.int32) < length

    def pick(rows):
        return matmul(slot_table, rows).astype(jnp.bfloat16).reshape(expert_total, capacity, model_width)

    def dispatch(rows):
        arrived = lax.all_to_all(pick(rows), "expert", split_axis=0, concat_axis=0, tiled=True)
        return arrived.reshape(slots, model_width)

    def spread(rows):
        return lax.all_gather(rows, "dp", axis=0, tiled=True)

    def unspread(rows):
        return lax.psum_scatter(rows, "dp", scatter_dimension=0, tiled=True)

    def give_back(summed):
        summed = summed.reshape(expert_total, capacity, model_width)
        back = lax.all_to_all(summed, "expert", split_axis=0, concat_axis=0, tiled=True)
        return matmul_tn(slot_table, back.reshape(slots, model_width))

    down_part = expert_down[0]

    upstream_low = jnp.where(valid_rows[:, None], cotangent, jnp.zeros_like(cotangent))
    upstream = upstream_low.astype(jnp.float32)
    qkv_full, out_full, small_full, up_part, pulled_here = gather_plane(
        [w_qkv, w_out, small], 0, expert_up[0], cotangent, routes, seq_lengths
    )
    slot_table = slots_of(lax.optimization_barrier((routes, qkv_full))[0], length, tok_rows).T
    pulled_rows = spread(pulled_here.reshape(slots, model_width))
    gain_one = small_full[:, 0].astype(jnp.float32)
    gain_two = small_full[:, 1].astype(jnp.float32)
    mix_full = small_full[:, 2:4]
    mix_lean = (mix_full[:, 0] - mix_full[:, 1].astype(jnp.float32)).astype(jnp.float32)

    inputs = tokens.astype(jnp.float32)
    scaled_one, inverse_one = norm_forward(inputs)
    normed_one = (scaled_one * gain_one).astype(jnp.bfloat16)
    joined = matmul(normed_one, qkv_full).astype(jnp.bfloat16)
    heads_out, log_total = attention_forward(joined, seq_lengths)
    after_attn = inputs + matmul(heads_out, out_full)
    scaled_two, inverse_two = norm_forward(after_attn)
    normed_two = (scaled_two * gain_two).astype(jnp.bfloat16)

    rows_here = dispatch(normed_two)
    rows_here, w_up, w_down = lax.optimization_barrier((rows_here, w_up, w_down))
    rows_in = spread(rows_here)
    up_full, down_full = gather_plane([w_up, w_down], 1)

    pulled_rows, up_full, down_full = lax.optimization_barrier((pulled_rows, up_full, down_full))
    mix_weights = jax.nn.softmax(matmul(normed_two, mix_full), axis=-1)
    grad_down, grad_up, normed_grad, dense_out, pull_dense = dense_branch(
        normed_two, up_full, down_full, upstream_low, mix_weights[:, 0:1]
    )
    lean_dense = mix_weights[:, 0:1] * mix_weights[:, 1:2] * pull_dense
    normed_grad = normed_grad + lean_dense * mix_lean[None, :]

    act_pull = matmul_nt(pulled_rows, down_part)
    rows_in, act_pull, grad_up, grad_down, normed_grad = lax.optimization_barrier(
        (rows_in, act_pull, grad_up, grad_down, normed_grad)
    )
    act_rows, pre_grad, row_mix, input_grad, lean_rows = expert_branch(
        rows_in, act_pull, up_part, small_full, mix_lean[None, :]
    )
    in_grad_here = unspread(input_grad)
    *sums, grad_expert_down, grad_expert_up = scatter_plane(
        [grad_up, grad_down], 2, (act_rows, pulled_rows, rows_in, pre_grad, down_part, row_mix)
    )
    grad_expert_down = grad_expert_down[None]
    in_grad_here, *sums = lax.optimization_barrier((in_grad_here, *sums))
    if len(sums) == 1:
        outs_here, grad_up, grad_down = finish_scatter(sums[0], slots, (w_up.shape, w_down.shape))
    else:
        grad_up, grad_down, outs_here = sums[0], sums[1], unspread(sums[2])
    in_grad_back = give_back(in_grad_here)

    normed_grad = normed_grad + in_grad_back
    lean_grad = jnp.sum(normed_two.astype(jnp.float32) * lean_dense, axis=0) - lean_rows[0]
    mlp_in_grad, grad_gain_two = norm_backward(normed_grad, scaled_two, inverse_two, gain_two)
    resid_grad = upstream + mlp_in_grad
    attn_grad = resid_grad.astype(jnp.bfloat16)
    grad_out = matmul_tn(heads_out, attn_grad)
    heads_grad = matmul_nt(attn_grad, out_full).astype(jnp.bfloat16)
    joined_grad = jnp.concatenate(
        attention_backward(joined, heads_grad, heads_out, log_total, seq_lengths), axis=1
    )
    grad_qkv = matmul_tn(normed_one, joined_grad)
    normed_one_grad = matmul_nt(joined_grad, qkv_full)
    attn_in_grad, grad_gain_one = norm_backward(normed_one_grad, scaled_one, inverse_one, gain_one)
    grad_inputs = resid_grad + attn_in_grad

    small_grads = jnp.stack([grad_gain_one, grad_gain_two, lean_grad, -lean_grad], axis=1)
    small_grads = jnp.pad(small_grads, ((0, 0), (0, 128 - small_grads.shape[1])))
    grad_expert_down = jnp.where(length >= 0, grad_expert_down, 0.0)
    small_grads, grad_expert_down = lax.optimization_barrier((small_grads.astype(jnp.bfloat16), grad_expert_down))
    grad_qkv, grad_out, small_grads, grad_expert_up, returned = scatter_plane(
        [grad_qkv.astype(jnp.bfloat16), grad_out.astype(jnp.bfloat16), small_grads],
        3,
        tall=grad_expert_up,
        summed=outs_here,
        tok_rows=tok_rows,
    )
    expert_out = matmul_tn(slot_table, returned.reshape(slots, model_width))
    result = after_attn + mix_weights[:, 0:1] * dense_out + mix_weights[:, 1:2] * expert_out
    grad_expert_up = grad_expert_up.astype(jnp.float32)[None]
    return (
        result,
        grad_inputs,
        grad_qkv,
        grad_out,
        grad_up,
        grad_down,
        small_grads[:, 0],
        small_grads[:, 1],
        small_grads[:, 2:4],
        grad_expert_up,
        grad_expert_down,
    )


def solution(mesh):
    rows, vector = P(both, None), P(both)
    experts = P("expert", "dp", None)
    return jax.shard_map(
        body,
        mesh=mesh,
        in_specs=(rows, vector, rows, rows, rows, rows, rows, vector, vector, rows, experts, experts, rows),
        out_specs=(rows, rows, rows, rows, rows, rows, vector, vector, rows, experts, experts),
        check_vma=False,
    )
```

```python
import functools

import jax
import jax.numpy as jnp
from jax import lax
from jax.experimental import pallas as pl
from jax.experimental.pallas import tpu as pltpu
from jax.sharding import PartitionSpec as P

HEADS = 16

epsilon = 1e-05
root_half = 0.7071067811865476
inv_root_two_pi = 0.3989422804014327
highest = lax.Precision.HIGHEST
both = ("dp", "expert")


def gelu_pair(values):
    half = 0.5 * (1.0 + lax.erf(values * root_half))
    return values * half, half + values * jnp.exp(-0.5 * values * values) * inv_root_two_pi


def dot(left, right, dims):
    return lax.dot_general(left, right, (dims, ((), ())), preferred_element_type=jnp.float32)


def matmul(left, right):
    return dot(left, right, ((1,), (0,)))


def matmul_nt(left, right):
    return dot(left, right, ((1,), (1,)))


def matmul_tn(left, right):
    return dot(left, right, ((0,), (0,)))


def norm_forward(values):
    row_mean = jnp.mean(values, axis=-1, keepdims=True)
    centred = values - row_mean
    row_var = jnp.mean(centred * centred, axis=-1, keepdims=True)
    inverse = lax.rsqrt(row_var + epsilon)
    return (centred * inverse, inverse)


def norm_backward(upstream, scaled, inverse, gain_row):
    gain_grad = jnp.sum(upstream * scaled, axis=0)
    inner = upstream * gain_row
    centred_grad = (
        inner
        - jnp.mean(inner, axis=-1, keepdims=True)
        - scaled * jnp.mean(inner * scaled, axis=-1, keepdims=True)
    )
    return (inverse * centred_grad, gain_grad)


def head_scores(queries, keys_all, length, row_start, scale):
    scores = matmul_nt(queries, keys_all) * scale
    rows_at = row_start + lax.broadcasted_iota(jnp.int32, scores.shape, 0)
    cols_at = lax.broadcasted_iota(jnp.int32, scores.shape, 1)
    return jnp.where((cols_at <= rows_at) & (cols_at < length), scores, -1000000000.0)


def attention_forward_kernel(head_width, bands, length_ref, q_ref, k_ref, v_ref, out_ref, log_ref):
    length = length_ref[0]
    scale = head_width ** (-0.5)
    tok_rows, lanes = q_ref.shape
    height = tok_rows // bands
    lane = lax.broadcasted_iota(jnp.int32, (1, lanes), 1) // head_width
    for band in range(bands):
        top, end = band * height, (band + 1) * height
        keys_all, values_all = k_ref[0:end, :], v_ref[0:end, :]
        queries = q_ref[top:end, :]
        mixed = jnp.zeros((height, lanes), jnp.float32)
        logs = []
        for head in range(lanes // head_width):
            mine = lane == head
            scores = head_scores(jnp.where(mine, queries, 0), keys_all, length, top, scale)
            top_score = jnp.max(scores, axis=-1, keepdims=True)
            raised = jnp.exp(scores - top_score)
            row_total = jnp.sum(raised, axis=-1, keepdims=True)
            probs = (raised / row_total).astype(jnp.bfloat16)
            mixed = mixed + matmul(probs, jnp.where(mine, values_all, 0))
            logs.append(top_score + jnp.log(row_total))
        out_ref[top:end, :] = mixed.astype(jnp.bfloat16)
        spread = jnp.broadcast_to(logs[0], (height, lanes))
        for head in range(1, len(logs)):
            spread = jnp.where(lane == head, logs[head], spread)
        log_ref[top:end, :] = spread


def attention_forward(joined, length):
    tok_rows, width = joined.shape[0], joined.shape[1] // 3
    head_width = width // HEADS
    lanes = max(128, head_width)
    tiles = width // lanes
    bands = 2

    def part(which):
        return pl.BlockSpec((tok_rows, lanes), lambda i: (0, which * tiles + i))

    return pl.pallas_call(
        functools.partial(attention_forward_kernel, head_width, bands),
        grid=(tiles,),
        out_shape=[
            jax.ShapeDtypeStruct((tok_rows, width), jnp.bfloat16),
            jax.ShapeDtypeStruct((tok_rows, width), jnp.float32),
        ],
        in_specs=[pl.BlockSpec(memory_space=pltpu.SMEM), part(0), part(1), part(2)],
        out_specs=[part(0), part(0)],
        compiler_params=pltpu.CompilerParams(vmem_limit_bytes=32 * 2**20),
        cost_estimate=pl.CostEstimate(flops=4 * tok_rows * tok_rows * width, bytes_accessed=10 * tok_rows * width, transcendentals=0),
        name="attention_forward",
    )(length, joined, joined, joined)


def attention_backward_kernel(head_width, bands, length_ref, q_ref, k_ref, v_ref, g_ref, o_ref, log_ref, dq_ref, dk_ref, dv_ref, dk_sum, dv_sum):
    length = length_ref[0]
    scale = head_width ** (-0.5)
    tok_rows, lanes = q_ref.shape
    height = tok_rows // bands
    lane = lax.broadcasted_iota(jnp.int32, (1, lanes), 1) // head_width
    for band in range(bands):
        top, end = band * height, (band + 1) * height
        keys_all, values_all = k_ref[0:end, :], v_ref[0:end, :]
        queries, grads = q_ref[top:end, :], g_ref[top:end, :]
        turned = lax.transpose(log_ref[top:end, :], (1, 0))
        products = lax.transpose(grads.astype(jnp.float32) * o_ref[top:end, :].astype(jnp.float32), (1, 0))
        dq = jnp.zeros((height, lanes), jnp.float32)
        dk = jnp.zeros((end, lanes), jnp.float32)
        dv = jnp.zeros((end, lanes), jnp.float32)
        keys_at = lax.broadcasted_iota(jnp.int32, (end, height), 0)
        rows_at = top + lax.broadcasted_iota(jnp.int32, (end, height), 1)
        allowed = (keys_at <= rows_at) & (keys_at < length)
        for head in range(lanes // head_width):
            mine = lane == head
            own_q, own_g = jnp.where(mine, queries, 0), jnp.where(mine, grads, 0)
            log_total = turned[head * head_width : head * head_width + 1, :]
            delta = jnp.sum(products[head * head_width : (head + 1) * head_width, :], axis=0, keepdims=True)
            scores = jnp.where(allowed, matmul_nt(keys_all, own_q) * scale, -1000000000.0)
            probs = jnp.exp(scores - log_total)
            prob_grad = matmul_nt(values_all, own_g)
            score_grad = (probs * (prob_grad - delta)).astype(jnp.bfloat16)
            dv = dv + matmul(probs.astype(jnp.bfloat16), own_g)
            dk = dk + matmul(score_grad, own_q)
            dq = dq + matmul_tn(score_grad, jnp.where(mine, keys_all, 0))
        dq_ref[top:end, :] = (dq * scale).astype(jnp.bfloat16)
        if band == 0:
            dk_sum[...] = jnp.zeros_like(dk_sum)
            dv_sum[...] = jnp.zeros_like(dv_sum)
        dk_sum[0:end, :] += dk
        dv_sum[0:end, :] += dv
    dk_ref[...] = (dk_sum[...] * scale).astype(jnp.bfloat16)
    dv_ref[...] = dv_sum[...].astype(jnp.bfloat16)


def attention_backward(joined, heads_grad, heads_out, log_total, length):
    tok_rows, width = joined.shape[0], joined.shape[1] // 3
    head_width = width // HEADS
    lanes = max(128, head_width)
    tiles = width // lanes
    bands = 2

    def part(which):
        return pl.BlockSpec((tok_rows, lanes), lambda i: (0, which * tiles + i))

    return pl.pallas_call(
        functools.partial(attention_backward_kernel, head_width, bands),
        grid=(tiles,),
        out_shape=[jax.ShapeDtypeStruct((tok_rows, width), jnp.bfloat16)] * 3,
        in_specs=[pl.BlockSpec(memory_space=pltpu.SMEM), part(0), part(1), part(2), part(0), part(0), part(0)],
        out_specs=[part(0)] * 3,
        scratch_shapes=[pltpu.VMEM((tok_rows, lanes), jnp.float32)] * 2,
        compiler_params=pltpu.CompilerParams(vmem_limit_bytes=32 * 2**20),
        cost_estimate=pl.CostEstimate(flops=10 * tok_rows * tok_rows * width, bytes_accessed=20 * tok_rows * width, transcendentals=0),
        name="attention_backward",
    )(length, joined, joined, joined, heads_grad, heads_out, log_total)


def expert_kernel(rows_ref, pull_ref, up_ref, small_ref, lean_ref, act_ref, pre_ref, mix_ref, in_ref, sum_ref):
    low = jnp.bfloat16
    chains = [slice(top, top + 256) for top in range(0, rows_ref.shape[0], 256)]
    pre_acts = [matmul(rows_ref[rows, :], up_ref[...]) for rows in chains]
    all_logits = [matmul(rows_ref[rows, :], small_ref[...]) for rows in chains]
    parts = []
    for rows, pre_act, logits in zip(chains, pre_acts, all_logits):
        first, second = logits[:, 2:3], logits[:, 3:4]
        top = jnp.maximum(first, second)
        first, second = jnp.exp(first - top), jnp.exp(second - top)
        mix_dense, mix_expert = first / (first + second), second / (first + second)
        act_pull = pull_ref[rows, :]
        gelu, slope = gelu_pair(pre_act)
        act = gelu.astype(low)
        act_ref[rows, :] = act
        lean = mix_dense * mix_expert * jnp.sum(act.astype(jnp.float32) * act_pull, axis=1, keepdims=True)
        pre_grad = (mix_expert * act_pull * slope).astype(low)
        pre_ref[rows, :] = pre_grad
        in_ref[rows, :] = (matmul_nt(pre_grad, up_ref[...]) - lean * lean_ref[...]).astype(low)
        mix_ref[rows, :] = mix_expert
        parts.append(jnp.sum(rows_ref[rows, :].astype(jnp.float32) * lean, axis=0, keepdims=True))
    part = sum(parts[1:], parts[0])
    sum_ref[...] = jnp.where(pl.program_id(0) == 0, part, sum_ref[...] + part)


def expert_branch(rows_in, act_pull, up_part, small_full, mix_lean):
    count, width = rows_in.shape
    hidden = up_part.shape[1]
    height = 512

    def tall(columns):
        return pl.BlockSpec((height, columns), lambda i: (i, 0))

    def whole(array):
        return pl.BlockSpec(array.shape, lambda i: (0, 0))

    low = jnp.bfloat16
    return pl.pallas_call(
        expert_kernel,
        grid=(count // height,),
        out_shape=[
            jax.ShapeDtypeStruct((count, hidden), low),
            jax.ShapeDtypeStruct((count, hidden), low),
            jax.ShapeDtypeStruct((count, 1), jnp.float32),
            jax.ShapeDtypeStruct((count, width), low),
            jax.ShapeDtypeStruct((1, width), jnp.float32),
        ],
        in_specs=[tall(width), tall(hidden), whole(up_part), whole(small_full), whole(mix_lean)],
        out_specs=[tall(hidden), tall(hidden), tall(1), tall(width), whole(mix_lean)],
        compiler_params=pltpu.CompilerParams(vmem_limit_bytes=58 * 2**20),
        cost_estimate=pl.CostEstimate(
            flops=4 * count * width * hidden, bytes_accessed=16 * count * width, transcendentals=0
        ),
        name="expert_branch",
    )(rows_in, act_pull, up_part, small_full, mix_lean)


def dense_kernel(normed_ref, up_ref, down_ref, grad_ref, mix_ref, gdown_ref, gup_ref, ngrad_ref, out_ref, pull_ref):
    normed, upstream, mix = normed_ref[...], grad_ref[...], mix_ref[...]
    hidden = matmul(normed, up_ref[...])
    dense_pull = matmul_nt(upstream, down_ref[...])
    gelu, slope = gelu_pair(hidden)
    act = gelu.astype(jnp.bfloat16)
    pull = jnp.sum(act.astype(jnp.float32) * dense_pull, axis=1, keepdims=True)
    hidden_grad = (mix * dense_pull * slope).astype(jnp.bfloat16)
    grad_out = (upstream.astype(jnp.float32) * mix).astype(jnp.bfloat16)
    gdown_ref[...] = matmul_tn(act, grad_out).astype(jnp.bfloat16)
    gup_ref[...] = matmul_tn(normed, hidden_grad).astype(jnp.bfloat16)
    ngrad = matmul_nt(hidden_grad, up_ref[...])
    dense_out = matmul(act, down_ref[...])

    @pl.when(pl.program_id(0) == 0)
    def _():
        ngrad_ref[...] = ngrad
        out_ref[...] = dense_out
        pull_ref[...] = pull

    @pl.when(pl.program_id(0) > 0)
    def _():
        ngrad_ref[...] += ngrad
        out_ref[...] += dense_out
        pull_ref[...] += pull


def dense_branch(normed_two, up_full, down_full, upstream_low, mix):
    rows, width = normed_two.shape
    ff = up_full.shape[1]
    block = 512

    def whole(columns):
        return pl.BlockSpec((rows, columns), lambda i: (0, 0))

    across, down = pl.BlockSpec((width, block), lambda i: (0, i)), pl.BlockSpec((block, width), lambda i: (i, 0))
    return pl.pallas_call(
        dense_kernel,
        grid=(ff // block,),
        out_shape=[
            jax.ShapeDtypeStruct((ff, width), jnp.bfloat16),
            jax.ShapeDtypeStruct((width, ff), jnp.bfloat16),
            jax.ShapeDtypeStruct((rows, width), jnp.float32),
            jax.ShapeDtypeStruct((rows, width), jnp.float32),
            jax.ShapeDtypeStruct((rows, 1), jnp.float32),
        ],
        in_specs=[whole(width), across, down, whole(width), whole(1)],
        out_specs=[down, across, whole(width), whole(width), whole(1)],
        compiler_params=pltpu.CompilerParams(vmem_limit_bytes=48 * 2**20),
        cost_estimate=pl.CostEstimate(flops=12 * rows * width * ff, bytes_accessed=8 * width * ff, transcendentals=0),
        name="dense_branch",
    )(normed_two, up_full, down_full, upstream_low, mix)


MESH = pl.DeviceIdType.MESH


def plane():
    here = lax.axis_index("expert")
    core, x, y = here % 2, (here // 2) % 2, here // 4
    return here // 2, core, x, y, here + 1 - 2 * core, here + 2 - 4 * x, here + 4 - 8 * y


def greet(depth, others, count):
    level = lax.axis_index("dp")
    barrier = pltpu.get_barrier_semaphore()
    for other in others:
        pl.semaphore_signal(barrier, inc=1, device_id=(level, other), device_id_type=MESH)
    if count:
        for step in range(1, depth):
            pl.semaphore_signal(
                barrier,
                inc=1,
                device_id=((level + step) % depth, lax.axis_index("expert")),
                device_id_type=MESH,
            )
    pl.semaphore_wait(barrier, len(others) + (depth - 1 if count else 0))


def remote(source, target, sems, slot, level, where):
    return pltpu.make_async_remote_copy(
        src_ref=source,
        dst_ref=target,
        send_sem=sems[0].at[slot],
        recv_sem=sems[1].at[slot],
        device_id=(level, where),
        device_id_type=MESH,
    )


def slot_shape(tok_rows):
    experts = lax.axis_size("expert")
    return (experts, max(2, 5 * tok_rows // (4 * experts)))


def slots_of(routes, length, tok_rows):
    experts, capacity = slot_shape(tok_rows)
    rows_at = lax.broadcasted_iota(jnp.int32, (1, tok_rows), 1)
    hits = (routes == lax.broadcasted_iota(jnp.int32, (experts, tok_rows), 0)) & (rows_at < length)
    hits = hits.astype(jnp.float32)
    earlier = lax.broadcasted_iota(jnp.int32, (tok_rows, tok_rows), 0) < lax.broadcasted_iota(jnp.int32, (tok_rows, tok_rows), 1)
    ranks = matmul(hits.astype(jnp.bfloat16), earlier.astype(jnp.bfloat16))
    rank = jnp.sum(hits * ranks, axis=0, keepdims=True)
    kept = (rows_at < length) & (rank < capacity)
    slot = routes * capacity + rank.astype(jnp.int32)
    slots_at = lax.broadcasted_iota(jnp.int32, (experts * capacity, tok_rows), 0)
    return ((slots_at == slot) & kept).astype(jnp.bfloat16)


def pick_rows(rows, routes, length, picked):
    experts, capacity, _ = picked.shape
    table = slots_of(routes[...], length[0], rows.shape[0])
    chosen = matmul(table, rows[...]).astype(jnp.bfloat16)
    for expert in range(experts):
        picked[expert] = chosen[expert * capacity : (expert + 1) * capacity]


def gather_kernel(depth, count, more, *refs):
    shards, refs = refs[:count], refs[count:]
    if more:
        wide, rows, routes, length, refs = refs[0], refs[1], refs[2], refs[3], refs[4:]
    fulls, refs = refs[:count], refs[count:]
    if more:
        parts, arrived, picked, refs = refs[0], refs[1], refs[-1], refs[2:-1]
    keep, sems = refs[0], refs[1:]
    up_sems, x_sems, y_sems, d_sems, c_sems, w_sems, p_sems, low_sems = (sems[2 * i : 2 * i + 2] for i in range(8))
    z_sems = (up_sems, low_sems)
    level, here = lax.axis_index("dp"), lax.axis_index("expert")
    chip, core, x, y, twin, x_next, y_next = plane()
    x_chip, y_chip, far_chip = chip + 1 - 2 * x, chip + 2 - 4 * y, 3 - chip
    mates = [(here + step) % 8 for step in range(1, 8)] if more else (twin, x_next, y_next)
    greet(depth, mates, True)
    started, locals_ = [], []

    def send(*a):
        copy = remote(*a)
        copy.start()
        started.append(copy)

    def stay(source, target, slot):
        copy = pltpu.make_async_copy(source, target, keep.at[slot])
        copy.start()
        locals_.append(copy)

    def to_twin(i, step, chip_at, source=None):
        spot = fulls[i].at[(level + depth - step) % depth, chip_at, core]
        send(spot if source is None else source, spot, c_sems, (i, step, chip_at), level, twin)

    def along(i, hop, way, source):
        block = fulls[i].at[source, chip, core]
        target = (level + (1 if way == 0 else depth - 1)) % depth
        return remote(shards[i] if hop == 0 else block, block, z_sems[way], (i, hop), target, here)

    def ahead(way):
        return level < depth - 1 if way == 0 else level > 0

    def comes(hop, way):
        return level >= hop if way == 0 else level < depth - hop

    def back(hop, way):
        return (level + depth - hop) % depth if way == 0 else (level + hop) % depth

    def across(i, step, origin, begin):
        block = fulls[i].at[(level + depth - step) % depth, chip, core]
        copies = (
            remote(origin, block, x_sems, (i, step), level, x_next),
            remote(origin, block, y_sems, (i, step), level, y_next),
            remote(origin, block, c_sems, (i, step, chip), level, twin),
        )
        for copy in copies:
            if begin:
                copy.start()
            else:
                copy.wait_send()

    if more:
        for step in range(1, depth):
            for i in range(count):
                target = (level + step) % depth
                send(shards[i], fulls[i].at[level, chip, core], up_sems, (i, step), target, here)
    else:
        for way in range(2):

            @pl.when(ahead(way))
            def _(way=way):
                for i in range(count):
                    along(i, 0, way, level).start()

    for i in range(count):
        stay(shards[i], fulls[i].at[level, chip, core], i)
        across(i, 0, shards[i], True)
    if more:
        width = wide.shape[1] // depth

        def columns(at):
            return wide.at[:, pl.ds(pl.multiple_of(at * width, width), width)]

        for way in range(1, depth):
            target = (level + way) % depth
            send(columns(target), parts.at[level], w_sems, (way,), target, here)
        stay(columns(level), parts.at[level], count)
        pick_rows(rows, routes, length, picked)
        for way in range(1, 8):
            mate = (here + way) % 8
            send(picked.at[mate], arrived.at[here], p_sems, (way,), level, mate)
        stay(picked.at[here], arrived.at[here], count + 1)
    for hop in range(1, depth):
        if more:
            for i in range(count):
                block = fulls[i].at[back(hop, 0), chip, core]
                remote(block, block, up_sems, (i, hop), level, here).wait_recv()
                across(i, hop, block, True)
            continue
        for way in range(2):

            @pl.when(comes(hop, way))
            def _(hop=hop, way=way):
                source = back(hop, way)
                for i in range(count):
                    block = fulls[i].at[source, chip, core]
                    remote(block, block, z_sems[way], (i, hop - 1), level, here).wait_recv()

                    @pl.when(ahead(way))
                    def _():
                        along(i, hop, way, source).start()

                    across(i, hop if way == 0 else depth - hop, block, True)

    for step in range(depth):
        source = (level + depth - step) % depth
        for i in range(count):
            x_spot, y_spot = fulls[i].at[source, x_chip, core], fulls[i].at[source, y_chip, core]
            remote(shards[i], x_spot, x_sems, (i, step), level, here).wait_recv()
            if step % 2 == 0:
                send(x_spot, x_spot, d_sems, (i, step), level, y_next)
            to_twin(i, step, x_chip)
            remote(shards[i], y_spot, y_sems, (i, step), level, here).wait_recv()
            if step % 2 == 1:
                send(y_spot, y_spot, d_sems, (i, step), level, x_next)
            to_twin(i, step, y_chip)
    for step in range(depth):
        source = (level + depth - step) % depth
        for i in range(count):
            spot = fulls[i].at[source, far_chip, core]
            remote(shards[i], spot, d_sems, (i, step), level, here).wait_recv()
            to_twin(i, step, far_chip)
    for step in range(depth):
        source = (level + depth - step) % depth
        for i in range(count):
            for chip_at in range(4):
                spot = fulls[i].at[source, chip_at, 1 - core]
                remote(shards[i], spot, c_sems, (i, step, chip_at), level, here).wait_recv()
    if more:
        for way in range(1, depth):
            spot = parts.at[(level + depth - way) % depth]
            remote(columns(level), spot, w_sems, (way,), level, here).wait_recv()
        for way in range(1, 8):
            spot = arrived.at[(here + 8 - way) % 8]
            remote(picked.at[here], spot, p_sems, (way,), level, here).wait_recv()
    for i in range(count):
        for step in range(depth):
            across(i, step, shards[i], False)
        for hop in () if more else range(depth):
            for way in range(2):

                @pl.when(comes(hop, way) & ahead(way))
                def _(i=i, hop=hop, way=way):
                    along(i, hop, way, back(hop, way)).wait_send()

    for copy in locals_:
        copy.wait()
    for copy in started:
        copy.wait_send()


def gather_plane(shards, ident, wide=None, rows=None, routes=None, length=None):
    depth, count, more = lax.axis_size("dp"), len(shards), wide is not None
    if lax.axis_size("expert") != 8:
        fulls = [lax.all_gather(s, both, axis=0, tiled=True) for s in shards]
        if more:
            fulls.append(lax.all_to_all(wide, "dp", split_axis=1, concat_axis=0, tiled=True))
            picked = matmul(slots_of(routes, length[0], rows.shape[0]), rows).astype(rows.dtype).reshape(slot_shape(rows.shape[0]) + rows.shape[1:])
            fulls.append(lax.all_to_all(picked, "expert", split_axis=0, concat_axis=0, tiled=True))
        return fulls
    extra, extra_out = [], []
    if more:
        picked = jax.ShapeDtypeStruct(slot_shape(rows.shape[0]) + rows.shape[1:], rows.dtype)
        extra = [wide, rows, routes, length]
        extra_out = [
            jax.ShapeDtypeStruct((depth, wide.shape[0], wide.shape[1] // depth), wide.dtype),
            jax.ShapeDtypeStruct(picked.shape, picked.dtype),
        ]
    kinds = []
    for shape in ((count, depth),) * 4 + ((count, depth, 4), (depth,), (8,), (count, depth)):
        kinds += [pltpu.SemaphoreType.DMA(shape)] * 2
    fulls = pl.pallas_call(
        functools.partial(gather_kernel, depth, count, more),
        out_shape=[jax.ShapeDtypeStruct((depth, 4, 2) + s.shape, s.dtype) for s in shards] + extra_out,
        in_specs=[pl.BlockSpec(memory_space=pl.ANY)] * (count + more)
        + [pl.BlockSpec(memory_space=pltpu.VMEM)] * 2 * more
        + [pl.BlockSpec(memory_space=pltpu.SMEM)] * more,
        out_specs=[pl.BlockSpec(memory_space=pl.ANY)] * (count + len(extra_out)),
        scratch_shapes=[pltpu.SemaphoreType.DMA((count + 2,))]
        + kinds
        + ([pltpu.VMEM(picked.shape, picked.dtype)] if more else []),
        compiler_params=pltpu.CompilerParams(collective_id=ident, has_side_effects=True),
        cost_estimate=pl.CostEstimate(flops=1, bytes_accessed=1, transcendentals=0),
        name=f"gather_plane_{ident}",
    )(*shards, *extra)
    full = [f.reshape((-1,) + s.shape[1:]) for f, s in zip(fulls, shards)]
    if more:
        full += [fulls[count].reshape((-1, extra_out[0].shape[2])), fulls[count + 1]]
    return full


def scatter_kernel(depth, count, work, *refs):
    grads, refs = refs[:count], refs[count:]
    if work:
        operands, packed, product, parts = refs[:6], refs[6], refs[7], refs[8]
        buffers, w_sems, keep, staged_sems, staged, refs = refs[-10:], refs[-12:-10], refs[-13], refs[-14], refs[-15], refs[9:-15]
        width = packed.shape[2]
        made_rows = operands[0].shape[0] // depth
        tops = [0]
        for grad in grads:
            tops.append(tops[-1] + grad.shape[3] * grad.shape[4] // width)
    else:
        outs, refs = refs[:count], refs[count:]
    own, twins, first, second = (refs[i * count : (i + 1) * count] for i in range(4))
    n = 4 * count
    load, c_sems, f_sems, s_sems = refs[n], refs[n + 1 : n + 3], refs[n + 3 : n + 5], refs[n + 5 : n + 7]
    level, here = lax.axis_index("dp"), lax.axis_index("expert")
    chip, core, x, y, twin, x_next, y_next = plane()
    greet(depth, (twin, x_next, y_next), work)
    started, loads, flown = [], {}, []

    def send(*a):
        copy = remote(*a)
        copy.start()
        started.append(copy)

    order = [(step, (step + level + 1) % depth) for step in range(depth)]
    for step, at in order:
        for i in range(count):
            send(grads[i].at[at, :, 1 - core], twins[i].at[step], c_sems, (i, step), level, twin)
            loads[i, step] = pltpu.make_async_copy(grads[i].at[at, :, core], own[i].at[step], load.at[i, step])
            loads[i, step].start()

    def part(at):
        wide = parts.shape[1] // depth
        return parts.at[:, pl.ds(pl.multiple_of(at * wide, wide), wide)]

    def hand_out(block, at, way):
        if way:
            send(block, part(level), w_sems, (way,), at, here)
        else:
            copy = pltpu.make_async_copy(block, part(level), keep.at[0])
            copy.start()
            flown.append(copy)

    jobs = expert_work(depth, level, operands, (packed, product), buffers, hand_out) if work else iter(())
    next(jobs, None)

    def add(target, other):
        target[...] = (target[...].astype(jnp.float32) + other[...].astype(jnp.float32)).astype(jnp.bfloat16)

    def chips(step):
        if step % 2 == 0:
            return (1 - x, 3 - x), (x, 2 + x), x_next, y_next
        return (2 - 2 * y, 3 - 2 * y), (2 * y, 2 * y + 1), y_next, x_next

    for step, at in order:
        away, near, first_next, second_next = chips(step)
        for i in range(count):
            loads[i, step].wait()
            remote(own[i].at[step], twins[i].at[step], c_sems, (i, step), level, here).wait_recv()
            for side in range(2):
                add(own[i].at[step, away[side]], twins[i].at[step, away[side]])
                send(own[i].at[step, away[side]], first[i].at[step, side], f_sems, (i, step, side), level, first_next)
        for i in range(count):
            for side in range(2):
                add(own[i].at[step, near[side]], twins[i].at[step, near[side]])
    next(jobs, None)
    for step, at in order:
        away, near, first_next, second_next = chips(step)
        for i in range(count):
            for side in range(2):
                remote(own[i].at[step, 0], first[i].at[step, side], f_sems, (i, step, side), level, here).wait_recv()
                add(own[i].at[step, near[side]], first[i].at[step, side])
            across = chip + 2 - 4 * y if step % 2 == 0 else chip + 1 - 2 * x
            send(own[i].at[step, across], second[i].at[step], s_sems, (i, step), level, second_next)
        if step == 1:
            next(jobs, None)
    for _ in jobs:
        pass
    for step, at in order:
        for i in range(count):
            remote(own[i].at[step, 0], second[i].at[step], s_sems, (i, step), level, here).wait_recv()
            add(second[i].at[step], own[i].at[step, chip])
            sums = second[i][step]
            if work:
                for piece in range(sums.shape[1] // width):
                    place = pl.ds(tops[i] + piece * sums.shape[0], sums.shape[0])
                    staged[step, place] = sums[:, piece * width : (piece + 1) * width]
            else:
                outs[i][at] = sums
        if work:
            copy = pltpu.make_async_copy(staged.at[step], packed.at[at, made_rows:], staged_sems.at[step])
            copy.start()
            flown.append(copy)
    if work:
        for way in range(1, depth):
            spot = part((level + depth - way) % depth)
            remote(spot, spot, w_sems, (way,), level, here).wait_recv()
    for copy in flown:
        copy.wait()
    for copy in started:
        copy.wait_send()


def expert_work(depth, level, operands, results, buffers, hand_out):
    act, pulled, rows_in, pre_grad, down, mix = operands
    act_at, grads_at, rows_at, pre_at, down_at, mix_at, tall, low, eup_at, sems = buffers
    pairs = ((act, act_at), (pulled, grads_at), (down, down_at), (rows_in, rows_at), (pre_grad, pre_at), (mix, mix_at))
    copies = [pltpu.make_async_copy(a, b, sems.at[i]) for i, (a, b) in enumerate(pairs)]
    for i in (3, 4, 0, 1, 5, 2):
        copies[i].start()
    tile = tall.shape[1]
    height = low.shape[1]

    def in_flight(slot, stage, target, sem):
        return pltpu.make_async_copy(stage.at[slot], target, sems.at[sem + slot])

    def tiles(number, stage, sem, compute, target):
        def body(i, carry):
            slot = i % 2

            @pl.when(i >= 2)
            def _():
                in_flight(slot, stage, target(i), sem).wait()

            stage[slot] = compute(i)
            in_flight(slot, stage, target(i), sem).start()
            return carry

        lax.fori_loop(0, number, body, 0)
        for slot in range(2):
            in_flight(slot, stage, target(0), sem).wait()

    def columns(array, i, size):
        return array[:, pl.ds(pl.multiple_of(i * size, size), size)]

    copies[3].wait()
    copies[4].wait()
    own_rows = eup_at.shape[1]
    for step in range(depth):
        at = (level + step) % depth
        eup_at[step] = matmul_tn(columns(rows_at, at, own_rows), pre_at[...]).astype(jnp.bfloat16)
        hand_out(eup_at.at[step], at, step)
    yield
    for i in (0, 1, 5):
        copies[i].wait()
    grads_at[...] = (grads_at[...].astype(jnp.float32) * mix_at[...]).astype(jnp.bfloat16)
    tiles(
        act_at.shape[1] // tile,
        tall,
        6,
        lambda i: matmul_tn(columns(act_at, i, tile), grads_at[...]),
        lambda i: results[1].at[pl.ds(pl.multiple_of(i * tile, tile), tile)],
    )
    yield
    copies[2].wait()
    tiles(
        results[0].shape[0],
        low,
        8,
        lambda i: matmul(act_at[pl.ds(pl.multiple_of(i * height, 16), height), :], down_at[...]).astype(jnp.bfloat16),
        lambda i: results[0].at[i, 0:height],
    )
    yield


def settle_kernel(depth, count, *refs):
    sums, summed, outs, returned = refs[:count], refs[count], refs[count + 1 : 2 * count + 1], refs[2 * count + 1]
    refs = refs[2 * count + 2 :]
    levels, z_sems, p_sems, keep = refs[:count], refs[count : count + 2], refs[count + 2 : count + 4], refs[count + 4]
    level, here = lax.axis_index("dp"), lax.axis_index("expert")
    greet(depth, [(here + way) % 8 for way in range(1, 8)], True)
    capacity = returned.shape[1]
    started = []

    def slots(mate):
        return summed.at[pl.ds(pl.multiple_of(mate * capacity, 16), capacity)]

    for step in range(1, depth):
        target = (level + step) % depth
        for i in range(count):
            started.append(remote(sums[i].at[target], levels[i].at[step - 1], z_sems, (i, step), target, here))
            started[-1].start()
    for way in range(1, 8):
        mate = (here + way) % 8
        started.append(remote(slots(mate), returned.at[here], p_sems, (way,), level, mate))
        started[-1].start()
    kept = pltpu.make_async_copy(slots(here), returned.at[here], keep.at[0])
    kept.start()
    for i in range(count):
        total = sums[i][level].astype(jnp.float32)
        for step in range(1, depth):
            remote(levels[i].at[step - 1], levels[i].at[step - 1], z_sems, (i, step), level, here).wait_recv()
            total = total + levels[i][step - 1].astype(jnp.float32)
        outs[i][...] = total
    for way in range(1, 8):
        spot = returned.at[(here + 8 - way) % 8]
        remote(spot, spot, p_sems, (way,), level, here).wait_recv()
    kept.wait()
    for copy in started:
        copy.wait_send()


def settle(sums, summed, tok_rows, ident):
    depth, count = lax.axis_size("dp"), len(sums)
    if lax.axis_size("expert") != 8:
        summed = summed.reshape(slot_shape(tok_rows) + summed.shape[1:])
        return [*sums, lax.all_to_all(summed, "expert", split_axis=0, concat_axis=0, tiled=True)]
    blocks = [s.shape[1:] for s in sums]
    vmem, whole = pl.BlockSpec(memory_space=pltpu.VMEM), pl.BlockSpec(memory_space=pl.ANY)
    return pl.pallas_call(
        functools.partial(settle_kernel, depth, count),
        out_shape=[jax.ShapeDtypeStruct(b, jnp.float32) for b in blocks]
        + [jax.ShapeDtypeStruct(slot_shape(tok_rows) + summed.shape[1:], summed.dtype)],
        in_specs=[vmem] * count + [whole],
        out_specs=[vmem] * count + [whole],
        scratch_shapes=[pltpu.VMEM((depth - 1,) + b, jnp.bfloat16) for b in blocks]
        + [pltpu.SemaphoreType.DMA((count, depth))] * 2
        + [pltpu.SemaphoreType.DMA((8,))] * 2
        + [pltpu.SemaphoreType.DMA((1,))],
        compiler_params=pltpu.CompilerParams(collective_id=ident, has_side_effects=True),
        cost_estimate=pl.CostEstimate(flops=1, bytes_accessed=1, transcendentals=0),
        name="settle",
    )(*sums, summed)


def scatter_plane(grads, ident, work=None):
    depth, count = lax.axis_size("dp"), len(grads)
    low = jnp.bfloat16
    if lax.axis_size("expert") != 8:
        sums = [lax.psum_scatter(g, both, scatter_dimension=0, tiled=True).astype(jnp.float32) for g in grads]
        if work is not None:
            act, pulled, rows_in, pre_grad, down, mix = work
            grad_rows = (pulled.astype(jnp.float32) * mix).astype(low)
            sums.append(matmul(act, down).astype(low))
            sums.append(matmul_tn(act, grad_rows))
            tall = matmul_tn(rows_in, pre_grad).astype(low)
            sums.append(lax.all_to_all(tall, "dp", split_axis=0, concat_axis=1, tiled=True))
        return sums
    grads = [g.reshape((depth, 4, 2, g.shape[0] // (8 * depth)) + g.shape[1:]) for g in grads]
    blocks = [g.shape[3:] for g in grads]
    width = min(b[1] for b in blocks)
    scratch = [pltpu.VMEM((depth, 4) + b, low) for b in blocks] * 2
    scratch += [pltpu.VMEM((depth, 2) + b, low) for b in blocks]
    scratch += [pltpu.VMEM((depth,) + b, low) for b in blocks]
    scratch += [pltpu.SemaphoreType.DMA((count, depth))] * 3 + [pltpu.SemaphoreType.DMA((count, depth, 2))] * 2
    scratch += [pltpu.SemaphoreType.DMA((count, depth))] * 2
    if work is None:
        operands = ()
        made = [jax.ShapeDtypeStruct((depth,) + b, low) for b in blocks]
    else:
        operands = tuple(work)
        act, rows_in, pre_grad, down = work[0], work[2], work[3], work[4]
        packed_rows, made_rows = sum(b[0] * b[1] for b in blocks) // width, act.shape[0] // depth
        own_rows = rows_in.shape[1] // depth
        made = [
            jax.ShapeDtypeStruct((depth, made_rows + packed_rows, width), low),
            jax.ShapeDtypeStruct((act.shape[1], act.shape[1]), jnp.float32),
            jax.ShapeDtypeStruct((own_rows, pre_grad.shape[1] * depth), low),
        ]
        scratch += [pltpu.VMEM((depth, packed_rows, width), low), pltpu.SemaphoreType.DMA((depth,))]
        scratch += [pltpu.SemaphoreType.DMA((1,))] + [pltpu.SemaphoreType.DMA((depth,))] * 2
        scratch += [pltpu.VMEM(work[i].shape, work[i].dtype) for i in range(6)]
        scratch += [
            pltpu.VMEM((2, 256, down.shape[1]), jnp.float32),
            pltpu.VMEM((2, made_rows, down.shape[1]), low),
            pltpu.VMEM((depth, own_rows, pre_grad.shape[1]), low),
            pltpu.SemaphoreType.DMA((10,)),
        ]
    out_space = pltpu.VMEM if work is None else pl.ANY
    return list(
        pl.pallas_call(
            functools.partial(scatter_kernel, depth, count, work is not None),
            out_shape=made,
            in_specs=[pl.BlockSpec(memory_space=pl.ANY)] * (count + len(operands)),
            out_specs=[pl.BlockSpec(memory_space=out_space)] * len(made),
            scratch_shapes=scratch,
            compiler_params=pltpu.CompilerParams(
                collective_id=ident, has_side_effects=True, vmem_limit_bytes=58 * 2**20
            ),
            cost_estimate=pl.CostEstimate(flops=1, bytes_accessed=200 * 2**20, transcendentals=0),
            name=f"scatter_plane_{ident}",
        )(*grads, *operands)
    )


def finish_scatter(packed, top, shapes):
    packed = lax.psum_scatter(packed, "dp", scatter_dimension=0)
    width = packed.shape[1]
    outs = [packed]
    for rows, columns in shapes:
        pieces = columns // width
        blocks = [packed[top + i * rows : top + (i + 1) * rows].astype(jnp.float32) for i in range(pieces)]
        outs.append(jnp.concatenate(blocks, axis=1))
        top += pieces * rows
    return outs


def body(
    tokens,
    seq_lengths,
    routes,
    w_qkv,
    w_out,
    w_up,
    w_down,
    gain_attn,
    gain_mlp,
    w_mix,
    expert_up,
    expert_down,
    cotangent,
):
    tok_rows, model_width = tokens.shape
    axis_dp, axis_experts = lax.axis_size("dp"), lax.axis_size("expert")
    expert_total = axis_experts * expert_up.shape[0]
    capacity = max(2, 5 * tok_rows // (4 * expert_total))
    slots = expert_total * capacity
    ff_expert = expert_up.shape[2]

    small = jnp.concatenate([gain_attn[:, None], gain_mlp[:, None], w_mix], axis=1)
    small = jnp.pad(small, ((0, 0), (0, 128 - small.shape[1])))
    length = seq_lengths[0]
    valid_rows = jnp.arange(tok_rows, dtype=jnp.int32) < length

    def pick(rows):
        return matmul(slot_table, rows).astype(jnp.bfloat16).reshape(expert_total, capacity, model_width)

    def dispatch(rows):
        arrived = lax.all_to_all(pick(rows), "expert", split_axis=0, concat_axis=0, tiled=True)
        return arrived.reshape(slots, model_width)

    def spread(rows):
        return lax.all_gather(rows, "dp", axis=0, tiled=True)

    def unspread(rows):
        return lax.psum_scatter(rows, "dp", scatter_dimension=0, tiled=True)

    def give_back(summed):
        summed = summed.reshape(expert_total, capacity, model_width)
        back = lax.all_to_all(summed, "expert", split_axis=0, concat_axis=0, tiled=True)
        return matmul_tn(slot_table, back.reshape(slots, model_width))

    down_part = expert_down[0]

    upstream_low = jnp.where(valid_rows[:, None], cotangent, jnp.zeros_like(cotangent))
    upstream = upstream_low.astype(jnp.float32)
    route_row = routes.reshape((1, tok_rows))
    qkv_full, out_full, small_full, up_part, pulled_here = gather_plane(
        [w_qkv, w_out, small], 0, expert_up[0], cotangent, route_row, seq_lengths
    )
    slot_table = slots_of(lax.optimization_barrier((route_row, qkv_full))[0], length, tok_rows)
    pulled_rows = spread(pulled_here.reshape(slots, model_width))
    gain_one = small_full[:, 0].astype(jnp.float32)
    gain_two = small_full[:, 1].astype(jnp.float32)
    mix_full = small_full[:, 2:4]
    mix_lean = (mix_full[:, 0] - mix_full[:, 1].astype(jnp.float32)).astype(jnp.float32)

    inputs = tokens.astype(jnp.float32)
    scaled_one, inverse_one = norm_forward(inputs)
    normed_one = (scaled_one * gain_one).astype(jnp.bfloat16)
    joined = matmul(normed_one, qkv_full).astype(jnp.bfloat16)
    heads_out, log_total = attention_forward(joined, seq_lengths)
    after_attn = inputs + matmul(heads_out, out_full)
    scaled_two, inverse_two = norm_forward(after_attn)
    normed_two = (scaled_two * gain_two).astype(jnp.bfloat16)

    rows_here = dispatch(normed_two)
    rows_here, w_up, w_down = lax.optimization_barrier((rows_here, w_up, w_down))
    rows_in = spread(rows_here)
    up_full, down_full = gather_plane([w_up, w_down], 1)

    pulled_rows, up_full, down_full = lax.optimization_barrier((pulled_rows, up_full, down_full))
    mix_weights = jax.nn.softmax(matmul(normed_two, mix_full), axis=-1)
    grad_down, grad_up, normed_grad, dense_out, pull_dense = dense_branch(
        normed_two, up_full, down_full, upstream_low, mix_weights[:, 0:1]
    )
    lean_dense = mix_weights[:, 0:1] * mix_weights[:, 1:2] * pull_dense
    normed_grad = normed_grad + lean_dense * mix_lean[None, :]

    act_pull = matmul_nt(pulled_rows, down_part)
    rows_in, act_pull, grad_up, grad_down, normed_grad = lax.optimization_barrier(
        (rows_in, act_pull, grad_up, grad_down, normed_grad)
    )
    act_rows, pre_grad, row_mix, input_grad, lean_rows = expert_branch(
        rows_in, act_pull, up_part, small_full, mix_lean[None, :]
    )
    in_grad_here = unspread(input_grad)
    *sums, grad_expert_down, grad_expert_up = scatter_plane(
        [grad_up, grad_down], 2, (act_rows, pulled_rows, rows_in, pre_grad, down_part, row_mix)
    )
    grad_expert_down = grad_expert_down[None]
    in_grad_here, *sums = lax.optimization_barrier((in_grad_here, *sums))
    if len(sums) == 1:
        outs_here, grad_up, grad_down = finish_scatter(sums[0], slots, (w_up.shape, w_down.shape))
    else:
        grad_up, grad_down, outs_here = sums[0], sums[1], unspread(sums[2])
    in_grad_back = give_back(in_grad_here)

    normed_grad = normed_grad + in_grad_back
    lean_grad = jnp.sum(normed_two.astype(jnp.float32) * lean_dense, axis=0) - lean_rows[0]
    mlp_in_grad, grad_gain_two = norm_backward(normed_grad, scaled_two, inverse_two, gain_two)
    resid_grad = upstream + mlp_in_grad
    attn_grad = resid_grad.astype(jnp.bfloat16)
    grad_out = matmul_tn(heads_out, attn_grad)
    heads_grad = matmul_nt(attn_grad, out_full).astype(jnp.bfloat16)
    joined_grad = jnp.concatenate(
        attention_backward(joined, heads_grad, heads_out, log_total, seq_lengths), axis=1
    )
    grad_qkv = matmul_tn(normed_one, joined_grad)
    normed_one_grad = matmul_nt(joined_grad, qkv_full)
    attn_in_grad, grad_gain_one = norm_backward(normed_one_grad, scaled_one, inverse_one, gain_one)
    grad_inputs = resid_grad + attn_in_grad

    small_grads = jnp.stack([grad_gain_one, grad_gain_two, lean_grad, -lean_grad], axis=1)
    small_grads = jnp.pad(small_grads, ((0, 0), (0, 128 - small_grads.shape[1])))
    grad_expert_down = jnp.where(length >= 0, grad_expert_down, 0.0)
    grad_expert_up = grad_expert_up.astype(jnp.float32)[None]
    small_grads, grad_expert_down, grad_expert_up = lax.optimization_barrier(
        (small_grads.astype(jnp.bfloat16), grad_expert_down, grad_expert_up)
    )
    sums = scatter_plane([grad_qkv.astype(jnp.bfloat16), grad_out.astype(jnp.bfloat16), small_grads], 3)
    grad_qkv, grad_out, small_grads, returned = settle(sums, outs_here, tok_rows, 4)
    expert_out = matmul_tn(slot_table, returned.reshape(slots, model_width))
    result = after_attn + mix_weights[:, 0:1] * dense_out + mix_weights[:, 1:2] * expert_out
    return (
        result,
        grad_inputs,
        grad_qkv,
        grad_out,
        grad_up,
        grad_down,
        small_grads[:, 0],
        small_grads[:, 1],
        small_grads[:, 2:4],
        grad_expert_up,
        grad_expert_down,
    )


def solution(mesh):
    rows, vector = P(both, None), P(both)
    experts = P("expert", "dp", None)
    return jax.shard_map(
        body,
        mesh=mesh,
        in_specs=(rows, vector, rows, rows, rows, rows, rows, vector, vector, rows, experts, experts, rows),
        out_specs=(rows, rows, rows, rows, rows, rows, vector, vector, rows, experts, experts),
        check_vma=False,
    )
```

```python
import functools

import jax
import jax.numpy as jnp
from jax import lax
from jax.experimental import pallas as pl
from jax.experimental.pallas import tpu as pltpu
from jax.sharding import PartitionSpec as P

HEADS = 16

epsilon = 1e-05
root_half = 0.7071067811865476
inv_root_two_pi = 0.3989422804014327
highest = lax.Precision.HIGHEST
both = ("dp", "expert")


def gelu_pair(values):
    half = 0.5 * (1.0 + lax.erf(values * root_half))
    return values * half, half + values * jnp.exp(-0.5 * values * values) * inv_root_two_pi


def dot(left, right, dims):
    return lax.dot_general(left, right, (dims, ((), ())), preferred_element_type=jnp.float32)


def matmul(left, right):
    return dot(left, right, ((1,), (0,)))


def matmul_nt(left, right):
    return dot(left, right, ((1,), (1,)))


def matmul_tn(left, right):
    return dot(left, right, ((0,), (0,)))


def norm_forward(values):
    row_mean = jnp.mean(values, axis=-1, keepdims=True)
    centred = values - row_mean
    row_var = jnp.mean(centred * centred, axis=-1, keepdims=True)
    inverse = lax.rsqrt(row_var + epsilon)
    return (centred * inverse, inverse)


def norm_backward(upstream, scaled, inverse, gain_row):
    gain_grad = jnp.sum(upstream * scaled, axis=0)
    inner = upstream * gain_row
    centred_grad = (
        inner
        - jnp.mean(inner, axis=-1, keepdims=True)
        - scaled * jnp.mean(inner * scaled, axis=-1, keepdims=True)
    )
    return (inverse * centred_grad, gain_grad)


def head_scores(queries, keys_all, length, row_start, scale):
    scores = matmul_nt(queries, keys_all) * scale
    rows_at = row_start + lax.broadcasted_iota(jnp.int32, scores.shape, 0)
    cols_at = lax.broadcasted_iota(jnp.int32, scores.shape, 1)
    return jnp.where((cols_at <= rows_at) & (cols_at < length), scores, -1000000000.0)


def attention_forward_kernel(head_width, bands, length_ref, q_ref, k_ref, v_ref, out_ref, log_ref):
    length = length_ref[0]
    scale = head_width ** (-0.5)
    tok_rows, lanes = q_ref.shape
    height = tok_rows // bands
    lane = lax.broadcasted_iota(jnp.int32, (1, lanes), 1) // head_width
    for band in range(bands):
        top, end = band * height, (band + 1) * height
        keys_all, values_all = k_ref[0:end, :], v_ref[0:end, :]
        queries = q_ref[top:end, :]
        mixed = jnp.zeros((height, lanes), jnp.float32)
        logs = []
        for head in range(lanes // head_width):
            mine = lane == head
            scores = head_scores(jnp.where(mine, queries, 0), keys_all, length, top, scale)
            top_score = jnp.max(scores, axis=-1, keepdims=True)
            raised = jnp.exp(scores - top_score)
            row_total = jnp.sum(raised, axis=-1, keepdims=True)
            probs = (raised / row_total).astype(jnp.bfloat16)
            mixed = mixed + matmul(probs, jnp.where(mine, values_all, 0))
            logs.append(top_score + jnp.log(row_total))
        out_ref[top:end, :] = mixed.astype(jnp.bfloat16)
        spread = jnp.broadcast_to(logs[0], (height, lanes))
        for head in range(1, len(logs)):
            spread = jnp.where(lane == head, logs[head], spread)
        log_ref[top:end, :] = spread


def attention_forward(joined, length):
    tok_rows, width = joined.shape[0], joined.shape[1] // 3
    head_width = width // HEADS
    lanes = max(128, head_width)
    tiles = width // lanes
    bands = 2

    def part(which):
        return pl.BlockSpec((tok_rows, lanes), lambda i: (0, which * tiles + i))

    return pl.pallas_call(
        functools.partial(attention_forward_kernel, head_width, bands),
        grid=(tiles,),
        out_shape=[
            jax.ShapeDtypeStruct((tok_rows, width), jnp.bfloat16),
            jax.ShapeDtypeStruct((tok_rows, width), jnp.float32),
        ],
        in_specs=[pl.BlockSpec(memory_space=pltpu.SMEM), part(0), part(1), part(2)],
        out_specs=[part(0), part(0)],
        compiler_params=pltpu.CompilerParams(vmem_limit_bytes=32 * 2**20),
        cost_estimate=pl.CostEstimate(flops=4 * tok_rows * tok_rows * width, bytes_accessed=10 * tok_rows * width, transcendentals=0),
        name="attention_forward",
    )(length, joined, joined, joined)


def attention_backward_kernel(head_width, bands, length_ref, q_ref, k_ref, v_ref, g_ref, o_ref, log_ref, dq_ref, dk_ref, dv_ref, dk_sum, dv_sum):
    length = length_ref[0]
    scale = head_width ** (-0.5)
    tok_rows, lanes = q_ref.shape
    height = tok_rows // bands
    lane = lax.broadcasted_iota(jnp.int32, (1, lanes), 1) // head_width
    for band in range(bands):
        top, end = band * height, (band + 1) * height
        keys_all, values_all = k_ref[0:end, :], v_ref[0:end, :]
        queries, grads = q_ref[top:end, :], g_ref[top:end, :]
        turned = lax.transpose(log_ref[top:end, :], (1, 0))
        products = lax.transpose(grads.astype(jnp.float32) * o_ref[top:end, :].astype(jnp.float32), (1, 0))
        dq = jnp.zeros((height, lanes), jnp.float32)
        dk = jnp.zeros((end, lanes), jnp.float32)
        dv = jnp.zeros((end, lanes), jnp.float32)
        keys_at = lax.broadcasted_iota(jnp.int32, (end, height), 0)
        rows_at = top + lax.broadcasted_iota(jnp.int32, (end, height), 1)
        allowed = (keys_at <= rows_at) & (keys_at < length)
        for head in range(lanes // head_width):
            mine = lane == head
            own_q, own_g = jnp.where(mine, queries, 0), jnp.where(mine, grads, 0)
            log_total = turned[head * head_width : head * head_width + 1, :]
            delta = jnp.sum(products[head * head_width : (head + 1) * head_width, :], axis=0, keepdims=True)
            scores = jnp.where(allowed, matmul_nt(keys_all, own_q) * scale, -1000000000.0)
            probs = jnp.exp(scores - log_total)
            prob_grad = matmul_nt(values_all, own_g)
            score_grad = (probs * (prob_grad - delta)).astype(jnp.bfloat16)
            dv = dv + matmul(probs.astype(jnp.bfloat16), own_g)
            dk = dk + matmul(score_grad, own_q)
            dq = dq + matmul_tn(score_grad, jnp.where(mine, keys_all, 0))
        dq_ref[top:end, :] = (dq * scale).astype(jnp.bfloat16)
        if band == 0:
            dk_sum[...] = jnp.zeros_like(dk_sum)
            dv_sum[...] = jnp.zeros_like(dv_sum)
        dk_sum[0:end, :] += dk
        dv_sum[0:end, :] += dv
    dk_ref[...] = (dk_sum[...] * scale).astype(jnp.bfloat16)
    dv_ref[...] = dv_sum[...].astype(jnp.bfloat16)


def attention_backward(joined, heads_grad, heads_out, log_total, length):
    tok_rows, width = joined.shape[0], joined.shape[1] // 3
    head_width = width // HEADS
    lanes = max(128, head_width)
    tiles = width // lanes
    bands = 2

    def part(which):
        return pl.BlockSpec((tok_rows, lanes), lambda i: (0, which * tiles + i))

    return pl.pallas_call(
        functools.partial(attention_backward_kernel, head_width, bands),
        grid=(tiles,),
        out_shape=[jax.ShapeDtypeStruct((tok_rows, width), jnp.bfloat16)] * 3,
        in_specs=[pl.BlockSpec(memory_space=pltpu.SMEM), part(0), part(1), part(2), part(0), part(0), part(0)],
        out_specs=[part(0)] * 3,
        scratch_shapes=[pltpu.VMEM((tok_rows, lanes), jnp.float32)] * 2,
        compiler_params=pltpu.CompilerParams(vmem_limit_bytes=32 * 2**20),
        cost_estimate=pl.CostEstimate(flops=10 * tok_rows * tok_rows * width, bytes_accessed=20 * tok_rows * width, transcendentals=0),
        name="attention_backward",
    )(length, joined, joined, joined, heads_grad, heads_out, log_total)


def expert_kernel(tile, rows_ref, pull_ref, up_ref, small_ref, lean_ref, act_ref, pre_ref, mix_ref, in_ref, sum_ref):
    low = jnp.bfloat16
    rows_in = rows_ref[...]
    logits = matmul(rows_in, small_ref[...])
    first, second = logits[:, 2:3], logits[:, 3:4]
    top = jnp.maximum(first, second)
    first, second = jnp.exp(first - top), jnp.exp(second - top)
    mix_dense, mix_expert = first / (first + second), second / (first + second)
    mix_ref[...] = mix_expert
    tiles = [slice(left, left + tile) for left in range(0, up_ref.shape[1], tile)]
    pull = jnp.zeros_like(mix_expert)
    total = None
    coming = matmul(rows_in, up_ref[:, tiles[0]])
    for i, columns in enumerate(tiles):
        pre_act = coming
        if i + 1 < len(tiles):
            coming = matmul(rows_in, up_ref[:, tiles[i + 1]])
        act_pull = pull_ref[:, columns]
        gelu, slope = gelu_pair(pre_act)
        act = gelu.astype(low)
        act_ref[:, columns] = act
        pull = pull + jnp.sum(act.astype(jnp.float32) * act_pull, axis=1, keepdims=True)
        pre_grad = (mix_expert * act_pull * slope).astype(low)
        pre_ref[:, columns] = pre_grad
        part = matmul_nt(pre_grad, up_ref[:, columns])
        total = part if total is None else total + part
    lean = mix_dense * mix_expert * pull
    in_ref[...] = (total - lean * lean_ref[...]).astype(low)
    part = jnp.sum(rows_in.astype(jnp.float32) * lean, axis=0, keepdims=True)
    sum_ref[...] = jnp.where(pl.program_id(0) == 0, part, sum_ref[...] + part)


def expert_branch(rows_in, act_pull, up_part, small_full, mix_lean):
    count, width = rows_in.shape
    hidden = up_part.shape[1]
    height = 512

    def tall(columns):
        return pl.BlockSpec((height, columns), lambda i: (i, 0))

    def whole(array):
        return pl.BlockSpec(array.shape, lambda i: (0, 0))

    low = jnp.bfloat16
    return pl.pallas_call(
        functools.partial(expert_kernel, 256),
        grid=(count // height,),
        out_shape=[
            jax.ShapeDtypeStruct((count, hidden), low),
            jax.ShapeDtypeStruct((count, hidden), low),
            jax.ShapeDtypeStruct((count, 1), jnp.float32),
            jax.ShapeDtypeStruct((count, width), low),
            jax.ShapeDtypeStruct((1, width), jnp.float32),
        ],
        in_specs=[tall(width), tall(hidden), whole(up_part), whole(small_full), whole(mix_lean)],
        out_specs=[tall(hidden), tall(hidden), tall(1), tall(width), whole(mix_lean)],
        compiler_params=pltpu.CompilerParams(vmem_limit_bytes=58 * 2**20),
        cost_estimate=pl.CostEstimate(
            flops=4 * count * width * hidden, bytes_accessed=16 * count * width, transcendentals=0
        ),
        name="expert_branch",
    )(rows_in, act_pull, up_part, small_full, mix_lean)


def dense_kernel(normed_ref, up_ref, down_ref, grad_ref, mix_ref, gdown_ref, gup_ref, ngrad_ref, out_ref, pull_ref):
    normed, upstream, mix = normed_ref[...], grad_ref[...], mix_ref[...]
    hidden = matmul(normed, up_ref[...])
    dense_pull = matmul_nt(upstream, down_ref[...])
    gelu, slope = gelu_pair(hidden)
    act = gelu.astype(jnp.bfloat16)
    pull = jnp.sum(act.astype(jnp.float32) * dense_pull, axis=1, keepdims=True)
    hidden_grad = (mix * dense_pull * slope).astype(jnp.bfloat16)
    grad_out = (upstream.astype(jnp.float32) * mix).astype(jnp.bfloat16)
    gdown_ref[...] = matmul_tn(act, grad_out).astype(jnp.bfloat16)
    gup_ref[...] = matmul_tn(normed, hidden_grad).astype(jnp.bfloat16)
    ngrad = matmul_nt(hidden_grad, up_ref[...])
    dense_out = matmul(act, down_ref[...])

    @pl.when(pl.program_id(0) == 0)
    def _():
        ngrad_ref[...] = ngrad
        out_ref[...] = dense_out
        pull_ref[...] = pull

    @pl.when(pl.program_id(0) > 0)
    def _():
        ngrad_ref[...] += ngrad
        out_ref[...] += dense_out
        pull_ref[...] += pull


def dense_branch(normed_two, up_full, down_full, upstream_low, mix):
    rows, width = normed_two.shape
    ff = up_full.shape[1]
    block = 512

    def whole(columns):
        return pl.BlockSpec((rows, columns), lambda i: (0, 0))

    across, down = pl.BlockSpec((width, block), lambda i: (0, i)), pl.BlockSpec((block, width), lambda i: (i, 0))
    return pl.pallas_call(
        dense_kernel,
        grid=(ff // block,),
        out_shape=[
            jax.ShapeDtypeStruct((ff, width), jnp.bfloat16),
            jax.ShapeDtypeStruct((width, ff), jnp.bfloat16),
            jax.ShapeDtypeStruct((rows, width), jnp.float32),
            jax.ShapeDtypeStruct((rows, width), jnp.float32),
            jax.ShapeDtypeStruct((rows, 1), jnp.float32),
        ],
        in_specs=[whole(width), across, down, whole(width), whole(1)],
        out_specs=[down, across, whole(width), whole(width), whole(1)],
        compiler_params=pltpu.CompilerParams(vmem_limit_bytes=48 * 2**20),
        cost_estimate=pl.CostEstimate(flops=12 * rows * width * ff, bytes_accessed=8 * width * ff, transcendentals=0),
        name="dense_branch",
    )(normed_two, up_full, down_full, upstream_low, mix)


MESH = pl.DeviceIdType.MESH


def plane():
    here = lax.axis_index("expert")
    core, x, y = here % 2, (here // 2) % 2, here // 4
    return here // 2, core, x, y, here + 1 - 2 * core, here + 2 - 4 * x, here + 4 - 8 * y


def greet(depth, others, count):
    level = lax.axis_index("dp")
    barrier = pltpu.get_barrier_semaphore()
    for other in others:
        pl.semaphore_signal(barrier, inc=1, device_id=(level, other), device_id_type=MESH)
    if count:
        for step in range(1, depth):
            pl.semaphore_signal(
                barrier,
                inc=1,
                device_id=((level + step) % depth, lax.axis_index("expert")),
                device_id_type=MESH,
            )
    pl.semaphore_wait(barrier, len(others) + (depth - 1 if count else 0))


def remote(source, target, sems, slot, level, where):
    return pltpu.make_async_remote_copy(
        src_ref=source,
        dst_ref=target,
        send_sem=sems[0].at[slot],
        recv_sem=sems[1].at[slot],
        device_id=(level, where),
        device_id_type=MESH,
    )


def slot_shape(tok_rows):
    experts = lax.axis_size("expert")
    return (experts, max(2, 5 * tok_rows // (4 * experts)))


def slots_of(routes, length, tok_rows):
    experts, capacity = slot_shape(tok_rows)
    rows_at = lax.broadcasted_iota(jnp.int32, (1, tok_rows), 1)
    hits = (routes == lax.broadcasted_iota(jnp.int32, (experts, tok_rows), 0)) & (rows_at < length)
    hits = hits.astype(jnp.float32)
    earlier = lax.broadcasted_iota(jnp.int32, (tok_rows, tok_rows), 0) < lax.broadcasted_iota(jnp.int32, (tok_rows, tok_rows), 1)
    ranks = matmul(hits.astype(jnp.bfloat16), earlier.astype(jnp.bfloat16))
    rank = jnp.sum(hits * ranks, axis=0, keepdims=True)
    kept = (rows_at < length) & (rank < capacity)
    slot = routes * capacity + rank.astype(jnp.int32)
    slots_at = lax.broadcasted_iota(jnp.int32, (experts * capacity, tok_rows), 0)
    return ((slots_at == slot) & kept).astype(jnp.bfloat16)


def pick_rows(rows, routes, length, picked):
    experts, capacity, _ = picked.shape
    table = slots_of(routes[...], length[0], rows.shape[0])
    chosen = matmul(table, rows[...]).astype(jnp.bfloat16)
    for expert in range(experts):
        picked[expert] = chosen[expert * capacity : (expert + 1) * capacity]


def gather_kernel(depth, count, more, *refs):
    shards, refs = refs[:count], refs[count:]
    if more:
        wide, rows, routes, length, refs = refs[0], refs[1], refs[2], refs[3], refs[4:]
    fulls, refs = refs[:count], refs[count:]
    if more:
        parts, arrived, picked, refs = refs[0], refs[1], refs[-1], refs[2:-1]
    keep, sems = refs[0], refs[1:]
    up_sems, x_sems, y_sems, d_sems, c_sems, w_sems, p_sems, low_sems = (sems[2 * i : 2 * i + 2] for i in range(8))
    z_sems = (up_sems, low_sems)
    level, here = lax.axis_index("dp"), lax.axis_index("expert")
    chip, core, x, y, twin, x_next, y_next = plane()
    x_chip, y_chip, far_chip = chip + 1 - 2 * x, chip + 2 - 4 * y, 3 - chip
    mates = [(here + step) % 8 for step in range(1, 8)] if more else (twin, x_next, y_next)
    greet(depth, mates, True)
    started, locals_ = [], []

    def send(*a):
        copy = remote(*a)
        copy.start()
        started.append(copy)

    def stay(source, target, slot):
        copy = pltpu.make_async_copy(source, target, keep.at[slot])
        copy.start()
        locals_.append(copy)

    def to_twin(i, step, chip_at, source=None):
        spot = fulls[i].at[(level + depth - step) % depth, chip_at, core]
        send(spot if source is None else source, spot, c_sems, (i, step, chip_at), level, twin)

    def along(i, hop, way, source):
        block = fulls[i].at[source, chip, core]
        target = (level + (1 if way == 0 else depth - 1)) % depth
        return remote(shards[i] if hop == 0 else block, block, z_sems[way], (i, hop), target, here)

    def ahead(way):
        return level < depth - 1 if way == 0 else level > 0

    def comes(hop, way):
        return level >= hop if way == 0 else level < depth - hop

    def back(hop, way):
        return (level + depth - hop) % depth if way == 0 else (level + hop) % depth

    def across(i, step, origin, begin):
        block = fulls[i].at[(level + depth - step) % depth, chip, core]
        copies = (
            remote(origin, block, x_sems, (i, step), level, x_next),
            remote(origin, block, y_sems, (i, step), level, y_next),
            remote(origin, block, c_sems, (i, step, chip), level, twin),
        )
        for copy in copies:
            if begin:
                copy.start()
            else:
                copy.wait_send()

    if more:
        for step in range(1, depth):
            for i in range(count):
                target = (level + step) % depth
                send(shards[i], fulls[i].at[level, chip, core], up_sems, (i, step), target, here)
    else:
        for way in range(2):

            @pl.when(ahead(way))
            def _(way=way):
                for i in range(count):
                    along(i, 0, way, level).start()

    for i in range(count):
        stay(shards[i], fulls[i].at[level, chip, core], i)
        across(i, 0, shards[i], True)
    if more:
        width = wide.shape[1] // depth

        def columns(at):
            return wide.at[:, pl.ds(pl.multiple_of(at * width, width), width)]

        for way in range(1, depth):
            target = (level + way) % depth
            send(columns(target), parts.at[level], w_sems, (way,), target, here)
        stay(columns(level), parts.at[level], count)
        pick_rows(rows, routes, length, picked)
        for way in range(1, 8):
            mate = (here + way) % 8
            send(picked.at[mate], arrived.at[here], p_sems, (way,), level, mate)
        stay(picked.at[here], arrived.at[here], count + 1)
    for hop in range(1, depth):
        if more:
            for i in range(count):
                block = fulls[i].at[back(hop, 0), chip, core]
                remote(block, block, up_sems, (i, hop), level, here).wait_recv()
                across(i, hop, block, True)
            continue
        for way in range(2):

            @pl.when(comes(hop, way))
            def _(hop=hop, way=way):
                source = back(hop, way)
                for i in range(count):
                    block = fulls[i].at[source, chip, core]
                    remote(block, block, z_sems[way], (i, hop - 1), level, here).wait_recv()

                    @pl.when(ahead(way))
                    def _():
                        along(i, hop, way, source).start()

                    across(i, hop if way == 0 else depth - hop, block, True)

    for step in range(depth):
        source = (level + depth - step) % depth
        for i in range(count):
            x_spot, y_spot = fulls[i].at[source, x_chip, core], fulls[i].at[source, y_chip, core]
            remote(shards[i], x_spot, x_sems, (i, step), level, here).wait_recv()
            if step % 2 == 0:
                send(x_spot, x_spot, d_sems, (i, step), level, y_next)
            to_twin(i, step, x_chip)
            remote(shards[i], y_spot, y_sems, (i, step), level, here).wait_recv()
            if step % 2 == 1:
                send(y_spot, y_spot, d_sems, (i, step), level, x_next)
            to_twin(i, step, y_chip)
    for step in range(depth):
        source = (level + depth - step) % depth
        for i in range(count):
            spot = fulls[i].at[source, far_chip, core]
            remote(shards[i], spot, d_sems, (i, step), level, here).wait_recv()
            to_twin(i, step, far_chip)
    for step in range(depth):
        source = (level + depth - step) % depth
        for i in range(count):
            for chip_at in range(4):
                spot = fulls[i].at[source, chip_at, 1 - core]
                remote(shards[i], spot, c_sems, (i, step, chip_at), level, here).wait_recv()
    if more:
        for way in range(1, depth):
            spot = parts.at[(level + depth - way) % depth]
            remote(columns(level), spot, w_sems, (way,), level, here).wait_recv()
        for way in range(1, 8):
            spot = arrived.at[(here + 8 - way) % 8]
            remote(picked.at[here], spot, p_sems, (way,), level, here).wait_recv()
    for i in range(count):
        for step in range(depth):
            across(i, step, shards[i], False)
        for hop in () if more else range(depth):
            for way in range(2):

                @pl.when(comes(hop, way) & ahead(way))
                def _(i=i, hop=hop, way=way):
                    along(i, hop, way, back(hop, way)).wait_send()

    for copy in locals_:
        copy.wait()
    for copy in started:
        copy.wait_send()


def gather_plane(shards, ident, wide=None, rows=None, routes=None, length=None):
    depth, count, more = lax.axis_size("dp"), len(shards), wide is not None
    if lax.axis_size("expert") != 8:
        fulls = [lax.all_gather(s, both, axis=0, tiled=True) for s in shards]
        if more:
            fulls.append(lax.all_to_all(wide, "dp", split_axis=1, concat_axis=0, tiled=True))
            picked = matmul(slots_of(routes, length[0], rows.shape[0]), rows).astype(rows.dtype).reshape(slot_shape(rows.shape[0]) + rows.shape[1:])
            fulls.append(lax.all_to_all(picked, "expert", split_axis=0, concat_axis=0, tiled=True))
        return fulls
    extra, extra_out = [], []
    if more:
        picked = jax.ShapeDtypeStruct(slot_shape(rows.shape[0]) + rows.shape[1:], rows.dtype)
        extra = [wide, rows, routes, length]
        extra_out = [
            jax.ShapeDtypeStruct((depth, wide.shape[0], wide.shape[1] // depth), wide.dtype),
            jax.ShapeDtypeStruct(picked.shape, picked.dtype),
        ]
    kinds = []
    for shape in ((count, depth),) * 4 + ((count, depth, 4), (depth,), (8,), (count, depth)):
        kinds += [pltpu.SemaphoreType.DMA(shape)] * 2
    fulls = pl.pallas_call(
        functools.partial(gather_kernel, depth, count, more),
        out_shape=[jax.ShapeDtypeStruct((depth, 4, 2) + s.shape, s.dtype) for s in shards] + extra_out,
        in_specs=[pl.BlockSpec(memory_space=pl.ANY)] * (count + more)
        + [pl.BlockSpec(memory_space=pltpu.VMEM)] * 2 * more
        + [pl.BlockSpec(memory_space=pltpu.SMEM)] * more,
        out_specs=[pl.BlockSpec(memory_space=pl.ANY)] * (count + len(extra_out)),
        scratch_shapes=[pltpu.SemaphoreType.DMA((count + 2,))]
        + kinds
        + ([pltpu.VMEM(picked.shape, picked.dtype)] if more else []),
        compiler_params=pltpu.CompilerParams(collective_id=ident, has_side_effects=True),
        cost_estimate=pl.CostEstimate(flops=1, bytes_accessed=1, transcendentals=0),
        name=f"gather_plane_{ident}",
    )(*shards, *extra)
    full = [f.reshape((-1,) + s.shape[1:]) for f, s in zip(fulls, shards)]
    if more:
        full += [fulls[count].reshape((-1, extra_out[0].shape[2])), fulls[count + 1]]
    return full


def scatter_kernel(depth, count, work, *refs):
    grads, refs = refs[:count], refs[count:]
    if work:
        operands, packed, product, parts = refs[:6], refs[6], refs[7], refs[8]
        buffers, w_sems, keep, staged_sems, staged, refs = refs[-10:], refs[-12:-10], refs[-13], refs[-14], refs[-15], refs[9:-15]
        width = packed.shape[2]
        made_rows = operands[0].shape[0] // depth
        tops = [0]
        for grad in grads:
            tops.append(tops[-1] + grad.shape[3] * grad.shape[4] // width)
    else:
        outs, refs = refs[:count], refs[count:]
    own, twins, first, second = (refs[i * count : (i + 1) * count] for i in range(4))
    n = 4 * count
    load, c_sems, f_sems, s_sems = refs[n], refs[n + 1 : n + 3], refs[n + 3 : n + 5], refs[n + 5 : n + 7]
    level, here = lax.axis_index("dp"), lax.axis_index("expert")
    chip, core, x, y, twin, x_next, y_next = plane()
    greet(depth, (twin, x_next, y_next), work)
    started, loads, flown = [], {}, []

    def send(*a):
        copy = remote(*a)
        copy.start()
        started.append(copy)

    order = [(step, (step + level + 1) % depth) for step in range(depth)]
    for step, at in order:
        for i in range(count):
            send(grads[i].at[at, :, 1 - core], twins[i].at[step], c_sems, (i, step), level, twin)
            loads[i, step] = pltpu.make_async_copy(grads[i].at[at, :, core], own[i].at[step], load.at[i, step])
            loads[i, step].start()

    def part(at):
        wide = parts.shape[1] // depth
        return parts.at[:, pl.ds(pl.multiple_of(at * wide, wide), wide)]

    def hand_out(block, at, way):
        if way:
            send(block, part(level), w_sems, (way,), at, here)
        else:
            copy = pltpu.make_async_copy(block, part(level), keep.at[0])
            copy.start()
            flown.append(copy)

    jobs = expert_work(depth, level, operands, (packed, product), buffers, hand_out) if work else iter(())
    next(jobs, None)

    def add(target, other):
        target[...] = (target[...].astype(jnp.float32) + other[...].astype(jnp.float32)).astype(jnp.bfloat16)

    def chips(step):
        if step % 2 == 0:
            return (1 - x, 3 - x), (x, 2 + x), x_next, y_next
        return (2 - 2 * y, 3 - 2 * y), (2 * y, 2 * y + 1), y_next, x_next

    for step, at in order:
        away, near, first_next, second_next = chips(step)
        for i in range(count):
            loads[i, step].wait()
            remote(own[i].at[step], twins[i].at[step], c_sems, (i, step), level, here).wait_recv()
            for side in range(2):
                add(own[i].at[step, away[side]], twins[i].at[step, away[side]])
                send(own[i].at[step, away[side]], first[i].at[step, side], f_sems, (i, step, side), level, first_next)
        for i in range(count):
            for side in range(2):
                add(own[i].at[step, near[side]], twins[i].at[step, near[side]])
    next(jobs, None)
    for step, at in order:
        away, near, first_next, second_next = chips(step)
        for i in range(count):
            for side in range(2):
                remote(own[i].at[step, 0], first[i].at[step, side], f_sems, (i, step, side), level, here).wait_recv()
                add(own[i].at[step, near[side]], first[i].at[step, side])
            across = chip + 2 - 4 * y if step % 2 == 0 else chip + 1 - 2 * x
            send(own[i].at[step, across], second[i].at[step], s_sems, (i, step), level, second_next)
        if step == 1:
            next(jobs, None)
    for _ in jobs:
        pass
    for step, at in order:
        for i in range(count):
            remote(own[i].at[step, 0], second[i].at[step], s_sems, (i, step), level, here).wait_recv()
            add(second[i].at[step], own[i].at[step, chip])
            sums = second[i][step]
            if work:
                for piece in range(sums.shape[1] // width):
                    place = pl.ds(tops[i] + piece * sums.shape[0], sums.shape[0])
                    staged[step, place] = sums[:, piece * width : (piece + 1) * width]
            else:
                outs[i][at] = sums
        if work:
            copy = pltpu.make_async_copy(staged.at[step], packed.at[at, made_rows:], staged_sems.at[step])
            copy.start()
            flown.append(copy)
    if work:
        for way in range(1, depth):
            spot = part((level + depth - way) % depth)
            remote(spot, spot, w_sems, (way,), level, here).wait_recv()
    for copy in flown:
        copy.wait()
    for copy in started:
        copy.wait_send()


def expert_work(depth, level, operands, results, buffers, hand_out):
    act, pulled, rows_in, pre_grad, down, mix = operands
    act_at, grads_at, rows_at, pre_at, down_at, mix_at, tall, low, eup_at, sems = buffers
    pairs = ((act, act_at), (pulled, grads_at), (down, down_at), (rows_in, rows_at), (pre_grad, pre_at), (mix, mix_at))
    copies = [pltpu.make_async_copy(a, b, sems.at[i]) for i, (a, b) in enumerate(pairs)]
    for i in (3, 4, 0, 1, 5, 2):
        copies[i].start()
    tile = tall.shape[1]
    height = low.shape[1]

    def in_flight(slot, stage, target, sem):
        return pltpu.make_async_copy(stage.at[slot], target, sems.at[sem + slot])

    def tiles(number, stage, sem, compute, target):
        def body(i, carry):
            slot = i % 2

            @pl.when(i >= 2)
            def _():
                in_flight(slot, stage, target(i), sem).wait()

            stage[slot] = compute(i)
            in_flight(slot, stage, target(i), sem).start()
            return carry

        lax.fori_loop(0, number, body, 0)
        for slot in range(2):
            in_flight(slot, stage, target(0), sem).wait()

    def columns(array, i, size):
        return array[:, pl.ds(pl.multiple_of(i * size, size), size)]

    copies[3].wait()
    copies[4].wait()
    own_rows = eup_at.shape[1]
    for step in range(depth):
        at = (level + step) % depth
        eup_at[step] = matmul_tn(columns(rows_at, at, own_rows), pre_at[...]).astype(jnp.bfloat16)
        hand_out(eup_at.at[step], at, step)
    yield
    for i in (0, 1, 5):
        copies[i].wait()
    grads_at[...] = (grads_at[...].astype(jnp.float32) * mix_at[...]).astype(jnp.bfloat16)
    tiles(
        act_at.shape[1] // tile,
        tall,
        6,
        lambda i: matmul_tn(columns(act_at, i, tile), grads_at[...]),
        lambda i: results[1].at[pl.ds(pl.multiple_of(i * tile, tile), tile)],
    )
    yield
    copies[2].wait()
    tiles(
        results[0].shape[0],
        low,
        8,
        lambda i: matmul(act_at[pl.ds(pl.multiple_of(i * height, 16), height), :], down_at[...]).astype(jnp.bfloat16),
        lambda i: results[0].at[i, 0:height],
    )
    yield


def settle_kernel(depth, count, *refs):
    sums, summed, table, refs = refs[:count], refs[count], refs[count + 1], refs[count + 2 :]
    outs, expert_out, refs = refs[:count], refs[count], refs[count + 1 :]
    levels, z_sems, p_sems, keep = refs[:count], refs[count : count + 2], refs[count + 2 : count + 4], refs[count + 4]
    returned = refs[count + 5]
    level, here = lax.axis_index("dp"), lax.axis_index("expert")
    greet(depth, [(here + way) % 8 for way in range(1, 8)], True)
    capacity = returned.shape[1]
    started = []

    def slots(mate):
        return summed.at[pl.ds(pl.multiple_of(mate * capacity, 16), capacity)]

    for step in range(1, depth):
        target = (level + step) % depth
        for i in range(count):
            started.append(remote(sums[i].at[target], levels[i].at[step - 1], z_sems, (i, step), target, here))
            started[-1].start()
    for way in range(1, 8):
        mate = (here + way) % 8
        started.append(remote(slots(mate), returned.at[here], p_sems, (way,), level, mate))
        started[-1].start()
    kept = pltpu.make_async_copy(slots(here), returned.at[here], keep.at[0])
    kept.start()
    for way in range(1, 8):
        spot = returned.at[(here + 8 - way) % 8]
        remote(spot, spot, p_sems, (way,), level, here).wait_recv()
    kept.wait()
    rows = returned[...].reshape((-1, returned.shape[2]))
    expert_out[...] = matmul_tn(table[...], rows).astype(jnp.bfloat16)
    for i in range(count):
        total = sums[i][level].astype(jnp.float32)
        for step in range(1, depth):
            remote(levels[i].at[step - 1], levels[i].at[step - 1], z_sems, (i, step), level, here).wait_recv()
            total = total + levels[i][step - 1].astype(jnp.float32)
        outs[i][...] = total
    for copy in started:
        copy.wait_send()


def settle(sums, summed, table, ident):
    depth, count = lax.axis_size("dp"), len(sums)
    if lax.axis_size("expert") != 8:
        summed = summed.reshape(slot_shape(table.shape[1]) + summed.shape[1:])
        summed = lax.all_to_all(summed, "expert", split_axis=0, concat_axis=0, tiled=True)
        return [*sums, matmul_tn(table, summed.reshape((-1, summed.shape[2]))).astype(summed.dtype)]
    blocks = [s.shape[1:] for s in sums]
    vmem, whole = pl.BlockSpec(memory_space=pltpu.VMEM), pl.BlockSpec(memory_space=pl.ANY)
    return pl.pallas_call(
        functools.partial(settle_kernel, depth, count),
        out_shape=[jax.ShapeDtypeStruct(b, jnp.float32) for b in blocks]
        + [jax.ShapeDtypeStruct((table.shape[1],) + summed.shape[1:], summed.dtype)],
        in_specs=[vmem] * count + [whole, vmem],
        out_specs=[vmem] * (count + 1),
        scratch_shapes=[pltpu.VMEM((depth - 1,) + b, jnp.bfloat16) for b in blocks]
        + [pltpu.SemaphoreType.DMA((count, depth))] * 2
        + [pltpu.SemaphoreType.DMA((8,))] * 2
        + [pltpu.SemaphoreType.DMA((1,)), pltpu.VMEM(slot_shape(table.shape[1]) + summed.shape[1:], summed.dtype)],
        compiler_params=pltpu.CompilerParams(collective_id=ident, has_side_effects=True),
        cost_estimate=pl.CostEstimate(flops=1, bytes_accessed=1, transcendentals=0),
        name="settle",
    )(*sums, summed, table)


def scatter_plane(grads, ident, work=None):
    depth, count = lax.axis_size("dp"), len(grads)
    low = jnp.bfloat16
    if lax.axis_size("expert") != 8:
        sums = [lax.psum_scatter(g, both, scatter_dimension=0, tiled=True).astype(jnp.float32) for g in grads]
        if work is not None:
            act, pulled, rows_in, pre_grad, down, mix = work
            grad_rows = (pulled.astype(jnp.float32) * mix).astype(low)
            sums.append(matmul(act, down).astype(low))
            sums.append(matmul_tn(act, grad_rows))
            tall = matmul_tn(rows_in, pre_grad).astype(low)
            sums.append(lax.all_to_all(tall, "dp", split_axis=0, concat_axis=1, tiled=True))
        return sums
    grads = [g.reshape((depth, 4, 2, g.shape[0] // (8 * depth)) + g.shape[1:]) for g in grads]
    blocks = [g.shape[3:] for g in grads]
    width = min(b[1] for b in blocks)
    scratch = [pltpu.VMEM((depth, 4) + b, low) for b in blocks] * 2
    scratch += [pltpu.VMEM((depth, 2) + b, low) for b in blocks]
    scratch += [pltpu.VMEM((depth,) + b, low) for b in blocks]
    scratch += [pltpu.SemaphoreType.DMA((count, depth))] * 3 + [pltpu.SemaphoreType.DMA((count, depth, 2))] * 2
    scratch += [pltpu.SemaphoreType.DMA((count, depth))] * 2
    if work is None:
        operands = ()
        made = [jax.ShapeDtypeStruct((depth,) + b, low) for b in blocks]
    else:
        operands = tuple(work)
        act, rows_in, pre_grad, down = work[0], work[2], work[3], work[4]
        packed_rows, made_rows = sum(b[0] * b[1] for b in blocks) // width, act.shape[0] // depth
        own_rows = rows_in.shape[1] // depth
        made = [
            jax.ShapeDtypeStruct((depth, made_rows + packed_rows, width), low),
            jax.ShapeDtypeStruct((act.shape[1], act.shape[1]), jnp.float32),
            jax.ShapeDtypeStruct((own_rows, pre_grad.shape[1] * depth), low),
        ]
        scratch += [pltpu.VMEM((depth, packed_rows, width), low), pltpu.SemaphoreType.DMA((depth,))]
        scratch += [pltpu.SemaphoreType.DMA((1,))] + [pltpu.SemaphoreType.DMA((depth,))] * 2
        scratch += [pltpu.VMEM(work[i].shape, work[i].dtype) for i in range(6)]
        scratch += [
            pltpu.VMEM((2, 256, down.shape[1]), jnp.float32),
            pltpu.VMEM((2, made_rows, down.shape[1]), low),
            pltpu.VMEM((depth, own_rows, pre_grad.shape[1]), low),
            pltpu.SemaphoreType.DMA((10,)),
        ]
    out_space = pltpu.VMEM if work is None else pl.ANY
    return list(
        pl.pallas_call(
            functools.partial(scatter_kernel, depth, count, work is not None),
            out_shape=made,
            in_specs=[pl.BlockSpec(memory_space=pl.ANY)] * (count + len(operands)),
            out_specs=[pl.BlockSpec(memory_space=out_space)] * len(made),
            scratch_shapes=scratch,
            compiler_params=pltpu.CompilerParams(
                collective_id=ident, has_side_effects=True, vmem_limit_bytes=58 * 2**20
            ),
            cost_estimate=pl.CostEstimate(flops=1, bytes_accessed=200 * 2**20, transcendentals=0),
            name=f"scatter_plane_{ident}",
        )(*grads, *operands)
    )


def finish_scatter(packed, top, shapes):
    packed = lax.psum_scatter(packed, "dp", scatter_dimension=0)
    width = packed.shape[1]
    outs = [packed]
    for rows, columns in shapes:
        pieces = columns // width
        blocks = [packed[top + i * rows : top + (i + 1) * rows].astype(jnp.float32) for i in range(pieces)]
        outs.append(jnp.concatenate(blocks, axis=1))
        top += pieces * rows
    return outs


def body(
    tokens,
    seq_lengths,
    routes,
    w_qkv,
    w_out,
    w_up,
    w_down,
    gain_attn,
    gain_mlp,
    w_mix,
    expert_up,
    expert_down,
    cotangent,
):
    tok_rows, model_width = tokens.shape
    axis_dp, axis_experts = lax.axis_size("dp"), lax.axis_size("expert")
    expert_total = axis_experts * expert_up.shape[0]
    capacity = max(2, 5 * tok_rows // (4 * expert_total))
    slots = expert_total * capacity
    ff_expert = expert_up.shape[2]

    small = jnp.concatenate([gain_attn[:, None], gain_mlp[:, None], w_mix], axis=1)
    small = jnp.pad(small, ((0, 0), (0, 128 - small.shape[1])))
    length = seq_lengths[0]
    valid_rows = jnp.arange(tok_rows, dtype=jnp.int32) < length

    def pick(rows):
        return matmul(slot_table, rows).astype(jnp.bfloat16).reshape(expert_total, capacity, model_width)

    def dispatch(rows):
        arrived = lax.all_to_all(pick(rows), "expert", split_axis=0, concat_axis=0, tiled=True)
        return arrived.reshape(slots, model_width)

    def spread(rows):
        return lax.all_gather(rows, "dp", axis=0, tiled=True)

    def unspread(rows):
        return lax.psum_scatter(rows, "dp", scatter_dimension=0, tiled=True)

    def give_back(summed):
        summed = summed.reshape(expert_total, capacity, model_width)
        back = lax.all_to_all(summed, "expert", split_axis=0, concat_axis=0, tiled=True)
        return matmul_tn(slot_table, back.reshape(slots, model_width))

    down_part = expert_down[0]

    upstream_low = jnp.where(valid_rows[:, None], cotangent, jnp.zeros_like(cotangent))
    upstream = upstream_low.astype(jnp.float32)
    route_row = routes.reshape((1, tok_rows))
    qkv_full, out_full, small_full, up_part, pulled_here = gather_plane(
        [w_qkv, w_out, small], 0, expert_up[0], cotangent, route_row, seq_lengths
    )
    slot_table = slots_of(lax.optimization_barrier((route_row, qkv_full))[0], length, tok_rows)
    pulled_rows = spread(pulled_here.reshape(slots, model_width))
    gain_one = small_full[:, 0].astype(jnp.float32)
    gain_two = small_full[:, 1].astype(jnp.float32)
    mix_full = small_full[:, 2:4]
    mix_lean = (mix_full[:, 0] - mix_full[:, 1].astype(jnp.float32)).astype(jnp.float32)

    inputs = tokens.astype(jnp.float32)
    scaled_one, inverse_one = norm_forward(inputs)
    normed_one = (scaled_one * gain_one).astype(jnp.bfloat16)
    joined = matmul(normed_one, qkv_full).astype(jnp.bfloat16)
    heads_out, log_total = attention_forward(joined, seq_lengths)
    after_attn = inputs + matmul(heads_out, out_full)
    scaled_two, inverse_two = norm_forward(after_attn)
    normed_two = (scaled_two * gain_two).astype(jnp.bfloat16)

    rows_here = dispatch(normed_two)
    rows_here, w_up, w_down = lax.optimization_barrier((rows_here, w_up, w_down))
    rows_in = spread(rows_here)
    up_full, down_full = gather_plane([w_up, w_down], 1)

    pulled_rows, up_full, down_full = lax.optimization_barrier((pulled_rows, up_full, down_full))
    mix_weights = jax.nn.softmax(matmul(normed_two, mix_full), axis=-1)
    grad_down, grad_up, normed_grad, dense_out, pull_dense = dense_branch(
        normed_two, up_full, down_full, upstream_low, mix_weights[:, 0:1]
    )
    lean_dense = mix_weights[:, 0:1] * mix_weights[:, 1:2] * pull_dense
    normed_grad = normed_grad + lean_dense * mix_lean[None, :]

    act_pull = matmul_nt(pulled_rows, down_part)
    rows_in, act_pull, grad_up, grad_down, normed_grad = lax.optimization_barrier(
        (rows_in, act_pull, grad_up, grad_down, normed_grad)
    )
    act_rows, pre_grad, row_mix, input_grad, lean_rows = expert_branch(
        rows_in, act_pull, up_part, small_full, mix_lean[None, :]
    )
    in_grad_here = unspread(input_grad)
    *sums, grad_expert_down, grad_expert_up = scatter_plane(
        [grad_up, grad_down], 2, (act_rows, pulled_rows, rows_in, pre_grad, down_part, row_mix)
    )
    grad_expert_down = grad_expert_down[None]
    in_grad_here, *sums = lax.optimization_barrier((in_grad_here, *sums))
    if len(sums) == 1:
        outs_here, grad_up, grad_down = finish_scatter(sums[0], slots, (w_up.shape, w_down.shape))
    else:
        grad_up, grad_down, outs_here = sums[0], sums[1], unspread(sums[2])
    in_grad_back = give_back(in_grad_here)

    normed_grad = normed_grad + in_grad_back
    lean_grad = jnp.sum(normed_two.astype(jnp.float32) * lean_dense, axis=0) - lean_rows[0]
    mlp_in_grad, grad_gain_two = norm_backward(normed_grad, scaled_two, inverse_two, gain_two)
    resid_grad = upstream + mlp_in_grad
    attn_grad = resid_grad.astype(jnp.bfloat16)
    grad_out = matmul_tn(heads_out, attn_grad)
    heads_grad = matmul_nt(attn_grad, out_full).astype(jnp.bfloat16)
    joined_grad = jnp.concatenate(
        attention_backward(joined, heads_grad, heads_out, log_total, seq_lengths), axis=1
    )
    grad_qkv = matmul_tn(normed_one, joined_grad)
    normed_one_grad = matmul_nt(joined_grad, qkv_full)
    attn_in_grad, grad_gain_one = norm_backward(normed_one_grad, scaled_one, inverse_one, gain_one)
    grad_inputs = resid_grad + attn_in_grad

    small_grads = jnp.stack([grad_gain_one, grad_gain_two, lean_grad, -lean_grad], axis=1)
    small_grads = jnp.pad(small_grads, ((0, 0), (0, 128 - small_grads.shape[1])))
    grad_expert_down = jnp.where(length >= 0, grad_expert_down, 0.0)
    grad_expert_up = grad_expert_up.astype(jnp.float32)[None]
    small_grads, grad_expert_down, grad_expert_up = lax.optimization_barrier(
        (small_grads.astype(jnp.bfloat16), grad_expert_down, grad_expert_up)
    )
    sums = scatter_plane([grad_qkv.astype(jnp.bfloat16), grad_out.astype(jnp.bfloat16), small_grads], 3)
    grad_qkv, grad_out, small_grads, expert_out = settle(sums, outs_here, slot_table, 4)
    result = after_attn + mix_weights[:, 0:1] * dense_out + mix_weights[:, 1:2] * expert_out
    return (
        result,
        grad_inputs,
        grad_qkv,
        grad_out,
        grad_up,
        grad_down,
        small_grads[:, 0],
        small_grads[:, 1],
        small_grads[:, 2:4],
        grad_expert_up,
        grad_expert_down,
    )


def solution(mesh):
    rows, vector = P(both, None), P(both)
    experts = P("expert", "dp", None)
    return jax.shard_map(
        body,
        mesh=mesh,
        in_specs=(rows, vector, rows, rows, rows, rows, rows, vector, vector, rows, experts, experts, rows),
        out_specs=(rows, rows, rows, rows, rows, rows, vector, vector, rows, experts, experts),
        check_vma=False,
    )
```

```python
import functools

import jax
import jax.numpy as jnp
from jax import lax
from jax.experimental import pallas as pl
from jax.experimental.pallas import tpu as pltpu
from jax.sharding import PartitionSpec as P

HEADS = 16

epsilon = 1e-05
root_half = 0.7071067811865476
inv_root_two_pi = 0.3989422804014327
highest = lax.Precision.HIGHEST
both = ("dp", "expert")


def gelu_pair(values):
    scaled = values * root_half
    half = 0.5 + 0.5 * lax.erf(scaled)
    return values * half, half + (values * inv_root_two_pi) * jnp.exp(-(scaled * scaled))


def dot(left, right, dims):
    return lax.dot_general(left, right, (dims, ((), ())), preferred_element_type=jnp.float32)


def matmul(left, right):
    return dot(left, right, ((1,), (0,)))


def matmul_nt(left, right):
    return dot(left, right, ((1,), (1,)))


def matmul_tn(left, right):
    return dot(left, right, ((0,), (0,)))


def norm_forward(values):
    row_mean = jnp.mean(values, axis=-1, keepdims=True)
    centred = values - row_mean
    row_var = jnp.mean(centred * centred, axis=-1, keepdims=True)
    inverse = lax.rsqrt(row_var + epsilon)
    return (centred * inverse, inverse)


def norm_backward(upstream, scaled, inverse, gain_row):
    gain_grad = jnp.sum(upstream * scaled, axis=0)
    inner = upstream * gain_row
    centred_grad = (
        inner
        - jnp.mean(inner, axis=-1, keepdims=True)
        - scaled * jnp.mean(inner * scaled, axis=-1, keepdims=True)
    )
    return (inverse * centred_grad, gain_grad)


def head_scores(queries, keys_all, length, row_start, scale):
    scores = matmul_nt(queries, keys_all) * scale
    rows_at = row_start + lax.broadcasted_iota(jnp.int32, scores.shape, 0)
    cols_at = lax.broadcasted_iota(jnp.int32, scores.shape, 1)
    return jnp.where((cols_at <= rows_at) & (cols_at < length), scores, -1000000000.0)


def attention_forward_kernel(head_width, bands, length_ref, q_ref, k_ref, v_ref, out_ref, log_ref):
    length = length_ref[0]
    scale = head_width ** (-0.5)
    tok_rows, lanes = q_ref.shape
    height = tok_rows // bands
    lane = lax.broadcasted_iota(jnp.int32, (1, lanes), 1) // head_width
    for band in range(bands):
        top, end = band * height, (band + 1) * height
        keys_all, values_all = k_ref[0:end, :], v_ref[0:end, :]
        queries = q_ref[top:end, :]
        mixed = jnp.zeros((height, lanes), jnp.float32)
        logs = []
        for head in range(lanes // head_width):
            mine = lane == head
            scores = head_scores(jnp.where(mine, queries, 0), keys_all, length, top, scale)
            top_score = jnp.max(scores, axis=-1, keepdims=True)
            raised = jnp.exp(scores - top_score)
            row_total = jnp.sum(raised, axis=-1, keepdims=True)
            probs = (raised / row_total).astype(jnp.bfloat16)
            mixed = mixed + matmul(probs, jnp.where(mine, values_all, 0))
            logs.append(top_score + jnp.log(row_total))
        out_ref[top:end, :] = mixed.astype(jnp.bfloat16)
        spread = jnp.broadcast_to(logs[0], (height, lanes))
        for head in range(1, len(logs)):
            spread = jnp.where(lane == head, logs[head], spread)
        log_ref[top:end, :] = spread


def attention_forward(joined, length):
    tok_rows, width = joined.shape[0], joined.shape[1] // 3
    head_width = width // HEADS
    lanes = max(128, head_width)
    tiles = width // lanes
    bands = 2

    def part(which):
        return pl.BlockSpec((tok_rows, lanes), lambda i: (0, which * tiles + i))

    return pl.pallas_call(
        functools.partial(attention_forward_kernel, head_width, bands),
        grid=(tiles,),
        out_shape=[
            jax.ShapeDtypeStruct((tok_rows, width), jnp.bfloat16),
            jax.ShapeDtypeStruct((tok_rows, width), jnp.float32),
        ],
        in_specs=[pl.BlockSpec(memory_space=pltpu.SMEM), part(0), part(1), part(2)],
        out_specs=[part(0), part(0)],
        compiler_params=pltpu.CompilerParams(vmem_limit_bytes=32 * 2**20),
        cost_estimate=pl.CostEstimate(flops=4 * tok_rows * tok_rows * width, bytes_accessed=10 * tok_rows * width, transcendentals=0),
        name="attention_forward",
    )(length, joined, joined, joined)


def attention_backward_kernel(head_width, bands, length_ref, q_ref, k_ref, v_ref, g_ref, o_ref, log_ref, dq_ref, dk_ref, dv_ref, dk_sum, dv_sum):
    length = length_ref[0]
    scale = head_width ** (-0.5)
    tok_rows, lanes = q_ref.shape
    height = tok_rows // bands
    lane = lax.broadcasted_iota(jnp.int32, (1, lanes), 1) // head_width
    for band in range(bands):
        top, end = band * height, (band + 1) * height
        keys_all, values_all = k_ref[0:end, :], v_ref[0:end, :]
        queries, grads = q_ref[top:end, :], g_ref[top:end, :]
        turned = lax.transpose(log_ref[top:end, :], (1, 0))
        products = lax.transpose(grads.astype(jnp.float32) * o_ref[top:end, :].astype(jnp.float32), (1, 0))
        dq = jnp.zeros((height, lanes), jnp.float32)
        dk = jnp.zeros((end, lanes), jnp.float32)
        dv = jnp.zeros((end, lanes), jnp.float32)
        keys_at = lax.broadcasted_iota(jnp.int32, (end, height), 0)
        rows_at = top + lax.broadcasted_iota(jnp.int32, (end, height), 1)
        allowed = (keys_at <= rows_at) & (keys_at < length)
        for head in range(lanes // head_width):
            mine = lane == head
            own_q, own_g = jnp.where(mine, queries, 0), jnp.where(mine, grads, 0)
            log_total = turned[head * head_width : head * head_width + 1, :]
            delta = jnp.sum(products[head * head_width : (head + 1) * head_width, :], axis=0, keepdims=True)
            scores = jnp.where(allowed, matmul_nt(keys_all, own_q) * scale, -1000000000.0)
            probs = jnp.exp(scores - log_total)
            prob_grad = matmul_nt(values_all, own_g)
            score_grad = (probs * (prob_grad - delta)).astype(jnp.bfloat16)
            dv = dv + matmul(probs.astype(jnp.bfloat16), own_g)
            dk = dk + matmul(score_grad, own_q)
            dq = dq + matmul_tn(score_grad, jnp.where(mine, keys_all, 0))
        dq_ref[top:end, :] = (dq * scale).astype(jnp.bfloat16)
        if band == 0:
            dk_sum[...] = jnp.zeros_like(dk_sum)
            dv_sum[...] = jnp.zeros_like(dv_sum)
        dk_sum[0:end, :] += dk
        dv_sum[0:end, :] += dv
    dk_ref[...] = (dk_sum[...] * scale).astype(jnp.bfloat16)
    dv_ref[...] = dv_sum[...].astype(jnp.bfloat16)


def attention_backward(joined, heads_grad, heads_out, log_total, length):
    tok_rows, width = joined.shape[0], joined.shape[1] // 3
    head_width = width // HEADS
    lanes = max(128, head_width)
    tiles = width // lanes
    bands = 2

    def part(which):
        return pl.BlockSpec((tok_rows, lanes), lambda i: (0, which * tiles + i))

    return pl.pallas_call(
        functools.partial(attention_backward_kernel, head_width, bands),
        grid=(tiles,),
        out_shape=[jax.ShapeDtypeStruct((tok_rows, width), jnp.bfloat16)] * 3,
        in_specs=[pl.BlockSpec(memory_space=pltpu.SMEM), part(0), part(1), part(2), part(0), part(0), part(0)],
        out_specs=[part(0)] * 3,
        scratch_shapes=[pltpu.VMEM((tok_rows, lanes), jnp.float32)] * 2,
        compiler_params=pltpu.CompilerParams(vmem_limit_bytes=32 * 2**20),
        cost_estimate=pl.CostEstimate(flops=10 * tok_rows * tok_rows * width, bytes_accessed=20 * tok_rows * width, transcendentals=0),
        name="attention_backward",
    )(length, joined, joined, joined, heads_grad, heads_out, log_total)


def expert_kernel(tile, rows_ref, pull_ref, up_ref, small_ref, lean_ref, act_ref, pre_ref, mix_ref, in_ref, sum_ref):
    low = jnp.bfloat16
    rows_in = rows_ref[...]
    logits = matmul(rows_in, small_ref[...])
    first, second = logits[:, 2:3], logits[:, 3:4]
    top = jnp.maximum(first, second)
    first, second = jnp.exp(first - top), jnp.exp(second - top)
    mix_dense, mix_expert = first / (first + second), second / (first + second)
    mix_ref[...] = mix_expert
    tiles = [slice(left, left + tile) for left in range(0, up_ref.shape[1], tile)]
    pull = jnp.zeros_like(mix_expert)
    total = None
    coming = matmul(rows_in, up_ref[:, tiles[0]])
    for i, columns in enumerate(tiles):
        pre_act = coming
        if i + 1 < len(tiles):
            coming = matmul(rows_in, up_ref[:, tiles[i + 1]])
        act_pull = pull_ref[:, columns]
        gelu, slope = gelu_pair(pre_act)
        act = gelu.astype(low)
        act_ref[:, columns] = act
        pull = pull + jnp.sum(act.astype(jnp.float32) * act_pull, axis=1, keepdims=True)
        pre_grad = (mix_expert * act_pull * slope).astype(low)
        pre_ref[:, columns] = pre_grad
        part = matmul_nt(pre_grad, up_ref[:, columns])
        total = part if total is None else total + part
    lean = mix_dense * mix_expert * pull
    in_ref[...] = (total - lean * lean_ref[...]).astype(low)
    part = jnp.sum(rows_in.astype(jnp.float32) * lean, axis=0, keepdims=True)
    sum_ref[...] = jnp.where(pl.program_id(0) == 0, part, sum_ref[...] + part)


def expert_branch(rows_in, act_pull, up_part, small_full, mix_lean):
    count, width = rows_in.shape
    hidden = up_part.shape[1]
    height = 512

    def tall(columns):
        return pl.BlockSpec((height, columns), lambda i: (i, 0))

    def whole(array):
        return pl.BlockSpec(array.shape, lambda i: (0, 0))

    low = jnp.bfloat16
    return pl.pallas_call(
        functools.partial(expert_kernel, 256),
        grid=(count // height,),
        out_shape=[
            jax.ShapeDtypeStruct((count, hidden), low),
            jax.ShapeDtypeStruct((count, hidden), low),
            jax.ShapeDtypeStruct((count, 1), jnp.float32),
            jax.ShapeDtypeStruct((count, width), low),
            jax.ShapeDtypeStruct((1, width), jnp.float32),
        ],
        in_specs=[tall(width), tall(hidden), whole(up_part), whole(small_full), whole(mix_lean)],
        out_specs=[tall(hidden), tall(hidden), tall(1), tall(width), whole(mix_lean)],
        compiler_params=pltpu.CompilerParams(vmem_limit_bytes=58 * 2**20),
        cost_estimate=pl.CostEstimate(
            flops=4 * count * width * hidden, bytes_accessed=16 * count * width, transcendentals=0
        ),
        name="expert_branch",
    )(rows_in, act_pull, up_part, small_full, mix_lean)


def dense_kernel(normed_ref, up_ref, down_ref, grad_ref, mix_ref, gdown_ref, gup_ref, ngrad_ref, out_ref, pull_ref):
    normed, upstream, mix = normed_ref[...], grad_ref[...], mix_ref[...]
    hidden = matmul(normed, up_ref[...])
    dense_pull = matmul_nt(upstream, down_ref[...])
    gelu, slope = gelu_pair(hidden)
    act = gelu.astype(jnp.bfloat16)
    pull = jnp.sum(act.astype(jnp.float32) * dense_pull, axis=1, keepdims=True)
    hidden_grad = (mix * dense_pull * slope).astype(jnp.bfloat16)
    grad_out = (upstream.astype(jnp.float32) * mix).astype(jnp.bfloat16)
    gdown_ref[...] = matmul_tn(act, grad_out).astype(jnp.bfloat16)
    gup_ref[...] = matmul_tn(normed, hidden_grad).astype(jnp.bfloat16)
    ngrad = matmul_nt(hidden_grad, up_ref[...])
    dense_out = matmul(act, down_ref[...])

    @pl.when(pl.program_id(0) == 0)
    def _():
        ngrad_ref[...] = ngrad
        out_ref[...] = dense_out
        pull_ref[...] = pull

    @pl.when(pl.program_id(0) > 0)
    def _():
        ngrad_ref[...] += ngrad
        out_ref[...] += dense_out
        pull_ref[...] += pull


def dense_branch(normed_two, up_full, down_full, upstream_low, mix):
    rows, width = normed_two.shape
    ff = up_full.shape[1]
    block = 512

    def whole(columns):
        return pl.BlockSpec((rows, columns), lambda i: (0, 0))

    across, down = pl.BlockSpec((width, block), lambda i: (0, i)), pl.BlockSpec((block, width), lambda i: (i, 0))
    return pl.pallas_call(
        dense_kernel,
        grid=(ff // block,),
        out_shape=[
            jax.ShapeDtypeStruct((ff, width), jnp.bfloat16),
            jax.ShapeDtypeStruct((width, ff), jnp.bfloat16),
            jax.ShapeDtypeStruct((rows, width), jnp.float32),
            jax.ShapeDtypeStruct((rows, width), jnp.float32),
            jax.ShapeDtypeStruct((rows, 1), jnp.float32),
        ],
        in_specs=[whole(width), across, down, whole(width), whole(1)],
        out_specs=[down, across, whole(width), whole(width), whole(1)],
        compiler_params=pltpu.CompilerParams(vmem_limit_bytes=48 * 2**20),
        cost_estimate=pl.CostEstimate(flops=12 * rows * width * ff, bytes_accessed=8 * width * ff, transcendentals=0),
        name="dense_branch",
    )(normed_two, up_full, down_full, upstream_low, mix)


MESH = pl.DeviceIdType.MESH


def plane():
    here = lax.axis_index("expert")
    core, x, y = here % 2, (here // 2) % 2, here // 4
    return here // 2, core, x, y, here + 1 - 2 * core, here + 2 - 4 * x, here + 4 - 8 * y


def greet(depth, others, count):
    level = lax.axis_index("dp")
    barrier = pltpu.get_barrier_semaphore()
    for other in others:
        pl.semaphore_signal(barrier, inc=1, device_id=(level, other), device_id_type=MESH)
    if count:
        for step in range(1, depth):
            pl.semaphore_signal(
                barrier,
                inc=1,
                device_id=((level + step) % depth, lax.axis_index("expert")),
                device_id_type=MESH,
            )
    pl.semaphore_wait(barrier, len(others) + (depth - 1 if count else 0))


def remote(source, target, sems, slot, level, where):
    return pltpu.make_async_remote_copy(
        src_ref=source,
        dst_ref=target,
        send_sem=sems[0].at[slot],
        recv_sem=sems[1].at[slot],
        device_id=(level, where),
        device_id_type=MESH,
    )


def slot_shape(tok_rows):
    experts = lax.axis_size("expert")
    return (experts, max(2, 5 * tok_rows // (4 * experts)))


def slots_of(routes, length, tok_rows):
    experts, capacity = slot_shape(tok_rows)
    rows_at = lax.broadcasted_iota(jnp.int32, (1, tok_rows), 1)
    hits = (routes == lax.broadcasted_iota(jnp.int32, (experts, tok_rows), 0)) & (rows_at < length)
    hits = hits.astype(jnp.float32)
    earlier = lax.broadcasted_iota(jnp.int32, (tok_rows, tok_rows), 0) < lax.broadcasted_iota(jnp.int32, (tok_rows, tok_rows), 1)
    ranks = matmul(hits.astype(jnp.bfloat16), earlier.astype(jnp.bfloat16))
    rank = jnp.sum(hits * ranks, axis=0, keepdims=True)
    kept = (rows_at < length) & (rank < capacity)
    slot = routes * capacity + rank.astype(jnp.int32)
    slots_at = lax.broadcasted_iota(jnp.int32, (experts * capacity, tok_rows), 0)
    return ((slots_at == slot) & kept).astype(jnp.bfloat16)


def pick_rows(rows, routes, length, picked):
    experts, capacity, _ = picked.shape
    table = slots_of(routes[...], length[0], rows.shape[0])
    chosen = matmul(table, rows[...]).astype(jnp.bfloat16)
    for expert in range(experts):
        picked[expert] = chosen[expert * capacity : (expert + 1) * capacity]


def gather_kernel(depth, count, more, *refs):
    shards, refs = refs[:count], refs[count:]
    if more:
        wide, rows, routes, length, refs = refs[0], refs[1], refs[2], refs[3], refs[4:]
    fulls, refs = refs[:count], refs[count:]
    if more:
        parts, arrived, picked, refs = refs[0], refs[1], refs[-1], refs[2:-1]
    keep, sems = refs[0], refs[1:]
    up_sems, x_sems, y_sems, d_sems, c_sems, w_sems, p_sems, low_sems = (sems[2 * i : 2 * i + 2] for i in range(8))
    z_sems = (up_sems, low_sems)
    level, here = lax.axis_index("dp"), lax.axis_index("expert")
    chip, core, x, y, twin, x_next, y_next = plane()
    x_chip, y_chip, far_chip = chip + 1 - 2 * x, chip + 2 - 4 * y, 3 - chip
    mates = [(here + step) % 8 for step in range(1, 8)] if more else (twin, x_next, y_next)
    greet(depth, mates, True)
    started, locals_ = [], []

    def send(*a):
        copy = remote(*a)
        copy.start()
        started.append(copy)

    def stay(source, target, slot):
        copy = pltpu.make_async_copy(source, target, keep.at[slot])
        copy.start()
        locals_.append(copy)

    def to_twin(i, step, chip_at, source=None):
        spot = fulls[i].at[(level + depth - step) % depth, chip_at, core]
        send(spot if source is None else source, spot, c_sems, (i, step, chip_at), level, twin)

    def along(i, hop, way, source):
        block = fulls[i].at[source, chip, core]
        target = (level + (1 if way == 0 else depth - 1)) % depth
        return remote(shards[i] if hop == 0 else block, block, z_sems[way], (i, hop), target, here)

    def ahead(way):
        return level < depth - 1 if way == 0 else level > 0

    def comes(hop, way):
        return level >= hop if way == 0 else level < depth - hop

    def back(hop, way):
        return (level + depth - hop) % depth if way == 0 else (level + hop) % depth

    def across(i, step, origin, begin):
        block = fulls[i].at[(level + depth - step) % depth, chip, core]
        copies = (
            remote(origin, block, x_sems, (i, step), level, x_next),
            remote(origin, block, y_sems, (i, step), level, y_next),
            remote(origin, block, c_sems, (i, step, chip), level, twin),
        )
        for copy in copies:
            if begin:
                copy.start()
            else:
                copy.wait_send()

    if more:
        for step in range(1, depth):
            for i in range(count):
                target = (level + step) % depth
                send(shards[i], fulls[i].at[level, chip, core], up_sems, (i, step), target, here)
    else:
        for way in range(2):

            @pl.when(ahead(way))
            def _(way=way):
                for i in range(count):
                    along(i, 0, way, level).start()

    for i in range(count):
        stay(shards[i], fulls[i].at[level, chip, core], i)
        across(i, 0, shards[i], True)
    if more:
        width = wide.shape[1] // depth

        def columns(at):
            return wide.at[:, pl.ds(pl.multiple_of(at * width, width), width)]

        for way in range(1, depth):
            target = (level + way) % depth
            send(columns(target), parts.at[level], w_sems, (way,), target, here)
        stay(columns(level), parts.at[level], count)
        pick_rows(rows, routes, length, picked)
        for way in range(1, 8):
            mate = (here + way) % 8
            send(picked.at[mate], arrived.at[here], p_sems, (way,), level, mate)
        stay(picked.at[here], arrived.at[here], count + 1)
    for hop in range(1, depth):
        if more:
            for i in range(count):
                block = fulls[i].at[back(hop, 0), chip, core]
                remote(block, block, up_sems, (i, hop), level, here).wait_recv()
                across(i, hop, block, True)
            continue
        for way in range(2):

            @pl.when(comes(hop, way))
            def _(hop=hop, way=way):
                source = back(hop, way)
                for i in range(count):
                    block = fulls[i].at[source, chip, core]
                    remote(block, block, z_sems[way], (i, hop - 1), level, here).wait_recv()

                    @pl.when(ahead(way))
                    def _():
                        along(i, hop, way, source).start()

                    across(i, hop if way == 0 else depth - hop, block, True)

    for step in range(depth):
        source = (level + depth - step) % depth
        for i in range(count):
            x_spot, y_spot = fulls[i].at[source, x_chip, core], fulls[i].at[source, y_chip, core]
            remote(shards[i], x_spot, x_sems, (i, step), level, here).wait_recv()
            if step % 2 == 0:
                send(x_spot, x_spot, d_sems, (i, step), level, y_next)
            to_twin(i, step, x_chip)
            remote(shards[i], y_spot, y_sems, (i, step), level, here).wait_recv()
            if step % 2 == 1:
                send(y_spot, y_spot, d_sems, (i, step), level, x_next)
            to_twin(i, step, y_chip)
    for step in range(depth):
        source = (level + depth - step) % depth
        for i in range(count):
            spot = fulls[i].at[source, far_chip, core]
            remote(shards[i], spot, d_sems, (i, step), level, here).wait_recv()
            to_twin(i, step, far_chip)
    for step in range(depth):
        source = (level + depth - step) % depth
        for i in range(count):
            for chip_at in range(4):
                spot = fulls[i].at[source, chip_at, 1 - core]
                remote(shards[i], spot, c_sems, (i, step, chip_at), level, here).wait_recv()
    if more:
        for way in range(1, depth):
            spot = parts.at[(level + depth - way) % depth]
            remote(columns(level), spot, w_sems, (way,), level, here).wait_recv()
        for way in range(1, 8):
            spot = arrived.at[(here + 8 - way) % 8]
            remote(picked.at[here], spot, p_sems, (way,), level, here).wait_recv()
    for i in range(count):
        for step in range(depth):
            across(i, step, shards[i], False)
        for hop in () if more else range(depth):
            for way in range(2):

                @pl.when(comes(hop, way) & ahead(way))
                def _(i=i, hop=hop, way=way):
                    along(i, hop, way, back(hop, way)).wait_send()

    for copy in locals_:
        copy.wait()
    for copy in started:
        copy.wait_send()


def gather_plane(shards, ident, wide=None, rows=None, routes=None, length=None):
    depth, count, more = lax.axis_size("dp"), len(shards), wide is not None
    if lax.axis_size("expert") != 8:
        fulls = [lax.all_gather(s, both, axis=0, tiled=True) for s in shards]
        if more:
            fulls.append(lax.all_to_all(wide, "dp", split_axis=1, concat_axis=0, tiled=True))
            picked = matmul(slots_of(routes, length[0], rows.shape[0]), rows).astype(rows.dtype).reshape(slot_shape(rows.shape[0]) + rows.shape[1:])
            fulls.append(lax.all_to_all(picked, "expert", split_axis=0, concat_axis=0, tiled=True))
        return fulls
    extra, extra_out = [], []
    if more:
        picked = jax.ShapeDtypeStruct(slot_shape(rows.shape[0]) + rows.shape[1:], rows.dtype)
        extra = [wide, rows, routes, length]
        extra_out = [
            jax.ShapeDtypeStruct((depth, wide.shape[0], wide.shape[1] // depth), wide.dtype),
            jax.ShapeDtypeStruct(picked.shape, picked.dtype),
        ]
    kinds = []
    for shape in ((count, depth),) * 4 + ((count, depth, 4), (depth,), (8,), (count, depth)):
        kinds += [pltpu.SemaphoreType.DMA(shape)] * 2
    fulls = pl.pallas_call(
        functools.partial(gather_kernel, depth, count, more),
        out_shape=[jax.ShapeDtypeStruct((depth, 4, 2) + s.shape, s.dtype) for s in shards] + extra_out,
        in_specs=[pl.BlockSpec(memory_space=pl.ANY)] * (count + more)
        + [pl.BlockSpec(memory_space=pltpu.VMEM)] * 2 * more
        + [pl.BlockSpec(memory_space=pltpu.SMEM)] * more,
        out_specs=[pl.BlockSpec(memory_space=pl.ANY)] * (count + len(extra_out)),
        scratch_shapes=[pltpu.SemaphoreType.DMA((count + 2,))]
        + kinds
        + ([pltpu.VMEM(picked.shape, picked.dtype)] if more else []),
        compiler_params=pltpu.CompilerParams(collective_id=ident, has_side_effects=True),
        cost_estimate=pl.CostEstimate(flops=1, bytes_accessed=1, transcendentals=0),
        name=f"gather_plane_{ident}",
    )(*shards, *extra)
    full = [f.reshape((-1,) + s.shape[1:]) for f, s in zip(fulls, shards)]
    if more:
        full += [fulls[count].reshape((-1, extra_out[0].shape[2])), fulls[count + 1]]
    return full


def scatter_kernel(depth, count, work, *refs):
    grads, refs = refs[:count], refs[count:]
    if work:
        operands, packed, product, parts = refs[:6], refs[6], refs[7], refs[8]
        buffers, w_sems, keep, staged_sems, staged, refs = refs[-10:], refs[-12:-10], refs[-13], refs[-14], refs[-15], refs[9:-15]
        width = packed.shape[2]
        made_rows = operands[0].shape[0] // depth
        tops = [0]
        for grad in grads:
            tops.append(tops[-1] + grad.shape[3] * grad.shape[4] // width)
    else:
        outs, refs = refs[:count], refs[count:]
    own, twins, first, second = (refs[i * count : (i + 1) * count] for i in range(4))
    n = 4 * count
    load, c_sems, f_sems, s_sems = refs[n], refs[n + 1 : n + 3], refs[n + 3 : n + 5], refs[n + 5 : n + 7]
    level, here = lax.axis_index("dp"), lax.axis_index("expert")
    chip, core, x, y, twin, x_next, y_next = plane()
    greet(depth, (twin, x_next, y_next), work)
    started, loads, flown = [], {}, []

    def send(*a):
        copy = remote(*a)
        copy.start()
        started.append(copy)

    order = [(step, (step + level + 1) % depth) for step in range(depth)]
    for step, at in order:
        for i in range(count):
            send(grads[i].at[at, :, 1 - core], twins[i].at[step], c_sems, (i, step), level, twin)
            loads[i, step] = pltpu.make_async_copy(grads[i].at[at, :, core], own[i].at[step], load.at[i, step])
            loads[i, step].start()

    def part(at):
        wide = parts.shape[1] // depth
        return parts.at[:, pl.ds(pl.multiple_of(at * wide, wide), wide)]

    def hand_out(block, at, way):
        if way:
            send(block, part(level), w_sems, (way,), at, here)
        else:
            copy = pltpu.make_async_copy(block, part(level), keep.at[0])
            copy.start()
            flown.append(copy)

    jobs = expert_work(depth, level, operands, (packed, product), buffers, hand_out) if work else iter(())
    next(jobs, None)

    def add(target, other):
        target[...] = (target[...].astype(jnp.float32) + other[...].astype(jnp.float32)).astype(jnp.bfloat16)

    def chips(step):
        if step % 2 == 0:
            return (1 - x, 3 - x), (x, 2 + x), x_next, y_next
        return (2 - 2 * y, 3 - 2 * y), (2 * y, 2 * y + 1), y_next, x_next

    for step, at in order:
        away, near, first_next, second_next = chips(step)
        for i in range(count):
            loads[i, step].wait()
            remote(own[i].at[step], twins[i].at[step], c_sems, (i, step), level, here).wait_recv()
            for side in range(2):
                add(own[i].at[step, away[side]], twins[i].at[step, away[side]])
                send(own[i].at[step, away[side]], first[i].at[step, side], f_sems, (i, step, side), level, first_next)
        for i in range(count):
            for side in range(2):
                add(own[i].at[step, near[side]], twins[i].at[step, near[side]])
    next(jobs, None)
    for step, at in order:
        away, near, first_next, second_next = chips(step)
        for i in range(count):
            for side in range(2):
                remote(own[i].at[step, 0], first[i].at[step, side], f_sems, (i, step, side), level, here).wait_recv()
                add(own[i].at[step, near[side]], first[i].at[step, side])
            across = chip + 2 - 4 * y if step % 2 == 0 else chip + 1 - 2 * x
            send(own[i].at[step, across], second[i].at[step], s_sems, (i, step), level, second_next)
        if step == 1:
            next(jobs, None)
    for _ in jobs:
        pass
    for step, at in order:
        for i in range(count):
            remote(own[i].at[step, 0], second[i].at[step], s_sems, (i, step), level, here).wait_recv()
            add(second[i].at[step], own[i].at[step, chip])
            sums = second[i][step]
            if work:
                for piece in range(sums.shape[1] // width):
                    place = pl.ds(tops[i] + piece * sums.shape[0], sums.shape[0])
                    staged[step, place] = sums[:, piece * width : (piece + 1) * width]
            else:
                outs[i][at] = sums
        if work:
            copy = pltpu.make_async_copy(staged.at[step], packed.at[at, made_rows:], staged_sems.at[step])
            copy.start()
            flown.append(copy)
    if work:
        for way in range(1, depth):
            spot = part((level + depth - way) % depth)
            remote(spot, spot, w_sems, (way,), level, here).wait_recv()
    for copy in flown:
        copy.wait()
    for copy in started:
        copy.wait_send()


def expert_work(depth, level, operands, results, buffers, hand_out):
    act, pulled, rows_in, pre_grad, down, mix = operands
    act_at, grads_at, rows_at, pre_at, down_at, mix_at, tall, low, eup_at, sems = buffers
    pairs = ((act, act_at), (pulled, grads_at), (down, down_at), (rows_in, rows_at), (pre_grad, pre_at), (mix, mix_at))
    copies = [pltpu.make_async_copy(a, b, sems.at[i]) for i, (a, b) in enumerate(pairs)]
    for i in (3, 4, 0, 1, 5, 2):
        copies[i].start()
    tile = tall.shape[1]
    height = low.shape[1]

    def in_flight(slot, stage, target, sem):
        return pltpu.make_async_copy(stage.at[slot], target, sems.at[sem + slot])

    def tiles(number, stage, sem, compute, target):
        def body(i, carry):
            slot = i % 2

            @pl.when(i >= 2)
            def _():
                in_flight(slot, stage, target(i), sem).wait()

            stage[slot] = compute(i)
            in_flight(slot, stage, target(i), sem).start()
            return carry

        lax.fori_loop(0, number, body, 0)
        for slot in range(2):
            in_flight(slot, stage, target(0), sem).wait()

    def columns(array, i, size):
        return array[:, pl.ds(pl.multiple_of(i * size, size), size)]

    copies[3].wait()
    copies[4].wait()
    own_rows = eup_at.shape[1]
    for step in range(depth):
        at = (level + step) % depth
        eup_at[step] = matmul_tn(columns(rows_at, at, own_rows), pre_at[...]).astype(jnp.bfloat16)
        hand_out(eup_at.at[step], at, step)
    yield
    for i in (0, 1, 5):
        copies[i].wait()
    grads_at[...] = (grads_at[...].astype(jnp.float32) * mix_at[...]).astype(jnp.bfloat16)
    tiles(
        act_at.shape[1] // tile,
        tall,
        6,
        lambda i: matmul_tn(columns(act_at, i, tile), grads_at[...]),
        lambda i: results[1].at[pl.ds(pl.multiple_of(i * tile, tile), tile)],
    )
    yield
    copies[2].wait()
    tiles(
        results[0].shape[0],
        low,
        8,
        lambda i: matmul(act_at[pl.ds(pl.multiple_of(i * height, 16), height), :], down_at[...]).astype(jnp.bfloat16),
        lambda i: results[0].at[i, 0:height],
    )
    yield


def settle_kernel(depth, count, *refs):
    sums, summed, table, refs = refs[:count], refs[count], refs[count + 1], refs[count + 2 :]
    outs, expert_out, refs = refs[:count], refs[count], refs[count + 1 :]
    levels, z_sems, p_sems, keep = refs[:count], refs[count : count + 2], refs[count + 2 : count + 4], refs[count + 4]
    returned = refs[count + 5]
    level, here = lax.axis_index("dp"), lax.axis_index("expert")
    greet(depth, [(here + way) % 8 for way in range(1, 8)], True)
    capacity = returned.shape[1]
    started = []

    def slots(mate):
        return summed.at[pl.ds(pl.multiple_of(mate * capacity, 16), capacity)]

    for step in range(1, depth):
        target = (level + step) % depth
        for i in range(count):
            started.append(remote(sums[i].at[target], levels[i].at[step - 1], z_sems, (i, step), target, here))
            started[-1].start()
    for way in range(1, 8):
        mate = (here + way) % 8
        started.append(remote(slots(mate), returned.at[here], p_sems, (way,), level, mate))
        started[-1].start()
    kept = pltpu.make_async_copy(slots(here), returned.at[here], keep.at[0])
    kept.start()
    for way in range(1, 8):
        spot = returned.at[(here + 8 - way) % 8]
        remote(spot, spot, p_sems, (way,), level, here).wait_recv()
    kept.wait()
    rows = returned[...].reshape((-1, returned.shape[2]))
    expert_out[...] = matmul_tn(table[...], rows).astype(jnp.bfloat16)
    for i in range(count):
        total = sums[i][level].astype(jnp.float32)
        for step in range(1, depth):
            remote(levels[i].at[step - 1], levels[i].at[step - 1], z_sems, (i, step), level, here).wait_recv()
            total = total + levels[i][step - 1].astype(jnp.float32)
        outs[i][...] = total
    for copy in started:
        copy.wait_send()


def settle(sums, summed, table, ident):
    depth, count = lax.axis_size("dp"), len(sums)
    if lax.axis_size("expert") != 8:
        summed = summed.reshape(slot_shape(table.shape[1]) + summed.shape[1:])
        summed = lax.all_to_all(summed, "expert", split_axis=0, concat_axis=0, tiled=True)
        return [*sums, matmul_tn(table, summed.reshape((-1, summed.shape[2]))).astype(summed.dtype)]
    blocks = [s.shape[1:] for s in sums]
    vmem, whole = pl.BlockSpec(memory_space=pltpu.VMEM), pl.BlockSpec(memory_space=pl.ANY)
    return pl.pallas_call(
        functools.partial(settle_kernel, depth, count),
        out_shape=[jax.ShapeDtypeStruct(b, jnp.float32) for b in blocks]
        + [jax.ShapeDtypeStruct((table.shape[1],) + summed.shape[1:], summed.dtype)],
        in_specs=[vmem] * count + [whole, vmem],
        out_specs=[vmem] * (count + 1),
        scratch_shapes=[pltpu.VMEM((depth - 1,) + b, jnp.bfloat16) for b in blocks]
        + [pltpu.SemaphoreType.DMA((count, depth))] * 2
        + [pltpu.SemaphoreType.DMA((8,))] * 2
        + [pltpu.SemaphoreType.DMA((1,)), pltpu.VMEM(slot_shape(table.shape[1]) + summed.shape[1:], summed.dtype)],
        compiler_params=pltpu.CompilerParams(collective_id=ident, has_side_effects=True),
        cost_estimate=pl.CostEstimate(flops=1, bytes_accessed=1, transcendentals=0),
        name="settle",
    )(*sums, summed, table)


def scatter_plane(grads, ident, work=None):
    depth, count = lax.axis_size("dp"), len(grads)
    low = jnp.bfloat16
    if lax.axis_size("expert") != 8:
        sums = [lax.psum_scatter(g, both, scatter_dimension=0, tiled=True).astype(jnp.float32) for g in grads]
        if work is not None:
            act, pulled, rows_in, pre_grad, down, mix = work
            grad_rows = (pulled.astype(jnp.float32) * mix).astype(low)
            sums.append(matmul(act, down).astype(low))
            sums.append(matmul_tn(act, grad_rows))
            tall = matmul_tn(rows_in, pre_grad).astype(low)
            sums.append(lax.all_to_all(tall, "dp", split_axis=0, concat_axis=1, tiled=True))
        return sums
    grads = [g.reshape((depth, 4, 2, g.shape[0] // (8 * depth)) + g.shape[1:]) for g in grads]
    blocks = [g.shape[3:] for g in grads]
    width = min(b[1] for b in blocks)
    scratch = [pltpu.VMEM((depth, 4) + b, low) for b in blocks] * 2
    scratch += [pltpu.VMEM((depth, 2) + b, low) for b in blocks]
    scratch += [pltpu.VMEM((depth,) + b, low) for b in blocks]
    scratch += [pltpu.SemaphoreType.DMA((count, depth))] * 3 + [pltpu.SemaphoreType.DMA((count, depth, 2))] * 2
    scratch += [pltpu.SemaphoreType.DMA((count, depth))] * 2
    if work is None:
        operands = ()
        made = [jax.ShapeDtypeStruct((depth,) + b, low) for b in blocks]
    else:
        operands = tuple(work)
        act, rows_in, pre_grad, down = work[0], work[2], work[3], work[4]
        packed_rows, made_rows = sum(b[0] * b[1] for b in blocks) // width, act.shape[0] // depth
        own_rows = rows_in.shape[1] // depth
        made = [
            jax.ShapeDtypeStruct((depth, made_rows + packed_rows, width), low),
            jax.ShapeDtypeStruct((act.shape[1], act.shape[1]), jnp.float32),
            jax.ShapeDtypeStruct((own_rows, pre_grad.shape[1] * depth), low),
        ]
        scratch += [pltpu.VMEM((depth, packed_rows, width), low), pltpu.SemaphoreType.DMA((depth,))]
        scratch += [pltpu.SemaphoreType.DMA((1,))] + [pltpu.SemaphoreType.DMA((depth,))] * 2
        scratch += [pltpu.VMEM(work[i].shape, work[i].dtype) for i in range(6)]
        scratch += [
            pltpu.VMEM((2, 256, down.shape[1]), jnp.float32),
            pltpu.VMEM((2, made_rows, down.shape[1]), low),
            pltpu.VMEM((depth, own_rows, pre_grad.shape[1]), low),
            pltpu.SemaphoreType.DMA((10,)),
        ]
    out_space = pltpu.VMEM if work is None else pl.ANY
    return list(
        pl.pallas_call(
            functools.partial(scatter_kernel, depth, count, work is not None),
            out_shape=made,
            in_specs=[pl.BlockSpec(memory_space=pl.ANY)] * (count + len(operands)),
            out_specs=[pl.BlockSpec(memory_space=out_space)] * len(made),
            scratch_shapes=scratch,
            compiler_params=pltpu.CompilerParams(
                collective_id=ident, has_side_effects=True, vmem_limit_bytes=58 * 2**20
            ),
            cost_estimate=pl.CostEstimate(flops=1, bytes_accessed=200 * 2**20, transcendentals=0),
            name=f"scatter_plane_{ident}",
        )(*grads, *operands)
    )


def finish_scatter(packed, top, shapes):
    packed = lax.psum_scatter(packed, "dp", scatter_dimension=0)
    width = packed.shape[1]
    outs = [packed]
    for rows, columns in shapes:
        pieces = columns // width
        blocks = [packed[top + i * rows : top + (i + 1) * rows].astype(jnp.float32) for i in range(pieces)]
        outs.append(jnp.concatenate(blocks, axis=1))
        top += pieces * rows
    return outs


def body(
    tokens,
    seq_lengths,
    routes,
    w_qkv,
    w_out,
    w_up,
    w_down,
    gain_attn,
    gain_mlp,
    w_mix,
    expert_up,
    expert_down,
    cotangent,
):
    tok_rows, model_width = tokens.shape
    axis_dp, axis_experts = lax.axis_size("dp"), lax.axis_size("expert")
    expert_total = axis_experts * expert_up.shape[0]
    capacity = max(2, 5 * tok_rows // (4 * expert_total))
    slots = expert_total * capacity
    ff_expert = expert_up.shape[2]

    small = jnp.concatenate([gain_attn[:, None], gain_mlp[:, None], w_mix], axis=1)
    small = jnp.pad(small, ((0, 0), (0, 128 - small.shape[1])))
    length = seq_lengths[0]
    valid_rows = jnp.arange(tok_rows, dtype=jnp.int32) < length

    def pick(rows):
        return matmul(slot_table, rows).astype(jnp.bfloat16).reshape(expert_total, capacity, model_width)

    def dispatch(rows):
        arrived = lax.all_to_all(pick(rows), "expert", split_axis=0, concat_axis=0, tiled=True)
        return arrived.reshape(slots, model_width)

    def spread(rows):
        return lax.all_gather(rows, "dp", axis=0, tiled=True)

    def unspread(rows):
        return lax.psum_scatter(rows, "dp", scatter_dimension=0, tiled=True)

    def give_back(summed):
        summed = summed.reshape(expert_total, capacity, model_width)
        back = lax.all_to_all(summed, "expert", split_axis=0, concat_axis=0, tiled=True)
        return matmul_tn(slot_table, back.reshape(slots, model_width))

    down_part = expert_down[0]

    upstream_low = jnp.where(valid_rows[:, None], cotangent, jnp.zeros_like(cotangent))
    upstream = upstream_low.astype(jnp.float32)
    route_row = routes.reshape((1, tok_rows))
    qkv_full, out_full, small_full, up_part, pulled_here = gather_plane(
        [w_qkv, w_out, small], 0, expert_up[0], cotangent, route_row, seq_lengths
    )
    slot_table = slots_of(lax.optimization_barrier((route_row, qkv_full))[0], length, tok_rows)
    pulled_rows = spread(pulled_here.reshape(slots, model_width))
    gain_one = small_full[:, 0].astype(jnp.float32)
    gain_two = small_full[:, 1].astype(jnp.float32)
    mix_full = small_full[:, 2:4]
    mix_lean = (mix_full[:, 0] - mix_full[:, 1].astype(jnp.float32)).astype(jnp.float32)

    inputs = tokens.astype(jnp.float32)
    scaled_one, inverse_one = norm_forward(inputs)
    normed_one = (scaled_one * gain_one).astype(jnp.bfloat16)
    joined = matmul(normed_one, qkv_full).astype(jnp.bfloat16)
    heads_out, log_total = attention_forward(joined, seq_lengths)
    after_attn = inputs + matmul(heads_out, out_full)
    scaled_two, inverse_two = norm_forward(after_attn)
    normed_two = (scaled_two * gain_two).astype(jnp.bfloat16)

    rows_here = dispatch(normed_two)
    rows_here, w_up, w_down = lax.optimization_barrier((rows_here, w_up, w_down))
    rows_in = spread(rows_here)
    up_full, down_full = gather_plane([w_up, w_down], 1)

    pulled_rows, up_full, down_full = lax.optimization_barrier((pulled_rows, up_full, down_full))
    mix_weights = jax.nn.softmax(matmul(normed_two, mix_full), axis=-1)
    grad_down, grad_up, normed_grad, dense_out, pull_dense = dense_branch(
        normed_two, up_full, down_full, upstream_low, mix_weights[:, 0:1]
    )
    lean_dense = mix_weights[:, 0:1] * mix_weights[:, 1:2] * pull_dense
    normed_grad = normed_grad + lean_dense * mix_lean[None, :]

    act_pull = matmul_nt(pulled_rows, down_part)
    rows_in, act_pull, grad_up, grad_down, normed_grad = lax.optimization_barrier(
        (rows_in, act_pull, grad_up, grad_down, normed_grad)
    )
    act_rows, pre_grad, row_mix, input_grad, lean_rows = expert_branch(
        rows_in, act_pull, up_part, small_full, mix_lean[None, :]
    )
    in_grad_here = unspread(input_grad)
    *sums, grad_expert_down, grad_expert_up = scatter_plane(
        [grad_up, grad_down], 2, (act_rows, pulled_rows, rows_in, pre_grad, down_part, row_mix)
    )
    grad_expert_down = grad_expert_down[None]
    in_grad_here, *sums = lax.optimization_barrier((in_grad_here, *sums))
    if len(sums) == 1:
        outs_here, grad_up, grad_down = finish_scatter(sums[0], slots, (w_up.shape, w_down.shape))
    else:
        grad_up, grad_down, outs_here = sums[0], sums[1], unspread(sums[2])
    in_grad_back = give_back(in_grad_here)

    normed_grad = normed_grad + in_grad_back
    lean_grad = jnp.sum(normed_two.astype(jnp.float32) * lean_dense, axis=0) - lean_rows[0]
    mlp_in_grad, grad_gain_two = norm_backward(normed_grad, scaled_two, inverse_two, gain_two)
    resid_grad = upstream + mlp_in_grad
    attn_grad = resid_grad.astype(jnp.bfloat16)
    grad_out = matmul_tn(heads_out, attn_grad)
    heads_grad = matmul_nt(attn_grad, out_full).astype(jnp.bfloat16)
    joined_grad = jnp.concatenate(
        attention_backward(joined, heads_grad, heads_out, log_total, seq_lengths), axis=1
    )
    grad_qkv = matmul_tn(normed_one, joined_grad)
    normed_one_grad = matmul_nt(joined_grad, qkv_full)
    attn_in_grad, grad_gain_one = norm_backward(normed_one_grad, scaled_one, inverse_one, gain_one)
    grad_inputs = resid_grad + attn_in_grad

    small_grads = jnp.stack([grad_gain_one, grad_gain_two, lean_grad, -lean_grad], axis=1)
    small_grads = jnp.pad(small_grads, ((0, 0), (0, 128 - small_grads.shape[1])))
    grad_expert_down = jnp.where(length >= 0, grad_expert_down, 0.0)
    grad_expert_up = grad_expert_up.astype(jnp.float32)[None]
    small_grads, grad_expert_down, grad_expert_up = lax.optimization_barrier(
        (small_grads.astype(jnp.bfloat16), grad_expert_down, grad_expert_up)
    )
    sums = scatter_plane([grad_qkv.astype(jnp.bfloat16), grad_out.astype(jnp.bfloat16), small_grads], 3)
    grad_qkv, grad_out, small_grads, expert_out = settle(sums, outs_here, slot_table, 4)
    result = after_attn + mix_weights[:, 0:1] * dense_out + mix_weights[:, 1:2] * expert_out
    return (
        result,
        grad_inputs,
        grad_qkv,
        grad_out,
        grad_up,
        grad_down,
        small_grads[:, 0],
        small_grads[:, 1],
        small_grads[:, 2:4],
        grad_expert_up,
        grad_expert_down,
    )


def solution(mesh):
    rows, vector = P(both, None), P(both)
    experts = P("expert", "dp", None)
    return jax.shard_map(
        body,
        mesh=mesh,
        in_specs=(rows, vector, rows, rows, rows, rows, rows, vector, vector, rows, experts, experts, rows),
        out_specs=(rows, rows, rows, rows, rows, rows, vector, vector, rows, experts, experts),
        check_vma=False,
    )
```
